32 devices in a mesh: width: 2 (over y), dp: 16 (over z, x, core).
Axes of the slice: x: 2, y: 2, z: 4, core: 2. Of those that a mesh axis runs over, the one named last changes fastest.
Arguments:
- tokens: bfloat16 [8192, 2048], P(('width', 'dp')), may hold values from -6 to 6
- cotangent: bfloat16 [8192, 2048], P(('width', 'dp')), may hold values from -6 to 6
- lengths: int32 [2, 8], P('width'), may hold values from 1 to 1024, 4096 in all within a row
- levels: int32 [2], P('width'), may hold values from 0 to 1, each once
- step_count: int32 [1], replicated, may hold values from 1 to 5
- weight_in: float32 [2048, 8512], P('dp'), may hold values from -0.125 to 0.125
- moment_in: float32 [2048, 8512], P('dp'), may hold values from -181.01933 to 181.01933
- second_in: float32 [2048, 8512], P('dp'), may hold values from 2048 to 8192
- weight_out: float32 [4096, 2048], P('dp'), may hold values from -0.09375 to 0.09375
- moment_out: float32 [4096, 2048], P('dp'), may hold values from -362.03867 to 362.03867
- second_out: float32 [4096, 2048], P('dp'), may hold values from 8192 to 32768
- small_params: float32 [28096], replicated, may hold values from -9 to 2
- moment_small: float32 [28096], replicated, may hold values from -1024 to 1024
- second_small: float32 [28096], replicated, may hold values from 4096 to 262144
Outputs:
- block_out: bfloat16 [8192, 2048], P(('width', 'dp'))
- grad_tokens: bfloat16 [8192, 2048], P(('width', 'dp'))
- new_weight_in: float32 [2048, 8512], P('dp')
- new_moment_in: float32 [2048, 8512], P('dp')
- new_second_in: float32 [2048, 8512], P('dp')
- low_weight_in: bfloat16 [2048, 8512], P('dp')
- new_weight_out: float32 [4096, 2048], P('dp')
- new_moment_out: float32 [4096, 2048], P('dp')
- new_second_out: float32 [4096, 2048], P('dp')
- low_weight_out: bfloat16 [4096, 2048], P('dp')
- new_small: float32 [28096], replicated
- new_moment_small: float32 [28096], replicated
- new_second_small: float32 [28096], replicated
The draws below stay inside these ranges and needn't reach their ends.
Inputs may be any that keep to these rules, and one draw needn't show every extreme that they name: Each row of lengths sums to 4096, and its longest sequence has exactly 1024 tokens. `levels`: each level 0 to 1 is held by exactly one width group.
All inputs are finite; a program needn't handle non-finite values.
Results may differ from the reference program's by a relative error of at most 0.0095.
Values may be sent and summed in bfloat16 or wider, within the bound.
No kernel may reach another device: no remote copies, remote signals or barrier semaphores. Data moves between devices by JAX's collectives and lax.ppermute only.
A program may use at most 448 MiB of HBM per device.

```python
import math
from functools import partial
import jax
import jax.numpy as jnp
import numpy as np
from jax import lax

D = 2048
E = 4096
H = 64
P_SIZE = 64
N = 128
KCONV = 4
STRETCH = 256
MAX_LEN = 1024
GROUP_TOK = 4096
SEQS = 8
TOKENS = 8192
K = 4352
C = 8512
SMALLN = 28096
N_WIDTH = 2


def moment_kappa():
    return jnp.concatenate([jnp.full((D,), 2.0, jnp.float32), jnp.full((E,), 1.0, jnp.float32), jnp.full((KCONV * K,), 1.0, jnp.float32), jnp.full((K,), 1.0, jnp.float32), jnp.full((H,), 1.0, jnp.float32), jnp.full((H,), 1.0, jnp.float32), jnp.full((H,), 4.0, jnp.float32)])


def draw_small_params(key, part):
    keys = jax.random.split(jax.random.fold_in(key, 11), 7)
    g_in = 1.0 + 0.1 * jnp.clip(jax.random.normal(keys[0], (D,), jnp.float32), -4.0, 4.0)
    g_out = 1.0 + 0.1 * jnp.clip(jax.random.normal(keys[1], (E,), jnp.float32), -4.0, 4.0)
    conv_w = 0.5 * jnp.clip(jax.random.normal(keys[2], (KCONV * K,), jnp.float32), -4.0, 4.0)
    dt_bias = jax.random.uniform(keys[5], (H,), jnp.float32, -8.0, -3.0)
    conv_b = jax.random.uniform(keys[3], (K,), jnp.float32, -0.5, 0.5)
    a_log = jax.random.uniform(keys[4], (H,), jnp.float32, -1.0, 2.0)
    d_skip = jax.random.uniform(keys[6], (H,), jnp.float32, 0.5, 1.5)
    return jnp.concatenate([g_in, g_out, conv_w, conv_b, a_log, dt_bias, d_skip])


def draw_moment_small(key, part):
    noise = jnp.clip(jax.random.normal(jax.random.fold_in(key, 23), (SMALLN,), jnp.float32), -4.0, 4.0)
    return moment_kappa() * math.sqrt(GROUP_TOK) * noise


def draw_second_small(key, part):
    spread = jnp.exp(jax.random.uniform(jax.random.fold_in(key, 37), (SMALLN,), jnp.float32, 0.0, math.log(4.0)))
    kappa = moment_kappa()
    return kappa * kappa * GROUP_TOK * spread


def raised(values, key, source, target, parts, factor):
    owner, partner = [(jnp.arange(values.shape[axis_at]) // (values.shape[axis_at] // parts)).reshape([-1 if axis == axis_at else 1 for axis in range(values.ndim)]) for axis_at in (source, target)]
    chosen = jax.random.permutation(key, parts)[partner]
    strong = (owner == chosen) | (owner == (partner + parts // 2) % parts)
    return jnp.where(strong, factor * values, values)


def block_scale(own_key, shape, cuts, low, high):
    gain = 1.0
    for dim, parts in cuts:
        steps = jax.random.uniform(jax.random.fold_in(jax.random.fold_in(own_key, 6), dim), (parts,), jnp.float32, low / len(cuts), high / len(cuts))
        gain = gain * jnp.repeat(jnp.exp(steps), shape[dim] // parts).reshape((-1,) + (1,) * (len(shape) - 1 - dim))
    return gain


def length_profile(amount, total, most, skew):
    loads = [(1 << 20) // math.isqrt(grade ** skew) + 1 for grade in range(2, amount + 1)]
    spare, counts = total - most - (amount - 1), [1] * (amount - 1)
    while spare > 0:
        free = [i for i in range(amount - 1) if counts[i] < most]
        pool, budget = sum([loads[i] for i in free]), spare
        for i in free:
            more = min(most - counts[i], max(1, budget * loads[i] // pool), spare)
            counts[i] = counts[i] + more
            spare = spare - more
    return np.array([most] + counts)


def uneven(rng, count, total, most, lean):
    if count == 2:
        one = jax.random.randint(rng, (), max(1, total - most), min(most, total - 1) + 1)
        return jnp.stack([one, total - one])
    tallies = jnp.asarray(length_profile(count, total, most, lean), jnp.int32)
    twos = (count - 1) // 2
    source_of, receiver = tallies[1:1 + 2 * twos:2], tallies[2:2 + 2 * twos:2]
    slack = jnp.minimum(source_of - 1, most - receiver)
    shifted = jax.random.randint(jax.random.fold_in(rng, 1), (twos,), 0, 1 << 20) % (slack + 1)
    tallies = tallies.at[1:1 + 2 * twos:2].set(source_of - shifted).at[2:2 + 2 * twos:2].set(receiver + shifted)
    return tallies[jax.random.permutation(jax.random.fold_in(rng, 2), count)]


def normal_values(stream_key, shape, width, limit, cuts=(), held_as=jnp.bfloat16):
    drawn = jax.random.normal(stream_key, shape, jnp.float32) * width
    if len(cuts) > 0:
        drawn = block_scale(stream_key, shape, cuts, -0.22, 0.18) * drawn
    return jnp.clip(drawn, min=-limit, max=limit).astype(held_as)


def heavy_noise(key, dims, deviation, reach, cuts, heavy, held_as=jnp.bfloat16):
    values = deviation * jax.random.normal(key, dims, jnp.float32)
    if cuts:
        values = values * block_scale(key, dims, cuts, -0.22, 0.18)
    return jnp.clip(raised(values, jax.random.fold_in(key, 3), *heavy), -reach, reach).astype(held_as)


def setup_inputs(seed: int = 0) -> dict:
    seeds = jax.random.split(jax.random.key(seed), 15)
    tokens = heavy_noise(seeds[0], (TOKENS, D), 1.0, 6.0, ((0, 32),), (0, 1, 32, 2.75))
    cotangent = normal_values(seeds[1], (TOKENS, D), 1.0, 6.0, ((0, 32),))
    lengths = jax.vmap(lambda own: uneven(own, SEQS, GROUP_TOK, MAX_LEN, 1))(jax.random.split(seeds[2], N_WIDTH)).reshape((N_WIDTH, SEQS)).astype(jnp.int32)
    levels = jax.random.permutation(seeds[3], N_WIDTH).astype(jnp.int32)
    step_count = jax.random.randint(seeds[4], (1,), 1, 6).astype(jnp.int32)
    weight_in = normal_values(seeds[5], (D, C), D ** -0.5, 0.125, ((0, 16),), jnp.float32)
    moment_in = normal_values(seeds[6], (D, C), ((GROUP_TOK // 2) ** 0.5), 181.01933, ((0, 16),), jnp.float32)
    second_in = jnp.clip(jnp.exp(math.log(8192.0) - 1.3862944 * jax.random.uniform(seeds[7], (D, C), jnp.float32) ** block_scale(seeds[7], (D, C), ((0, 16),), -0.2, 0.2)), 2048.0, 8192.0)
    weight_out = normal_values(seeds[8], (E, D), E ** -0.5, 0.09375, ((0, 16),), jnp.float32)
    moment_out = normal_values(seeds[9], (E, D), ((2 * GROUP_TOK) ** 0.5), 362.03867, ((0, 16),), jnp.float32)
    second_out = jnp.clip(jnp.exp(math.log(32768.0) - 1.3862944 * jax.random.uniform(seeds[10], (E, D), jnp.float32) ** block_scale(seeds[10], (E, D), ((0, 16),), -0.2, 0.2)), 8192.0, 32768.0)
    small_params = draw_small_params(jax.random.fold_in(seeds[14], 71), 0)
    moment_small = draw_moment_small(jax.random.fold_in(seeds[14], 71), 0)
    second_small = draw_second_small(jax.random.fold_in(seeds[14], 71), 0)
    return dict(tokens=tokens, cotangent=cotangent, lengths=lengths, levels=levels, step_count=step_count, weight_in=weight_in, moment_in=moment_in, second_in=second_in, weight_out=weight_out, moment_out=moment_out, second_out=second_out, small_params=small_params, moment_small=moment_small, second_small=second_small)


NORM_EPS = 1e-05
ADAM_EPS = 1e-08
BETA_ONE = 0.5
BETA_TWO = 0.5
MATRIX_RATE = 0.02
MATRIX_DECAY = 0.1
PRECISE = lax.Precision.HIGHEST

@jax.custom_vjp
def low(v):
    return lax.optimization_barrier(v.astype(jnp.bfloat16)).astype(jnp.float32)

@jax.custom_vjp
def low_back(v):
    return v

def low_keep(v):
    return (low(v), None)

def low_pass(kept, grad):
    return (grad,)

def back_keep(v):
    return (v, None)

def back_low(kept, grad):
    return (low(grad),)
low.defvjp(low_keep, low_pass)
low_back.defvjp(back_keep, back_low)

def small_table():
    rate_table = jnp.concatenate([jnp.full((D,), 0.3, jnp.float32), jnp.full((E,), 0.3, jnp.float32), jnp.full((KCONV * K,), 0.2, jnp.float32), jnp.full((K,), 0.2, jnp.float32), jnp.full((H,), 0.3, jnp.float32), jnp.full((H,), 1.0, jnp.float32), jnp.full((H,), 0.3, jnp.float32)])
    decay_table = jnp.concatenate([jnp.zeros((D + E,), jnp.float32), jnp.full((KCONV * K,), 0.1, jnp.float32), jnp.zeros((K + 3 * H,), jnp.float32)])
    return (rate_table, decay_table)

def unpack(small_params):
    offset = D + E
    conv_w = small_params[offset:offset + KCONV * K].reshape(KCONV, K)
    offset = offset + KCONV * K
    conv_b = small_params[offset:offset + K]
    offset = offset + K
    a_log = small_params[offset:offset + H]
    dt_bias = small_params[offset + H:offset + 2 * H]
    d_skip = small_params[offset + 2 * H:offset + 3 * H]
    return (small_params[:D], small_params[D:D + E], conv_w, conv_b, a_log, dt_bias, d_skip)

def positions(lengths_row, start, row_count):
    seq_ends = jnp.cumsum(lengths_row).astype(jnp.int32)
    place_at = start + jnp.arange(row_count, dtype=jnp.int32)
    before = lax.optimization_barrier(jnp.sum(jnp.where(seq_ends[None, :] <= place_at[:, None], lengths_row[None, :], 0), axis=1)).astype(jnp.int32)
    return place_at - before

def pre_norm(inputs_f, small_params):
    g_in = small_params[:D]
    return inputs_f * lax.rsqrt(lax.optimization_barrier(jnp.mean(inputs_f * inputs_f, axis=1, keepdims=True)) + NORM_EPS) * g_in

def front_part(projected, prior_rows, small_params, seq_place, live_units):
    g_in, g_out, conv_w, conv_b, a_log, dt_bias, d_skip = unpack(small_params)
    row_count = projected.shape[0]
    conv_input = jnp.concatenate([prior_rows, projected[:, E:E + K]], axis=0)
    conv_sum = conv_b + jnp.zeros((row_count, K), jnp.float32)
    for tap_index in range(KCONV):
        valid = (seq_place >= KCONV - 1 - tap_index).astype(jnp.float32)
        conv_sum = conv_sum + conv_w[tap_index] * conv_input[tap_index:tap_index + row_count] * valid[:, None]
    activated = jax.nn.silu(conv_sum)
    unit_mask = (jnp.arange(E, dtype=jnp.int32) < live_units).astype(jnp.float32)
    inner_x = activated[:, :E] * unit_mask
    b_values = activated[:, E:E + N]
    c_values = activated[:, E + N:]
    gate_raw = projected[:, :E]
    step_size = jax.nn.softplus(projected[:, E + K:] + dt_bias)
    log_decay = step_size * -jnp.exp(a_log)
    return (gate_raw, inner_x, step_size, log_decay, b_values, c_values)

def stretch_step(carried, pieces):
    values_x, step_size, log_decay, b_values, c_values, seq_place = pieces
    index_row = jnp.arange(STRETCH, dtype=jnp.int32)
    cumulate = jnp.cumsum(log_decay, axis=0)
    visible = (index_row[None, :] <= index_row[:, None]) & (seq_place[:, None] >= index_row[:, None] - index_row[None, :])
    gap_log = jnp.where(visible[:, :, None], cumulate[:, None, :] - cumulate[None, :, :], 0.0)
    gram = jnp.einsum('in,jn->ij', c_values, b_values, precision=PRECISE)
    mixing = jnp.where(visible[:, :, None], jnp.exp(gap_log), 0.0) * gram[:, :, None]
    scaled_x = values_x * step_size[:, :, None]
    within = jnp.einsum('ijh,jhp->ihp', mixing, scaled_x, precision=PRECISE)
    carrying = jnp.where((seq_place >= index_row + 1)[:, None], jnp.exp(cumulate), 0.0)
    across = jnp.einsum('in,hpn->ihp', c_values, carried, precision=PRECISE) * carrying[:, :, None]
    tail_ok = seq_place[STRETCH - 1] >= STRETCH - 1 - index_row
    tail_weight = jnp.where(tail_ok[:, None], jnp.exp(jnp.where(tail_ok[:, None], cumulate[STRETCH - 1][None, :] - cumulate, 0.0)), 0.0)
    fresh_state = jnp.einsum('jhp,jn->hpn', scaled_x * tail_weight[:, :, None], b_values, precision=PRECISE)
    updated = carried * carrying[STRETCH - 1][:, None, None] + fresh_state
    return (updated, within + across)

def ssd_whole(inner_x, step_size, log_decay, b_values, c_values, seq_place):
    row_count = inner_x.shape[0]
    blocks = row_count // STRETCH
    pieces = (inner_x.reshape(blocks, STRETCH, H, P_SIZE), step_size.reshape(blocks, STRETCH, H), log_decay.reshape(blocks, STRETCH, H), b_values.reshape(blocks, STRETCH, N), c_values.reshape(blocks, STRETCH, N), seq_place.reshape(blocks, STRETCH))
    final, outputs = lax.scan(jax.checkpoint(stretch_step), jnp.zeros((H, P_SIZE, N), jnp.float32), pieces)
    return outputs.reshape(row_count, E)

def back_end(y_local, y_carried, inner_x, gate_raw, small_params, live_units):
    d_skip = unpack(small_params)[6]
    row_count = inner_x.shape[0]
    mixed = y_local + y_carried + (inner_x.reshape(row_count, H, P_SIZE) * d_skip[:, None]).reshape(row_count, E)
    gated = mixed * jax.nn.silu(gate_raw)
    g_out = small_params[D:D + E]
    return gated * lax.rsqrt(lax.optimization_barrier(jnp.sum(gated * gated, axis=1, keepdims=True)) / live_units.astype(jnp.float32) + NORM_EPS) * g_out

def block_layer(inputs_f, weight_in_low, weight_out_low, small_params, seq_place, live_units):
    normed = pre_norm(inputs_f, small_params)
    projected = low_back(low(jnp.dot(low(normed), weight_in_low, precision=PRECISE, preferred_element_type=jnp.float32)))
    prior_rows = jnp.zeros((KCONV - 1, K), jnp.float32)
    gate_raw, inner_x, step_size, log_decay, b_values, c_values = front_part(projected, prior_rows, small_params, seq_place, live_units)
    y_local = ssd_whole(inner_x, step_size, log_decay, b_values, c_values, seq_place)
    normed_out = back_end(y_local, 0.0, inner_x, gate_raw, small_params, live_units)
    return inputs_f + jnp.dot(low(normed_out), weight_out_low, precision=PRECISE, preferred_element_type=jnp.float32)

def adamw_step(weight, moment, second, grad, rate, decay, step_float):
    first_new = BETA_ONE * moment + (1.0 - BETA_ONE) * grad
    second_new = BETA_TWO * second + (1.0 - BETA_TWO) * grad * grad
    first_hat = first_new / (1.0 - jnp.power(BETA_ONE, step_float))
    second_hat = second_new / (1.0 - jnp.power(BETA_TWO, step_float))
    return (weight - rate * (first_hat / (jnp.sqrt(second_hat) + ADAM_EPS) + decay * weight), first_new, second_new)

def reference(tokens, cotangent, lengths, levels, step_count, weight_in, moment_in, second_in, weight_out, moment_out, second_out, small_params, moment_small, second_small):
    weight_in_low = weight_in.astype(jnp.bfloat16).astype(jnp.float32)
    weight_out_low = weight_out.astype(jnp.bfloat16).astype(jnp.float32)
    grad_in_total = jnp.zeros((D, C), jnp.float32)
    grad_out_total = jnp.zeros((E, D), jnp.float32)
    grad_small_total = jnp.zeros((SMALLN,), jnp.float32)
    outputs_all = []
    grads_all = []
    for group_index in range(N_WIDTH):
        inputs_f = tokens[group_index * GROUP_TOK:(group_index + 1) * GROUP_TOK].astype(jnp.float32)
        back_f = cotangent[group_index * GROUP_TOK:(group_index + 1) * GROUP_TOK].astype(jnp.float32)
        live_units = jnp.right_shift(jnp.int32(E), (N_WIDTH - 1 - levels[group_index]).astype(jnp.int32))
        seq_place = positions(lengths[group_index], 0, GROUP_TOK)
        layer_fn = partial(block_layer, seq_place=seq_place, live_units=live_units)
        result, layer_back = jax.vjp(layer_fn, inputs_f, weight_in_low, weight_out_low, small_params)
        grad_inputs, grad_win, grad_wout, grad_small = layer_back(back_f)
        outputs_all.append(result.astype(jnp.bfloat16))
        grads_all.append(grad_inputs.astype(jnp.bfloat16))
        grad_in_total = grad_in_total + grad_win
        grad_out_total = grad_out_total + grad_wout
        grad_small_total = grad_small_total + grad_small
    step_float = step_count[0].astype(jnp.float32)
    new_in, mom_in, sec_in = adamw_step(weight_in, moment_in, second_in, grad_in_total, MATRIX_RATE, MATRIX_DECAY, step_float)
    new_out, mom_out, sec_out = adamw_step(weight_out, moment_out, second_out, grad_out_total, MATRIX_RATE, MATRIX_DECAY, step_float)
    rate_table, decay_table = small_table()
    new_small, mom_small, sec_small = adamw_step(small_params, moment_small, second_small, grad_small_total, rate_table, decay_table, step_float)
    return (jnp.concatenate(outputs_all, axis=0), jnp.concatenate(grads_all, axis=0), new_in, mom_in, sec_in, new_in.astype(jnp.bfloat16), new_out, mom_out, sec_out, new_out.astype(jnp.bfloat16), new_small, mom_small, sec_small)
```

```python
from functools import partial

import jax
import jax.numpy as jnp
from jax import lax
from jax.experimental import pallas as pl
from jax.experimental.pallas import tpu as pltpu
from jax.sharding import PartitionSpec as P

D = 2048
E = 4096
H = 64
P_SIZE = 64
N = 128
KCONV = 4
STRETCH = 256
K = 4352

NORM_EPS = 1e-05
ADAM_EPS = 1e-08
BETA_ONE = 0.5
BETA_TWO = 0.5
MATRIX_RATE = 0.02
MATRIX_DECAY = 0.1
PRECISE = lax.Precision.HIGHEST
BF = jnp.bfloat16
F32 = jnp.float32
LOW = -1e30
SHARED = 2 * N + H


def small_table():
    rate_table = jnp.concatenate(
        [
            jnp.full((D,), 0.3, F32),
            jnp.full((E,), 0.3, F32),
            jnp.full((KCONV * K,), 0.2, F32),
            jnp.full((K,), 0.2, F32),
            jnp.full((H,), 0.3, F32),
            jnp.full((H,), 1.0, F32),
            jnp.full((H,), 0.3, F32),
        ]
    )
    decay_table = jnp.concatenate(
        [
            jnp.zeros((D + E,), F32),
            jnp.full((KCONV * K,), 0.1, F32),
            jnp.zeros((K + 3 * H,), F32),
        ]
    )
    return (rate_table, decay_table)


def unpack(small_params):
    offset = D + E
    conv_w = small_params[offset : offset + KCONV * K].reshape(KCONV, K)
    offset = offset + KCONV * K
    conv_b = small_params[offset : offset + K]
    offset = offset + K
    a_log = small_params[offset : offset + H]
    dt_bias = small_params[offset + H : offset + 2 * H]
    d_skip = small_params[offset + 2 * H : offset + 3 * H]
    return (small_params[:D], small_params[D : D + E], conv_w, conv_b, a_log, dt_bias, d_skip)


def row_places(lengths_row, row_count):
    seq_ends = jnp.cumsum(lengths_row)
    at = jnp.arange(row_count, dtype=jnp.int32)
    passed = seq_ends[None, :] <= at[:, None]
    begin = jnp.max(jnp.where(passed, seq_ends[None, :], 0), axis=1)
    finish = jnp.min(jnp.where(passed, row_count, seq_ends[None, :]), axis=1)
    return (at - begin, finish - 1 - at)


def adamw_step(weight, moment, second, grad, rate, decay, step_float):
    first_new = BETA_ONE * moment + (1.0 - BETA_ONE) * grad
    second_new = BETA_TWO * second + (1.0 - BETA_TWO) * grad * grad
    first_hat = first_new / (1.0 - jnp.power(BETA_ONE, step_float))
    second_hat = second_new / (1.0 - jnp.power(BETA_TWO, step_float))
    return (
        weight - rate * (first_hat / (jnp.sqrt(second_hat) + ADAM_EPS) + decay * weight),
        first_new,
        second_new,
    )


def sigmoid(v):
    return 1.0 / (1.0 + jnp.exp(-v))


def dot(a, b, dims):
    return lax.dot_general(
        a.astype(BF), b.astype(BF), (dims, ((), ())), preferred_element_type=F32
    )


def spread(columns, heads):
    return jnp.concatenate(
        [
            jnp.broadcast_to(columns[:, h : h + 1], (columns.shape[0], P_SIZE))
            for h in range(heads)
        ],
        axis=1,
    )


def head_sums(values, heads):
    lane = lax.broadcasted_iota(jnp.int32, (values.shape[0], 128), 1)
    total = jnp.zeros((values.shape[0], 128), F32)
    for h in range(heads):
        part = jnp.sum(values[:, h * P_SIZE : (h + 1) * P_SIZE], axis=1, keepdims=True)
        total = jnp.where(lane == h, part, total)
    return total


def convolve(buffer, weights, bias, place):
    total = bias + jnp.zeros((STRETCH, buffer.shape[1]), F32)
    for tap in range(KCONV):
        back = KCONV - 1 - tap
        rows = buffer[8 - back : 8 - back + STRETCH, :]
        if back:
            rows = jnp.where(place >= back, rows, 0.0)
        total = total + weights[tap : tap + 1, :] * rows
    return total


def block_terms(place, remain, dt_in, pdt):
    row = lax.broadcasted_iota(jnp.int32, (STRETCH, STRETCH), 0)
    col = lax.broadcasted_iota(jnp.int32, (STRETCH, STRETCH), 1)
    at = lax.broadcasted_iota(jnp.int32, (STRETCH, 1), 0)
    visible = (col <= row) & (col >= at - place)
    biased = dt_in + pdt[0:1, :]
    step = jnp.maximum(biased, 0.0) + jnp.log1p(jnp.exp(-jnp.abs(biased)))
    log_decay = step * pdt[1:2, :]
    lower = jnp.where(col <= row, 1.0, 0.0).astype(F32)
    cum = lax.dot_general(
        lower, log_decay, (((1,), (0,)), ((), ())), precision=PRECISE, preferred_element_type=F32
    )
    cum_t = jnp.transpose(cum)
    carrying = jnp.where(place >= at + 1, jnp.exp(cum), 0.0)
    tail_ok = remain >= STRETCH - 1 - at
    tail = jnp.exp(jnp.where(tail_ok, cum[STRETCH - 1 : STRETCH, :] - cum, LOW))
    return visible, biased, step, log_decay, cum, cum_t, carrying, tail


def forward_kernel(
    heads,
    gate_ref,
    x_ref,
    bc_ref,
    dt_ref,
    place_ref,
    remain_ref,
    px_ref,
    pbc_ref,
    pdt_ref,
    zin_ref,
    mixed_ref,
    square_ref,
    states_ref,
    state,
    xbuf,
    bcbuf,
):
    @pl.when(pl.program_id(0) == 0)
    def _():
        state[...] = jnp.zeros_like(state)
        xbuf[0:8, :] = jnp.zeros((8, xbuf.shape[1]), F32)
        bcbuf[0:8, :] = jnp.zeros((8, bcbuf.shape[1]), F32)

    place = place_ref[...]
    remain = remain_ref[...]
    xbuf[8 : 8 + STRETCH, :] = x_ref[...].astype(F32)
    bcbuf[8 : 8 + STRETCH, :] = bc_ref[...].astype(F32)
    conv_x = convolve(xbuf, px_ref[0:4, :], px_ref[4:5, :], place)
    conv_bc = convolve(bcbuf, pbc_ref[0:4, :], pbc_ref[4:5, :], place)
    xbuf[0:8, :] = xbuf[STRETCH : STRETCH + 8, :]
    bcbuf[0:8, :] = bcbuf[STRETCH : STRETCH + 8, :]
    x = conv_x * sigmoid(conv_x) * px_ref[7:8, :]
    act_bc = conv_bc * sigmoid(conv_bc)
    b_low = act_bc[:, :N].astype(BF)
    c_low = act_bc[:, N:].astype(BF)
    visible, _, step, _, cum, cum_t, carrying, tail = block_terms(
        place, remain, dt_ref[...].astype(F32), pdt_ref[...]
    )
    scaled = x * spread(step, heads)
    scaled_low = scaled.astype(BF)
    gram = dot(c_low, b_low, ((1,), (1,)))
    old = state[...]
    states_ref[0] = old
    across = dot(c_low, old, ((1,), (1,))) * spread(carrying, heads)
    parts = []
    for h in range(heads):
        decay = jnp.exp(jnp.where(visible, cum[:, h : h + 1] - cum_t[h : h + 1, :], LOW))
        parts.append(
            dot(gram * decay, scaled_low[:, h * P_SIZE : (h + 1) * P_SIZE], ((1,), (0,)))
        )
    mixed = jnp.concatenate(parts, axis=1) + across + px_ref[5:6, :] * x
    fresh = dot(scaled * spread(tail, heads), b_low, ((0,), (0,)))
    for h in range(heads):
        rows = slice(h * P_SIZE, (h + 1) * P_SIZE)
        state[rows, :] = (
            old[rows, :] * carrying[STRETCH - 1 : STRETCH, h : h + 1] + fresh[rows, :]
        )
    gate = gate_ref[...].astype(F32)
    gated = mixed * (gate * sigmoid(gate))
    mixed_ref[...] = mixed
    zin_ref[...] = (gated * px_ref[6:7, :]).astype(BF)
    square_ref[...] = jnp.sum(gated * gated, axis=1, keepdims=True)


def backward_kernel(
    heads,
    gate_ref,
    x_ref,
    bc_ref,
    dt_ref,
    xprev_ref,
    bcprev_ref,
    place_ref,
    remain_ref,
    mixed_ref,
    gout_ref,
    scale_ref,
    pull_ref,
    states_ref,
    px_ref,
    pbc_ref,
    pdt_ref,
    gp_ref,
    low_ref,
    gx_ref,
    gbc_ref,
    gdt_ref,
    gstate,
    xbuf,
    bcbuf,
    gxbuf,
    gbcbuf,
):
    width = x_ref.shape[1]

    @pl.when(pl.program_id(0) == 0)
    def _():
        gstate[...] = jnp.zeros_like(gstate)
        gxbuf[STRETCH : STRETCH + 8, :] = jnp.zeros((8, width), F32)
        gbcbuf[STRETCH : STRETCH + 8, :] = jnp.zeros((8, 2 * N), F32)
        gx_ref[...] = jnp.zeros_like(gx_ref)
        gbc_ref[...] = jnp.zeros_like(gbc_ref)
        gdt_ref[...] = jnp.zeros_like(gdt_ref)

    place = place_ref[...]
    remain = remain_ref[...]
    xbuf[0:8, :] = xprev_ref[8:16, :].astype(F32)
    bcbuf[0:8, :] = bcprev_ref[8:16, :].astype(F32)
    xbuf[8 : 8 + STRETCH, :] = x_ref[...].astype(F32)
    bcbuf[8 : 8 + STRETCH, :] = bc_ref[...].astype(F32)
    conv_x = convolve(xbuf, px_ref[0:4, :], px_ref[4:5, :], place)
    conv_bc = convolve(bcbuf, pbc_ref[0:4, :], pbc_ref[4:5, :], place)
    sig_x = sigmoid(conv_x)
    sig_bc = sigmoid(conv_bc)
    x = conv_x * sig_x * px_ref[7:8, :]
    act_bc = conv_bc * sig_bc
    b_low = act_bc[:, :N].astype(BF)
    c_low = act_bc[:, N:].astype(BF)
    visible, biased, step, log_decay, cum, cum_t, carrying, tail = block_terms(
        place, remain, dt_ref[...].astype(F32), pdt_ref[...]
    )

    gate = gate_ref[...].astype(F32)
    sig = sigmoid(gate)
    silu = gate * sig
    mixed = mixed_ref[...]
    gated = mixed * silu
    g_out = px_ref[6:7, :]
    scale = scale_ref[...]
    upstream = gout_ref[...]
    low_ref[...] = (gated * scale * g_out).astype(BF)
    g_gated = scale * g_out * upstream - gated * pull_ref[...]
    g_mixed = g_gated * silu
    gp_ref[:, 0:width] = (g_gated * mixed * (sig * (1.0 + gate * (1.0 - sig)))).astype(BF)

    step_wide = spread(step, heads)
    carry_wide = spread(carrying, heads)
    tail_wide = spread(tail, heads)
    scaled = x * step_wide
    scaled_low = scaled.astype(BF)
    g_low = g_mixed.astype(BF)
    old = states_ref[0]
    g_new = gstate[...]
    old_low = old.astype(BF)
    g_new_low = g_new.astype(BF)
    gram = dot(c_low, b_low, ((1,), (1,)))
    across = dot(c_low, old_low, ((1,), (1,)))
    returned = dot(b_low, g_new_low, ((1,), (1,))) * tail_wide
    g_carried = g_mixed * carry_wide
    g_carried_low = g_carried.astype(BF)
    tailed_low = (scaled * tail_wide).astype(BF)

    g_gram = jnp.zeros((STRETCH, STRETCH), F32)
    lane = lax.broadcasted_iota(jnp.int32, (STRETCH, 128), 1)
    row_sum = jnp.zeros((STRETCH, 128), F32)
    col_rows = []
    parts = []
    for h in range(heads):
        cols = slice(h * P_SIZE, (h + 1) * P_SIZE)
        decay = jnp.exp(jnp.where(visible, cum[:, h : h + 1] - cum_t[h : h + 1, :], LOW))
        mixing = gram * decay
        g_mixing = dot(g_low[:, cols], scaled_low[:, cols], ((1,), (1,)))
        parts.append(dot(mixing, g_low[:, cols], ((0,), (0,))))
        g_gram = g_gram + g_mixing * decay
        both = g_mixing * mixing
        row_sum = jnp.where(lane == h, jnp.sum(both, axis=1, keepdims=True), row_sum)
        col_rows.append(jnp.sum(both, axis=0, keepdims=True))
    col_rows.append(jnp.zeros((128 - heads, STRETCH), F32))
    col_sum = jnp.transpose(jnp.concatenate(col_rows, axis=0))
    g_scaled = jnp.concatenate(parts, axis=1) + returned
    into = head_sums(g_carried * across, heads)
    outof = head_sums(scaled * returned, heads)
    state_dot = jnp.zeros((1, 128), F32)
    lane_one = lax.broadcasted_iota(jnp.int32, (1, 128), 1)
    product = g_new * old
    for h in range(heads):
        total = jnp.sum(
            jnp.sum(product[h * P_SIZE : (h + 1) * P_SIZE, :], axis=0, keepdims=True),
            axis=1,
            keepdims=True,
        )
        state_dot = jnp.where(lane_one == h, total, state_dot)
    g_c = dot(g_gram, b_low, ((1,), (0,))) + dot(g_carried_low, old_low, ((1,), (0,)))
    g_b = dot(g_gram, c_low, ((0,), (0,))) + dot(tailed_low, g_new_low, ((1,), (0,)))
    g_fresh = dot(g_carried_low, c_low, ((0,), (0,)))
    for h in range(heads):
        rows = slice(h * P_SIZE, (h + 1) * P_SIZE)
        gstate[rows, :] = (
            g_new[rows, :] * carrying[STRETCH - 1 : STRETCH, h : h + 1] + g_fresh[rows, :]
        )
    row = lax.broadcasted_iota(jnp.int32, (STRETCH, STRETCH), 0)
    col = lax.broadcasted_iota(jnp.int32, (STRETCH, STRETCH), 1)
    upper = jnp.where(col >= row, 1.0, 0.0).astype(F32)
    g_cum = row_sum - col_sum + into - outof
    g_decay = lax.dot_general(
        upper, g_cum, (((1,), (0,)), ((), ())), precision=PRECISE, preferred_element_type=F32
    ) + (
        jnp.sum(outof, axis=0, keepdims=True)
        + carrying[STRETCH - 1 : STRETCH, :] * state_dot
    )
    g_step = head_sums(x * g_scaled, heads) + g_decay * pdt_ref[1:2, :]
    g_dt = g_step * sigmoid(biased)
    gdt_ref[0:1, :] += jnp.sum(g_dt, axis=0, keepdims=True)
    gdt_ref[1:2, :] += jnp.sum(g_decay * log_decay, axis=0, keepdims=True)
    g_x = px_ref[5:6, :] * g_mixed + step_wide * g_scaled
    g_conv_x = g_x * px_ref[7:8, :] * (sig_x * (1.0 + conv_x * (1.0 - sig_x)))
    g_act = jnp.concatenate([g_b, g_c], axis=1)
    g_conv_bc = g_act * (sig_bc * (1.0 + conv_bc * (1.0 - sig_bc)))
    gx_ref[4:5, :] += jnp.sum(g_conv_x, axis=0, keepdims=True)
    gx_ref[5:6, :] += jnp.sum(g_mixed * x, axis=0, keepdims=True)
    gx_ref[6:7, :] += jnp.sum(upstream * gated * scale, axis=0, keepdims=True)
    gbc_ref[4:5, :] += jnp.sum(g_conv_bc, axis=0, keepdims=True)
    gxbuf[0:STRETCH, :] = g_conv_x
    gbcbuf[0:STRETCH, :] = g_conv_bc
    g_in_x = jnp.zeros((STRETCH, width), F32)
    g_in_bc = jnp.zeros((STRETCH, 2 * N), F32)
    for tap in range(KCONV):
        back = KCONV - 1 - tap
        rows_x = xbuf[8 - back : 8 - back + STRETCH, :]
        rows_bc = bcbuf[8 - back : 8 - back + STRETCH, :]
        later_x = gxbuf[back : back + STRETCH, :]
        later_bc = gbcbuf[back : back + STRETCH, :]
        if back:
            rows_x = jnp.where(place >= back, rows_x, 0.0)
            rows_bc = jnp.where(place >= back, rows_bc, 0.0)
            later_x = jnp.where(remain >= back, later_x, 0.0)
            later_bc = jnp.where(remain >= back, later_bc, 0.0)
        gx_ref[tap : tap + 1, :] += jnp.sum(g_conv_x * rows_x, axis=0, keepdims=True)
        gbc_ref[tap : tap + 1, :] += jnp.sum(g_conv_bc * rows_bc, axis=0, keepdims=True)
        g_in_x = g_in_x + px_ref[tap : tap + 1, :] * later_x
        g_in_bc = g_in_bc + pbc_ref[tap : tap + 1, :] * later_bc
    gxbuf[STRETCH : STRETCH + 8, :] = gxbuf[0:8, :]
    gbcbuf[STRETCH : STRETCH + 8, :] = gbcbuf[0:8, :]
    gp_ref[:, width : 2 * width] = g_in_x.astype(BF)
    gp_ref[:, 2 * width : 2 * width + 2 * N] = g_in_bc.astype(BF)
    gp_ref[:, 2 * width + 2 * N : 2 * width + 2 * N + 128] = g_dt.astype(BF)


def run_forward(projected, place, remain, px, pbc, pdt):
    total = projected.shape[0]
    width = px.shape[1]
    heads = width // P_SIZE
    blocks = total // STRETCH
    row_spec = lambda w, c: pl.BlockSpec((STRETCH, w), lambda i: (i, c))
    whole = lambda a: pl.BlockSpec(a.shape, lambda i: (0, 0))
    return pl.pallas_call(
        partial(forward_kernel, heads),
        grid=(blocks,),
        in_specs=[
            row_spec(width, 0),
            row_spec(width, 1),
            row_spec(2 * N, width // N),
            row_spec(128, (2 * width + 2 * N) // 128),
            row_spec(1, 0),
            row_spec(1, 0),
            whole(px),
            whole(pbc),
            whole(pdt),
        ],
        out_specs=[
            row_spec(width, 0),
            row_spec(width, 0),
            row_spec(1, 0),
            pl.BlockSpec((1, width, N), lambda i: (i, 0, 0)),
        ],
        out_shape=[
            jax.ShapeDtypeStruct((total, width), BF),
            jax.ShapeDtypeStruct((total, width), F32),
            jax.ShapeDtypeStruct((total, 1), F32),
            jax.ShapeDtypeStruct((blocks, width, N), F32),
        ],
        scratch_shapes=[
            pltpu.VMEM((width, N), F32),
            pltpu.VMEM((STRETCH + 8, width), F32),
            pltpu.VMEM((STRETCH + 8, 2 * N), F32),
        ],
        cost_estimate=pl.CostEstimate(
            flops=total * 256 * 1000, bytes_accessed=total * 5000, transcendentals=total * 1500
        ),
        name="scan_forward",
    )(projected, projected, projected, projected, place, remain, px, pbc, pdt)


def run_backward(projected, place, remain, mixed, g_out_low, scale, pull, states, px, pbc, pdt):
    total = projected.shape[0]
    width = px.shape[1]
    heads = width // P_SIZE
    blocks = total // STRETCH
    columns = projected.shape[1]
    rev = lambda i: blocks - 1 - i
    row_spec = lambda w, c: pl.BlockSpec((STRETCH, w), lambda i: (rev(i), c))
    prev_spec = lambda w, c: pl.BlockSpec(
        (16, w), lambda i: (jnp.maximum(rev(i) * (STRETCH // 16) - 1, 0), c)
    )
    whole = lambda a: pl.BlockSpec(a.shape, lambda i: (0, 0))
    fixed = lambda w: pl.BlockSpec((8, w), lambda i: (0, 0))
    return pl.pallas_call(
        partial(backward_kernel, heads),
        grid=(blocks,),
        in_specs=[
            row_spec(width, 0),
            row_spec(width, 1),
            row_spec(2 * N, width // N),
            row_spec(128, (2 * width + 2 * N) // 128),
            prev_spec(width, 1),
            prev_spec(2 * N, width // N),
            row_spec(1, 0),
            row_spec(1, 0),
            row_spec(width, 0),
            row_spec(width, 0),
            row_spec(1, 0),
            row_spec(1, 0),
            pl.BlockSpec((1, width, N), lambda i: (rev(i), 0, 0)),
            whole(px),
            whole(pbc),
            whole(pdt),
        ],
        out_specs=[
            row_spec(columns, 0),
            row_spec(width, 0),
            fixed(width),
            fixed(2 * N),
            fixed(128),
        ],
        out_shape=[
            jax.ShapeDtypeStruct((total, columns), BF),
            jax.ShapeDtypeStruct((total, width), BF),
            jax.ShapeDtypeStruct((8, width), F32),
            jax.ShapeDtypeStruct((8, 2 * N), F32),
            jax.ShapeDtypeStruct((8, 128), F32),
        ],
        scratch_shapes=[
            pltpu.VMEM((width, N), F32),
            pltpu.VMEM((STRETCH + 8, width), F32),
            pltpu.VMEM((STRETCH + 8, 2 * N), F32),
            pltpu.VMEM((STRETCH + 8, width), F32),
            pltpu.VMEM((STRETCH + 8, 2 * N), F32),
        ],
        cost_estimate=pl.CostEstimate(
            flops=total * 256 * 3000, bytes_accessed=total * 8000, transcendentals=total * 2000
        ),
        name="scan_backward",
    )(
        projected,
        projected,
        projected,
        projected,
        projected,
        projected,
        place,
        remain,
        mixed,
        g_out_low,
        scale,
        pull,
        states,
        px,
        pbc,
        pdt,
    )


def pad_to(values, width, axis):
    missing = width - values.shape[axis]
    if missing == 0:
        return values
    pads = [(0, 0)] * values.ndim
    pads[axis] = (0, missing)
    return jnp.pad(values, pads)


def width_sum(values):
    if lax.axis_size("width") == 2:
        return values.astype(F32) + lax.ppermute(values, "width", [(0, 1), (1, 0)]).astype(F32)
    return jnp.sum(lax.all_gather(values, "width").astype(F32), axis=0)


def per_device(
    tokens,
    cotangent,
    lengths,
    levels,
    step_count,
    weight_in,
    moment_in,
    second_in,
    weight_out,
    moment_out,
    second_out,
    small_params,
    moment_small,
    second_small,
):
    dp = lax.axis_size("dp")
    here = lax.axis_index("dp")
    rows = tokens.shape[0]
    total = rows * dp
    units = E // dp
    own_heads = H // dp
    wide = max(units, 128)
    shard = weight_in.shape[0]

    inputs_f = tokens.astype(F32)
    root = lax.rsqrt(jnp.mean(inputs_f * inputs_f, axis=1, keepdims=True) + NORM_EPS)
    g_in, g_out, conv_w, conv_b, a_log, dt_bias, d_skip = unpack(small_params)
    normed_low = (inputs_f * root * g_in).astype(BF)
    normed_all = lax.all_gather(normed_low, "dp", axis=0, tiled=True)

    weight_low = weight_in.astype(BF)
    pairs = jnp.concatenate(
        [
            weight_low[:, :E].reshape(shard, dp, units),
            weight_low[:, E : 2 * E].reshape(shard, dp, units),
        ],
        axis=2,
    ).transpose(1, 0, 2)
    own_cols = lax.all_to_all(pairs, "dp", 0, 0).reshape(D, 2 * units)
    shared = lax.all_gather(weight_low[:, 2 * E :], "dp", axis=0, tiled=True)
    own_dt = lax.dynamic_slice_in_dim(shared, 2 * N + here * own_heads, own_heads, 1)
    weight_own = jnp.concatenate(
        [
            pad_to(own_cols[:, :units], wide, 1),
            pad_to(own_cols[:, units:], wide, 1),
            shared[:, : 2 * N],
            pad_to(own_dt, 128, 1),
        ],
        axis=1,
    )
    out_weight_low = pad_to(weight_out.astype(BF), wide, 0)

    live_units = jnp.right_shift(jnp.int32(E), lax.axis_size("width") - 1 - levels[0])
    live = live_units.astype(F32)
    place, remain = row_places(lengths[0], total)
    place = place[:, None]
    remain = remain[:, None]
    own = lambda v: lax.dynamic_slice_in_dim(v, here * units, units, v.ndim - 1)
    own_h = lambda v: lax.dynamic_slice_in_dim(v, here * own_heads, own_heads, 0)
    unit_mask = (here * units + jnp.arange(units, dtype=jnp.int32) < live_units).astype(F32)
    px = pad_to(
        jnp.concatenate(
            [
                own(conv_w[:, :E]),
                own(conv_b[:E])[None],
                jnp.repeat(own_h(d_skip), P_SIZE)[None],
                own(g_out)[None],
                unit_mask[None],
            ],
            axis=0,
        ),
        wide,
        1,
    )
    pbc = pad_to(jnp.concatenate([conv_w[:, E:], conv_b[None, E:]], axis=0), 8, 0)
    pdt = pad_to(
        pad_to(jnp.stack([own_h(dt_bias), -jnp.exp(own_h(a_log))]), 128, 1), 8, 0
    )

    projected = jnp.dot(normed_all, weight_own, preferred_element_type=F32).astype(BF)
    zin, mixed, square, states = run_forward(projected, place, remain, px, pbc, pdt)

    partial_out = jnp.dot(zin, out_weight_low, preferred_element_type=F32).astype(BF)
    summed_out = lax.psum_scatter(partial_out, "dp", scatter_dimension=0, tiled=True)

    cotangent_all = lax.all_gather(cotangent, "dp", axis=0, tiled=True)
    g_out_low = lax.dot_general(
        cotangent_all, out_weight_low, (((1,), (1,)), ((), ())), preferred_element_type=F32
    )
    pull_part = jnp.sum(g_out_low * zin.astype(F32), axis=1)
    both = jnp.sum(lax.all_gather(jnp.stack([square[:, 0], pull_part]), "dp"), axis=0)
    scale = lax.rsqrt(both[0] / live + NORM_EPS)
    pull = scale * scale * scale / live * both[1]

    block_out = (
        inputs_f
        + summed_out.astype(F32)
        * lax.dynamic_slice_in_dim(scale, here * rows, rows, 0)[:, None]
    ).astype(BF)

    g_projected, out_low, gx, gbc, gdt = run_backward(
        projected,
        place,
        remain,
        mixed,
        g_out_low,
        scale[:, None],
        pull[:, None],
        states,
        px,
        pbc,
        pdt,
    )

    partial_normed = lax.dot_general(
        g_projected, weight_own, (((1,), (1,)), ((), ())), preferred_element_type=F32
    ).astype(BF)
    g_normed = lax.psum_scatter(partial_normed, "dp", scatter_dimension=0, tiled=True).astype(F32)
    g_weight = lax.dot_general(
        normed_all, g_projected, (((0,), (0,)), ((), ())), preferred_element_type=F32
    ).astype(BF)
    g_weight_out = lax.dot_general(
        out_low, cotangent_all, (((0,), (0,)), ((), ())), preferred_element_type=F32
    )[:units].astype(BF)

    g_pairs = jnp.concatenate(
        [g_weight[:, :units], g_weight[:, wide : wide + units]], axis=1
    ).reshape(dp, shard, 2 * units)
    g_pairs = lax.all_to_all(g_pairs, "dp", 0, 0).transpose(1, 0, 2)
    g_shared = lax.dynamic_update_slice_in_dim(
        pad_to(g_weight[:, 2 * wide : 2 * wide + 2 * N], SHARED, 1),
        g_weight[:, 2 * wide + 2 * N : 2 * wide + 2 * N + own_heads],
        2 * N + here * own_heads,
        1,
    )
    g_shared = lax.psum_scatter(g_shared, "dp", scatter_dimension=0, tiled=True)
    g_rows = jnp.concatenate(
        [
            g_pairs[:, :, :units].reshape(shard, E),
            g_pairs[:, :, units:].reshape(shard, E),
            g_shared,
        ],
        axis=1,
    )
    total_in = width_sum(g_rows)
    total_out = width_sum(g_weight_out)

    ratio = root * g_in
    lean = jnp.sum(g_in * g_normed * inputs_f, axis=1, keepdims=True)
    g_inputs = ratio * g_normed - inputs_f * (root * root * root / D * lean)
    grad_tokens = (cotangent.astype(F32) + g_inputs).astype(BF)
    g_g_in = jnp.sum(g_normed * inputs_f * root, axis=0)

    packed = jnp.concatenate(
        [
            g_g_in,
            gbc[:5].reshape(-1),
            gx[:5, :units].reshape(-1),
            gx[6, :units],
            jnp.sum(gx[5, :units].reshape(own_heads, P_SIZE), axis=1),
            gdt[1, :own_heads],
            gdt[0, :own_heads],
        ]
    )
    everyone = lax.all_gather(packed, "dp")
    everyone = jnp.sum(lax.all_gather(everyone, "width"), axis=0)
    cut = D + 10 * N
    common = jnp.sum(everyone[:, :cut], axis=0)
    bc_part = common[D:].reshape(5, 2 * N)
    mine = everyone[:, cut:]
    x_part = mine[:, : 5 * units].reshape(dp, 5, units).transpose(1, 0, 2).reshape(5, E)
    heads_part = mine[:, 6 * units :].reshape(dp, 3, own_heads).transpose(1, 0, 2).reshape(3, H)
    conv_part = jnp.concatenate([x_part, bc_part], axis=1)
    total_small = jnp.concatenate(
        [
            common[:D],
            mine[:, 5 * units : 6 * units].reshape(E),
            conv_part.reshape(-1),
            heads_part[1],
            heads_part[2],
            heads_part[0],
        ]
    )
    step_float = step_count[0].astype(F32)
    rate_table, decay_table = small_table()
    new_small, mom_small, sec_small = adamw_step(
        small_params, moment_small, second_small, total_small, rate_table, decay_table, step_float
    )
    new_in, mom_in, sec_in = adamw_step(
        weight_in, moment_in, second_in, total_in, MATRIX_RATE, MATRIX_DECAY, step_float
    )
    new_out, mom_out, sec_out = adamw_step(
        weight_out, moment_out, second_out, total_out, MATRIX_RATE, MATRIX_DECAY, step_float
    )
    return (
        block_out,
        grad_tokens,
        new_in,
        mom_in,
        sec_in,
        new_in.astype(BF),
        new_out,
        mom_out,
        sec_out,
        new_out.astype(BF),
        new_small,
        mom_small,
        sec_small,
    )


def solution(mesh):
    return jax.shard_map(
        per_device,
        mesh=mesh,
        in_specs=(
            P(("width", "dp"), None),
            P(("width", "dp"), None),
            P("width", None),
            P("width"),
            P(),
            P("dp", None),
            P("dp", None),
            P("dp", None),
            P("dp", None),
            P("dp", None),
            P("dp", None),
            P(),
            P(),
            P(),
        ),
        out_specs=(
            P(("width", "dp"), None),
            P(("width", "dp"), None),
            P("dp", None),
            P("dp", None),
            P("dp", None),
            P("dp", None),
            P("dp", None),
            P("dp", None),
            P("dp", None),
            P("dp", None),
            P(),
            P(),
            P(),
        ),
        check_vma=False,
    )
```

```python
from functools import partial

import jax
import jax.numpy as jnp
from jax import lax
from jax.experimental import pallas as pl
from jax.experimental.pallas import tpu as pltpu
from jax.sharding import PartitionSpec as P

D = 2048
E = 4096
H = 64
P_SIZE = 64
N = 128
KCONV = 4
STRETCH = 256
K = 4352

NORM_EPS = 1e-05
ADAM_EPS = 1e-08
BETA_ONE = 0.5
BETA_TWO = 0.5
MATRIX_RATE = 0.02
MATRIX_DECAY = 0.1
PRECISE = lax.Precision.HIGHEST
BF = jnp.bfloat16
F32 = jnp.float32
LOW = -1e30
SHARED = 2 * N + H
SPLITS = 1


def small_table():
    rate_table = jnp.concatenate(
        [
            jnp.full((D,), 0.3, F32),
            jnp.full((E,), 0.3, F32),
            jnp.full((KCONV * K,), 0.2, F32),
            jnp.full((K,), 0.2, F32),
            jnp.full((H,), 0.3, F32),
            jnp.full((H,), 1.0, F32),
            jnp.full((H,), 0.3, F32),
        ]
    )
    decay_table = jnp.concatenate(
        [
            jnp.zeros((D + E,), F32),
            jnp.full((KCONV * K,), 0.1, F32),
            jnp.zeros((K + 3 * H,), F32),
        ]
    )
    return (rate_table, decay_table)


def unpack(small_params):
    offset = D + E
    conv_w = small_params[offset : offset + KCONV * K].reshape(KCONV, K)
    offset = offset + KCONV * K
    conv_b = small_params[offset : offset + K]
    offset = offset + K
    a_log = small_params[offset : offset + H]
    dt_bias = small_params[offset + H : offset + 2 * H]
    d_skip = small_params[offset + 2 * H : offset + 3 * H]
    return (small_params[:D], small_params[D : D + E], conv_w, conv_b, a_log, dt_bias, d_skip)


def row_places(lengths_row, row_count):
    seq_ends = jnp.cumsum(lengths_row)
    at = jnp.arange(row_count, dtype=jnp.int32)
    passed = seq_ends[None, :] <= at[:, None]
    begin = jnp.max(jnp.where(passed, seq_ends[None, :], 0), axis=1)
    finish = jnp.min(jnp.where(passed, row_count, seq_ends[None, :]), axis=1)
    return (at - begin, finish - 1 - at)


def adamw_step(weight, moment, second, grad, rate, decay, step_float):
    first_new = BETA_ONE * moment + (1.0 - BETA_ONE) * grad
    second_new = BETA_TWO * second + (1.0 - BETA_TWO) * grad * grad
    first_hat = first_new / (1.0 - jnp.power(BETA_ONE, step_float))
    second_hat = second_new / (1.0 - jnp.power(BETA_TWO, step_float))
    return (
        weight - rate * (first_hat / (jnp.sqrt(second_hat) + ADAM_EPS) + decay * weight),
        first_new,
        second_new,
    )


def sigmoid(v):
    return 1.0 / (1.0 + jnp.exp(-v))


def dot(a, b, dims):
    return lax.dot_general(
        a.astype(BF), b.astype(BF), (dims, ((), ())), preferred_element_type=F32
    )


def spread(columns, heads):
    return jnp.concatenate(
        [
            jnp.broadcast_to(columns[:, h : h + 1], (columns.shape[0], P_SIZE))
            for h in range(heads)
        ],
        axis=1,
    )


def head_sums(values, heads):
    lane = lax.broadcasted_iota(jnp.int32, (values.shape[0], 128), 1)
    total = jnp.zeros((values.shape[0], 128), F32)
    for h in range(heads):
        part = jnp.sum(values[:, h * P_SIZE : (h + 1) * P_SIZE], axis=1, keepdims=True)
        total = jnp.where(lane == h, part, total)
    return total


def convolve(buffer, weights, bias, place):
    total = bias + jnp.zeros((STRETCH, buffer.shape[1]), F32)
    for tap in range(KCONV):
        back = KCONV - 1 - tap
        rows = buffer[8 - back : 8 - back + STRETCH, :]
        if back:
            rows = jnp.where(place >= back, rows, 0.0)
        total = total + weights[tap : tap + 1, :] * rows
    return total


def block_terms(place, remain, dt_in, pdt):
    row = lax.broadcasted_iota(jnp.int32, (STRETCH, STRETCH), 0)
    col = lax.broadcasted_iota(jnp.int32, (STRETCH, STRETCH), 1)
    at = lax.broadcasted_iota(jnp.int32, (STRETCH, 1), 0)
    visible = (col <= row) & (col >= at - place)
    biased = dt_in + pdt[0:1, :]
    step = jnp.maximum(biased, 0.0) + jnp.log1p(jnp.exp(-jnp.abs(biased)))
    log_decay = step * pdt[1:2, :]
    lower = jnp.where(col <= row, 1.0, 0.0).astype(F32)
    cum = lax.dot_general(
        lower, log_decay, (((1,), (0,)), ((), ())), precision=PRECISE, preferred_element_type=F32
    )
    cum_t = jnp.transpose(cum)
    carrying = jnp.where(place >= at + 1, jnp.exp(cum), 0.0)
    tail_ok = remain >= STRETCH - 1 - at
    tail = jnp.exp(jnp.where(tail_ok, cum[STRETCH - 1 : STRETCH, :] - cum, LOW))
    return visible, biased, step, log_decay, cum, cum_t, carrying, tail


def forward_kernel(
    heads,
    gate_ref,
    x_ref,
    bc_ref,
    dt_ref,
    place_ref,
    remain_ref,
    px_ref,
    pbc_ref,
    pdt_ref,
    zin_ref,
    mixed_ref,
    square_ref,
    states_ref,
    state,
    xbuf,
    bcbuf,
):
    @pl.when(pl.program_id(0) == 0)
    def _():
        state[...] = jnp.zeros_like(state)
        xbuf[0:8, :] = jnp.zeros((8, xbuf.shape[1]), F32)
        bcbuf[0:8, :] = jnp.zeros((8, bcbuf.shape[1]), F32)

    place = place_ref[...]
    remain = remain_ref[...]
    xbuf[8 : 8 + STRETCH, :] = x_ref[...].astype(F32)
    bcbuf[8 : 8 + STRETCH, :] = bc_ref[...].astype(F32)
    conv_x = convolve(xbuf, px_ref[0:4, :], px_ref[4:5, :], place)
    conv_bc = convolve(bcbuf, pbc_ref[0:4, :], pbc_ref[4:5, :], place)
    xbuf[0:8, :] = xbuf[STRETCH : STRETCH + 8, :]
    bcbuf[0:8, :] = bcbuf[STRETCH : STRETCH + 8, :]
    x = conv_x * sigmoid(conv_x) * px_ref[7:8, :]
    act_bc = conv_bc * sigmoid(conv_bc)
    b_low = act_bc[:, :N].astype(BF)
    c_low = act_bc[:, N:].astype(BF)
    visible, _, step, _, cum, cum_t, carrying, tail = block_terms(
        place, remain, dt_ref[...].astype(F32), pdt_ref[...]
    )
    scaled = x * spread(step, heads)
    scaled_low = scaled.astype(BF)
    gram = dot(c_low, b_low, ((1,), (1,)))
    old = state[...]
    states_ref[0] = old
    across = dot(c_low, old, ((1,), (1,))) * spread(carrying, heads)
    parts = []
    for h in range(heads):
        decay = jnp.exp(jnp.where(visible, cum[:, h : h + 1] - cum_t[h : h + 1, :], LOW))
        parts.append(
            dot(gram * decay, scaled_low[:, h * P_SIZE : (h + 1) * P_SIZE], ((1,), (0,)))
        )
    mixed = jnp.concatenate(parts, axis=1) + across + px_ref[5:6, :] * x
    fresh = dot(scaled * spread(tail, heads), b_low, ((0,), (0,)))
    for h in range(heads):
        rows = slice(h * P_SIZE, (h + 1) * P_SIZE)
        state[rows, :] = (
            old[rows, :] * carrying[STRETCH - 1 : STRETCH, h : h + 1] + fresh[rows, :]
        )
    gate = gate_ref[...].astype(F32)
    gated = mixed * (gate * sigmoid(gate))
    mixed_ref[...] = mixed
    zin_ref[...] = (gated * px_ref[6:7, :]).astype(BF)
    square_ref[...] = jnp.sum(gated * gated, axis=1, keepdims=True)


def backward_kernel(
    heads,
    gate_ref,
    x_ref,
    bc_ref,
    dt_ref,
    xprev_ref,
    bcprev_ref,
    place_ref,
    remain_ref,
    mixed_ref,
    gout_ref,
    scale_ref,
    pull_ref,
    states_ref,
    px_ref,
    pbc_ref,
    pdt_ref,
    gstate_in,
    gx_in,
    gbc_in,
    gdt_in,
    *rest,
):
    gp_ref, low_ref, gstate, gx_ref, gbc_ref, gdt_ref, xbuf, bcbuf, gxbuf, gbcbuf = rest[-10:]
    width = x_ref.shape[1]

    @pl.when(pl.program_id(0) == 0)
    def _():
        gstate[...] = gstate_in[...]
        gxbuf[STRETCH : STRETCH + 8, :] = gx_in[8:16, :]
        gbcbuf[STRETCH : STRETCH + 8, :] = gbc_in[8:16, :]
        gx_ref[...] = gx_in[...]
        gbc_ref[...] = gbc_in[...]
        gdt_ref[...] = gdt_in[...]

    place = place_ref[...]
    remain = remain_ref[...]
    xbuf[0:8, :] = xprev_ref[8:16, :].astype(F32)
    bcbuf[0:8, :] = bcprev_ref[8:16, :].astype(F32)
    xbuf[8 : 8 + STRETCH, :] = x_ref[...].astype(F32)
    bcbuf[8 : 8 + STRETCH, :] = bc_ref[...].astype(F32)
    conv_x = convolve(xbuf, px_ref[0:4, :], px_ref[4:5, :], place)
    conv_bc = convolve(bcbuf, pbc_ref[0:4, :], pbc_ref[4:5, :], place)
    sig_x = sigmoid(conv_x)
    sig_bc = sigmoid(conv_bc)
    x = conv_x * sig_x * px_ref[7:8, :]
    act_bc = conv_bc * sig_bc
    b_low = act_bc[:, :N].astype(BF)
    c_low = act_bc[:, N:].astype(BF)
    visible, biased, step, log_decay, cum, cum_t, carrying, tail = block_terms(
        place, remain, dt_ref[...].astype(F32), pdt_ref[...]
    )

    gate = gate_ref[...].astype(F32)
    sig = sigmoid(gate)
    silu = gate * sig
    mixed = mixed_ref[...]
    gated = mixed * silu
    g_out = px_ref[6:7, :]
    scale = scale_ref[...]
    upstream = gout_ref[...]
    low_ref[...] = (gated * scale * g_out).astype(BF)
    g_gated = scale * g_out * upstream - gated * pull_ref[...]
    g_mixed = g_gated * silu
    gp_ref[:, 0:width] = (g_gated * mixed * (sig * (1.0 + gate * (1.0 - sig)))).astype(BF)

    step_wide = spread(step, heads)
    carry_wide = spread(carrying, heads)
    tail_wide = spread(tail, heads)
    scaled = x * step_wide
    scaled_low = scaled.astype(BF)
    g_low = g_mixed.astype(BF)
    old = states_ref[0]
    g_new = gstate[...]
    old_low = old.astype(BF)
    g_new_low = g_new.astype(BF)
    gram = dot(c_low, b_low, ((1,), (1,)))
    across = dot(c_low, old_low, ((1,), (1,)))
    returned = dot(b_low, g_new_low, ((1,), (1,))) * tail_wide
    g_carried = g_mixed * carry_wide
    g_carried_low = g_carried.astype(BF)
    tailed_low = (scaled * tail_wide).astype(BF)

    g_gram = jnp.zeros((STRETCH, STRETCH), F32)
    lane = lax.broadcasted_iota(jnp.int32, (STRETCH, 128), 1)
    row_sum = jnp.zeros((STRETCH, 128), F32)
    col_rows = []
    parts = []
    for h in range(heads):
        cols = slice(h * P_SIZE, (h + 1) * P_SIZE)
        decay = jnp.exp(jnp.where(visible, cum[:, h : h + 1] - cum_t[h : h + 1, :], LOW))
        mixing = gram * decay
        g_mixing = dot(g_low[:, cols], scaled_low[:, cols], ((1,), (1,)))
        parts.append(dot(mixing, g_low[:, cols], ((0,), (0,))))
        g_gram = g_gram + g_mixing * decay
        both = g_mixing * mixing
        row_sum = jnp.where(lane == h, jnp.sum(both, axis=1, keepdims=True), row_sum)
        col_rows.append(jnp.sum(both, axis=0, keepdims=True))
    col_rows.append(jnp.zeros((128 - heads, STRETCH), F32))
    col_sum = jnp.transpose(jnp.concatenate(col_rows, axis=0))
    g_scaled = jnp.concatenate(parts, axis=1) + returned
    into = head_sums(g_carried * across, heads)
    outof = head_sums(scaled * returned, heads)
    state_dot = jnp.zeros((1, 128), F32)
    lane_one = lax.broadcasted_iota(jnp.int32, (1, 128), 1)
    product = g_new * old
    for h in range(heads):
        total = jnp.sum(
            jnp.sum(product[h * P_SIZE : (h + 1) * P_SIZE, :], axis=0, keepdims=True),
            axis=1,
            keepdims=True,
        )
        state_dot = jnp.where(lane_one == h, total, state_dot)
    g_c = dot(g_gram, b_low, ((1,), (0,))) + dot(g_carried_low, old_low, ((1,), (0,)))
    g_b = dot(g_gram, c_low, ((0,), (0,))) + dot(tailed_low, g_new_low, ((1,), (0,)))
    g_fresh = dot(g_carried_low, c_low, ((0,), (0,)))
    for h in range(heads):
        rows = slice(h * P_SIZE, (h + 1) * P_SIZE)
        gstate[rows, :] = (
            g_new[rows, :] * carrying[STRETCH - 1 : STRETCH, h : h + 1] + g_fresh[rows, :]
        )
    row = lax.broadcasted_iota(jnp.int32, (STRETCH, STRETCH), 0)
    col = lax.broadcasted_iota(jnp.int32, (STRETCH, STRETCH), 1)
    upper = jnp.where(col >= row, 1.0, 0.0).astype(F32)
    g_cum = row_sum - col_sum + into - outof
    g_decay = lax.dot_general(
        upper, g_cum, (((1,), (0,)), ((), ())), precision=PRECISE, preferred_element_type=F32
    ) + (
        jnp.sum(outof, axis=0, keepdims=True)
        + carrying[STRETCH - 1 : STRETCH, :] * state_dot
    )
    g_step = head_sums(x * g_scaled, heads) + g_decay * pdt_ref[1:2, :]
    g_dt = g_step * sigmoid(biased)
    gdt_ref[0:1, :] += jnp.sum(g_dt, axis=0, keepdims=True)
    gdt_ref[1:2, :] += jnp.sum(g_decay * log_decay, axis=0, keepdims=True)
    g_x = px_ref[5:6, :] * g_mixed + step_wide * g_scaled
    g_conv_x = g_x * px_ref[7:8, :] * (sig_x * (1.0 + conv_x * (1.0 - sig_x)))
    g_act = jnp.concatenate([g_b, g_c], axis=1)
    g_conv_bc = g_act * (sig_bc * (1.0 + conv_bc * (1.0 - sig_bc)))
    gx_ref[4:5, :] += jnp.sum(g_conv_x, axis=0, keepdims=True)
    gx_ref[5:6, :] += jnp.sum(g_mixed * x, axis=0, keepdims=True)
    gx_ref[6:7, :] += jnp.sum(upstream * gated * scale, axis=0, keepdims=True)
    gbc_ref[4:5, :] += jnp.sum(g_conv_bc, axis=0, keepdims=True)
    gxbuf[0:STRETCH, :] = g_conv_x
    gbcbuf[0:STRETCH, :] = g_conv_bc
    g_in_x = jnp.zeros((STRETCH, width), F32)
    g_in_bc = jnp.zeros((STRETCH, 2 * N), F32)
    for tap in range(KCONV):
        back = KCONV - 1 - tap
        rows_x = xbuf[8 - back : 8 - back + STRETCH, :]
        rows_bc = bcbuf[8 - back : 8 - back + STRETCH, :]
        later_x = gxbuf[back : back + STRETCH, :]
        later_bc = gbcbuf[back : back + STRETCH, :]
        if back:
            rows_x = jnp.where(place >= back, rows_x, 0.0)
            rows_bc = jnp.where(place >= back, rows_bc, 0.0)
            later_x = jnp.where(remain >= back, later_x, 0.0)
            later_bc = jnp.where(remain >= back, later_bc, 0.0)
        gx_ref[tap : tap + 1, :] += jnp.sum(g_conv_x * rows_x, axis=0, keepdims=True)
        gbc_ref[tap : tap + 1, :] += jnp.sum(g_conv_bc * rows_bc, axis=0, keepdims=True)
        g_in_x = g_in_x + px_ref[tap : tap + 1, :] * later_x
        g_in_bc = g_in_bc + pbc_ref[tap : tap + 1, :] * later_bc
    gxbuf[STRETCH : STRETCH + 8, :] = g_conv_x[0:8, :]
    gbcbuf[STRETCH : STRETCH + 8, :] = g_conv_bc[0:8, :]
    gx_ref[8:16, :] = g_conv_x[0:8, :]
    gbc_ref[8:16, :] = g_conv_bc[0:8, :]
    gp_ref[:, width : 2 * width] = g_in_x.astype(BF)
    gp_ref[:, 2 * width : 2 * width + 2 * N] = g_in_bc.astype(BF)
    gp_ref[:, 2 * width + 2 * N : 2 * width + 2 * N + 128] = g_dt.astype(BF)


def run_forward(projected, place, remain, px, pbc, pdt):
    total = projected.shape[0]
    width = px.shape[1]
    heads = width // P_SIZE
    blocks = total // STRETCH
    row_spec = lambda w, c: pl.BlockSpec((STRETCH, w), lambda i: (i, c))
    whole = lambda a: pl.BlockSpec(a.shape, lambda i: (0, 0))
    return pl.pallas_call(
        partial(forward_kernel, heads),
        grid=(blocks,),
        in_specs=[
            row_spec(width, 0),
            row_spec(width, 1),
            row_spec(2 * N, width // N),
            row_spec(128, (2 * width + 2 * N) // 128),
            row_spec(1, 0),
            row_spec(1, 0),
            whole(px),
            whole(pbc),
            whole(pdt),
        ],
        out_specs=[
            row_spec(width, 0),
            row_spec(width, 0),
            row_spec(1, 0),
            pl.BlockSpec((1, width, N), lambda i: (i, 0, 0)),
        ],
        out_shape=[
            jax.ShapeDtypeStruct((total, width), BF),
            jax.ShapeDtypeStruct((total, width), F32),
            jax.ShapeDtypeStruct((total, 1), F32),
            jax.ShapeDtypeStruct((blocks, width, N), F32),
        ],
        scratch_shapes=[
            pltpu.VMEM((width, N), F32),
            pltpu.VMEM((STRETCH + 8, width), F32),
            pltpu.VMEM((STRETCH + 8, 2 * N), F32),
        ],
        cost_estimate=pl.CostEstimate(
            flops=total * 256 * 1000, bytes_accessed=total * 5000, transcendentals=total * 1500
        ),
        name="scan_forward",
    )(projected, projected, projected, projected, place, remain, px, pbc, pdt)


def run_backward(carried, first, count, projected, rows_in, states, px, pbc, pdt):
    total = projected.shape[0]
    width = px.shape[1]
    heads = width // P_SIZE
    columns = projected.shape[1]
    rev = lambda i: first + count - 1 - i
    row_spec = lambda w, c: pl.BlockSpec((STRETCH, w), lambda i: (rev(i), c))
    prev_spec = lambda w, c: pl.BlockSpec(
        (16, w), lambda i: (jnp.maximum(rev(i) * (STRETCH // 16) - 1, 0), c)
    )
    whole = lambda a: pl.BlockSpec(a.shape, lambda i: (0, 0))
    fixed = lambda r, w: pl.BlockSpec((r, w), lambda i: (0, 0))
    place, remain, mixed, g_out_low, scale, pull = rows_in
    gstate, gx, gbc, gdt = carried[:4]
    filled = tuple(carried[4:])
    operands = (
        (projected,) * 6
        + (place, remain, mixed, g_out_low, scale, pull, states, px, pbc, pdt)
        + (gstate, gx, gbc, gdt)
        + filled
    )
    results = pl.pallas_call(
        partial(backward_kernel, heads),
        grid=(count,),
        in_specs=[
            row_spec(width, 0),
            row_spec(width, 1),
            row_spec(2 * N, width // N),
            row_spec(128, (2 * width + 2 * N) // 128),
            prev_spec(width, 1),
            prev_spec(2 * N, width // N),
            row_spec(1, 0),
            row_spec(1, 0),
            row_spec(width, 0),
            row_spec(width, 0),
            row_spec(1, 0),
            row_spec(1, 0),
            pl.BlockSpec((1, width, N), lambda i: (rev(i), 0, 0)),
            whole(px),
            whole(pbc),
            whole(pdt),
            whole(gstate),
            whole(gx),
            whole(gbc),
            whole(gdt),
        ]
        + [pl.BlockSpec(memory_space=pl.ANY)] * len(filled),
        out_specs=[
            row_spec(columns, 0),
            row_spec(width, 0),
            fixed(width, N),
            fixed(16, width),
            fixed(16, 2 * N),
            fixed(8, 128),
        ],
        out_shape=[
            jax.ShapeDtypeStruct((total, columns), BF),
            jax.ShapeDtypeStruct((total, width), BF),
            jax.ShapeDtypeStruct((width, N), F32),
            jax.ShapeDtypeStruct((16, width), F32),
            jax.ShapeDtypeStruct((16, 2 * N), F32),
            jax.ShapeDtypeStruct((8, 128), F32),
        ],
        scratch_shapes=[
            pltpu.VMEM((STRETCH + 8, width), F32),
            pltpu.VMEM((STRETCH + 8, 2 * N), F32),
            pltpu.VMEM((STRETCH + 8, width), F32),
            pltpu.VMEM((STRETCH + 8, 2 * N), F32),
        ],
        input_output_aliases={20: 0, 21: 1} if filled else {},
        cost_estimate=pl.CostEstimate(
            flops=count * STRETCH * 256 * 3000,
            bytes_accessed=count * STRETCH * 8000,
            transcendentals=count * STRETCH * 2000,
        ),
        name="scan_backward",
    )(*operands)
    return tuple(results[2:]) + tuple(results[:2])


def after(value, *others):
    return lax.optimization_barrier((value, others))[0]


def ring_chips():
    return [(z * 2 + x) for x, z in [(0, 0), (0, 1), (0, 2), (0, 3), (1, 3), (1, 2), (1, 1), (1, 0)]]


def hop(values, steps):
    chips = ring_chips()
    count = len(chips)
    pairs = [
        (2 * chips[p] + core, 2 * chips[(p + steps) % count] + core)
        for p in range(count)
        for core in (0, 1)
    ]
    return lax.ppermute(values, "dp", pairs)


def swap(values):
    return lax.ppermute(values, "dp", [(i, i ^ 1) for i in range(lax.axis_size("dp"))])


def ring_place():
    here = lax.axis_index("dp")
    core = here % 2
    chip = here // 2
    spot = jnp.where(chip % 2 == 0, chip // 2, 7 - chip // 2)
    return core, spot


def ring_chip(spot):
    spot = spot % 8
    return jnp.where(spot < 4, spot * 2, (7 - spot) * 2 + 1)


def gather_rows(values, pieces=2):
    if lax.axis_size("dp") != 16:
        return lax.all_gather(values, "dp", axis=0, tiled=True)
    rows = values.shape[0]
    core, spot = ring_place()
    chip = ring_chip(spot)
    out = jnp.zeros((16 * rows,) + values.shape[1:], values.dtype)

    def put(out, part, device, offset):
        return lax.dynamic_update_slice_in_dim(out, part, device * rows + offset, 0)

    out = put(out, values, 2 * chip + core, 0)
    out = put(out, swap(values), 2 * chip + 1 - core, 0)
    size = rows // pieces
    ahead = [values[i * size : (i + 1) * size] for i in range(pieces)]
    behind = list(ahead)
    for step in range(1, 5):
        for i in range(pieces):
            for way, held in ((1, ahead), (-1, behind)):
                part, offset = held[i], i * size
                if step == 4:
                    half = size // 2
                    part = part[:half] if way == 1 else part[half:]
                    offset = offset + (0 if way == 1 else half)
                part = hop(part, way)
                held[i] = part
                source = ring_chip(spot - way * step)
                out = put(out, part, 2 * source + core, offset)
                out = put(out, swap(part), 2 * source + 1 - core, offset)
    return out


def scatter_product(left, right, first, second):
    total = left.shape[0]
    if lax.axis_size("dp") != 16:
        full = jnp.dot(left, right, preferred_element_type=F32).astype(BF)
        return lax.psum_scatter(full, "dp", scatter_dimension=0, tiled=True).astype(F32)
    core, spot = ring_place()
    half = right.shape[1] // 2
    mine = after(lax.dynamic_slice_in_dim(right, core * half, half, 1), first)
    theirs = swap(lax.dynamic_slice_in_dim(right, (1 - core) * half, half, 1))
    product = jnp.dot(left, mine, preferred_element_type=F32) + jnp.dot(
        swap(left), theirs, preferred_element_type=F32
    )
    rows = total // 8
    product = product.reshape(8, rows, half)
    done = ring_sum(
        lambda steps: lax.dynamic_index_in_dim(product, ring_chip(spot + steps), 0, False),
        rows,
        second,
    )
    own = rows // 2
    kept = lax.dynamic_slice_in_dim(done, core * own, own, 0)
    got = swap(lax.dynamic_slice_in_dim(done, (1 - core) * own, own, 0))
    first = core == 0
    return jnp.concatenate(
        [jnp.where(first, kept, got), jnp.where(first, got, kept)], axis=1
    )


def scatter_rows(values):
    if lax.axis_size("dp") != 16:
        return lax.psum_scatter(values, "dp", scatter_dimension=0, tiled=True).astype(F32)
    core, spot = ring_place()
    rows = values.shape[0] // 16
    split = values.reshape(8, 2, rows, values.shape[1])
    pick = lambda c: lax.dynamic_index_in_dim(split, c, 1, False)
    both = pick(core).astype(F32) + swap(pick(1 - core)).astype(F32)
    return ring_sum(
        lambda steps: lax.dynamic_index_in_dim(both, ring_chip(spot + steps), 0, False), rows
    )


def ring_sum(part, rows, second=None):
    mid = rows // 2
    far = part(4).astype(BF)
    up = hop(far[:mid], 1).astype(F32)
    down = hop(far[mid:], -1).astype(F32)
    near = part(3)
    up = jnp.concatenate([near[:mid] + up, near[mid:]], axis=0)
    near = part(-3)
    down = jnp.concatenate([near[:mid], near[mid:] + down], axis=0)
    if second is not None:
        up, down, _ = lax.optimization_barrier((up, down, second))
    for step in (2, 1):
        up = part(step) + hop(up.astype(BF), 1).astype(F32)
        down = part(-step) + hop(down.astype(BF), -1).astype(F32)
    return part(0) + hop(up.astype(BF), 1).astype(F32) + hop(down.astype(BF), -1).astype(F32)


def tree_sum(values):
    if lax.axis_size("dp") != 16 or lax.axis_size("width") != 2:
        return lax.psum(values, ("width", "dp"))
    for bit in (1, 2, 4, 8):
        values = values + lax.ppermute(values, "dp", [(i, i ^ bit) for i in range(16)])
    return values + lax.ppermute(values, "width", [(0, 1), (1, 0)])


def pad_to(values, width, axis):
    missing = width - values.shape[axis]
    if missing == 0:
        return values
    pads = [(0, 0)] * values.ndim
    pads[axis] = (0, missing)
    return jnp.pad(values, pads)


def width_sum(values):
    if lax.axis_size("width") == 2:
        return values.astype(F32) + lax.ppermute(values, "width", [(0, 1), (1, 0)]).astype(F32)
    return jnp.sum(lax.all_gather(values, "width").astype(F32), axis=0)


def per_device(
    tokens,
    cotangent,
    lengths,
    levels,
    step_count,
    weight_in,
    moment_in,
    second_in,
    weight_out,
    moment_out,
    second_out,
    small_params,
    moment_small,
    second_small,
):
    dp = lax.axis_size("dp")
    here = lax.axis_index("dp")
    rows = tokens.shape[0]
    total = rows * dp
    units = E // dp
    own_heads = H // dp
    wide = max(units, 128)
    shard = weight_in.shape[0]

    inputs_f = tokens.astype(F32)
    root = lax.rsqrt(jnp.mean(inputs_f * inputs_f, axis=1, keepdims=True) + NORM_EPS)
    g_in, g_out, conv_w, conv_b, a_log, dt_bias, d_skip = unpack(small_params)
    normed_low = (inputs_f * root * g_in).astype(BF)
    normed_all = lax.all_gather(normed_low, "dp", axis=0, tiled=True)

    weight_low = weight_in.astype(BF)
    pairs = jnp.concatenate(
        [
            weight_low[:, :E].reshape(shard, dp, units),
            weight_low[:, E : 2 * E].reshape(shard, dp, units),
        ],
        axis=2,
    ).transpose(1, 0, 2)
    own_cols = lax.all_to_all(pairs, "dp", 0, 0).reshape(D, 2 * units)
    shared = gather_rows(weight_low[:, 2 * E :], 1)
    own_dt = lax.dynamic_slice_in_dim(shared, 2 * N + here * own_heads, own_heads, 1)
    weight_own = jnp.concatenate(
        [
            pad_to(own_cols[:, :units], wide, 1),
            pad_to(own_cols[:, units:], wide, 1),
            shared[:, : 2 * N],
            pad_to(own_dt, 128, 1),
        ],
        axis=1,
    )
    out_weight_low = pad_to(weight_out.astype(BF), wide, 0)

    live_units = jnp.right_shift(jnp.int32(E), lax.axis_size("width") - 1 - levels[0])
    live = live_units.astype(F32)
    place, remain = row_places(lengths[0], total)
    place = place[:, None]
    remain = remain[:, None]
    own = lambda v: lax.dynamic_slice_in_dim(v, here * units, units, v.ndim - 1)
    own_h = lambda v: lax.dynamic_slice_in_dim(v, here * own_heads, own_heads, 0)
    unit_mask = (here * units + jnp.arange(units, dtype=jnp.int32) < live_units).astype(F32)
    px = pad_to(
        jnp.concatenate(
            [
                own(conv_w[:, :E]),
                own(conv_b[:E])[None],
                jnp.repeat(own_h(d_skip), P_SIZE)[None],
                own(g_out)[None],
                unit_mask[None],
            ],
            axis=0,
        ),
        wide,
        1,
    )
    pbc = pad_to(jnp.concatenate([conv_w[:, E:], conv_b[None, E:]], axis=0), 8, 0)
    pdt = pad_to(
        pad_to(jnp.stack([own_h(dt_bias), -jnp.exp(own_h(a_log))]), 128, 1), 8, 0
    )

    projected = jnp.dot(normed_all, weight_own, preferred_element_type=F32).astype(BF)
    zin, mixed, square, states = run_forward(projected, place, remain, px, pbc, pdt)

    partial_out = jnp.dot(zin, out_weight_low, preferred_element_type=F32).astype(BF)
    summed_out = lax.psum_scatter(partial_out, "dp", scatter_dimension=0, tiled=True)

    later = after(cotangent, normed_all, weight_own)
    cotangent_all = lax.all_gather(later, "dp", axis=0, tiled=True)
    g_out_low = lax.dot_general(
        cotangent_all, out_weight_low, (((1,), (1,)), ((), ())), preferred_element_type=F32
    )
    pull_part = jnp.sum(g_out_low * zin.astype(F32), axis=1)
    both = jnp.sum(lax.all_gather(jnp.stack([square[:, 0], pull_part]), "dp"), axis=0)
    scale = lax.rsqrt(both[0] / live + NORM_EPS)
    pull = scale * scale * scale / live * both[1]

    block_out = (
        inputs_f
        + summed_out.astype(F32)
        * lax.dynamic_slice_in_dim(scale, here * rows, rows, 0)[:, None]
    ).astype(BF)

    rows_in = (place, remain, mixed, g_out_low, scale[:, None], pull[:, None])
    carried = (
        jnp.zeros((wide, N), F32),
        jnp.zeros((16, wide), F32),
        jnp.zeros((16, 2 * N), F32),
        jnp.zeros((8, 128), F32),
    )
    span = total // STRETCH // SPLITS
    for turn in reversed(range(SPLITS)):
        carried = run_backward(
            carried, turn * span, span, projected, rows_in, states, px, pbc, pdt
        )
    _, gx, gbc, gdt, g_projected, out_low = carried

    g_weight = lax.dot_general(
        normed_all, g_projected, (((0,), (0,)), ((), ())), preferred_element_type=F32
    ).astype(BF)
    g_weight_out = lax.dot_general(
        out_low, cotangent_all, (((0,), (0,)), ((), ())), preferred_element_type=F32
    )[:units].astype(BF)
    total_out = width_sum(g_weight_out)

    g_pairs = lax.all_to_all(
        jnp.concatenate(
            [g_weight[:, :units], g_weight[:, wide : wide + units]], axis=1
        ).reshape(dp, shard, 2 * units),
        "dp",
        0,
        0,
    )
    g_normed = scatter_product(g_projected, weight_own.T, g_weight, g_pairs)
    sum_pairs = width_sum(g_pairs).transpose(1, 0, 2)
    totals = [
        sum_pairs[:, :, :units].reshape(shard, E),
        sum_pairs[:, :, units:].reshape(shard, E),
    ]
    g_shared = lax.dynamic_update_slice_in_dim(
        pad_to(g_weight[:, 2 * wide : 2 * wide + 2 * N], SHARED, 1),
        g_weight[:, 2 * wide + 2 * N : 2 * wide + 2 * N + own_heads],
        2 * N + here * own_heads,
        1,
    )
    totals.append(width_sum(scatter_rows(g_shared).astype(BF)))
    total_in = jnp.concatenate(totals, axis=1)

    ratio = root * g_in
    lean = jnp.sum(g_in * g_normed * inputs_f, axis=1, keepdims=True)
    g_inputs = ratio * g_normed - inputs_f * (root * root * root / D * lean)
    grad_tokens = (cotangent.astype(F32) + g_inputs).astype(BF)
    g_g_in = jnp.sum(g_normed * inputs_f * root, axis=0)

    def placed(part, size):
        spots = jnp.zeros(part.shape[:-1] + (size,), F32)
        return lax.dynamic_update_slice_in_dim(
            spots, part, here * part.shape[-1], part.ndim - 1
        )

    conv_part = jnp.concatenate([placed(gx[:5, :units], E), gbc[:5]], axis=1)
    early = jnp.concatenate(
        [
            placed(gx[6, :units], E),
            conv_part.reshape(-1),
            placed(gdt[1, :own_heads], H),
            placed(gdt[0, :own_heads], H),
            placed(jnp.sum(gx[5, :units].reshape(own_heads, P_SIZE), axis=1), H),
        ]
    )
    total_small = jnp.concatenate([tree_sum(g_g_in), tree_sum(early)])
    step_float = step_count[0].astype(F32)
    rate_table, decay_table = small_table()
    new_small, mom_small, sec_small = adamw_step(
        small_params, moment_small, second_small, total_small, rate_table, decay_table, step_float
    )
    new_in, mom_in, sec_in = adamw_step(
        weight_in, moment_in, second_in, total_in, MATRIX_RATE, MATRIX_DECAY, step_float
    )
    new_out, mom_out, sec_out = adamw_step(
        weight_out, moment_out, second_out, total_out, MATRIX_RATE, MATRIX_DECAY, step_float
    )
    return (
        block_out,
        grad_tokens,
        new_in,
        mom_in,
        sec_in,
        new_in.astype(BF),
        new_out,
        mom_out,
        sec_out,
        new_out.astype(BF),
        new_small,
        mom_small,
        sec_small,
    )


def solution(mesh):
    return jax.shard_map(
        per_device,
        mesh=mesh,
        in_specs=(
            P(("width", "dp"), None),
            P(("width", "dp"), None),
            P("width", None),
            P("width"),
            P(),
            P("dp", None),
            P("dp", None),
            P("dp", None),
            P("dp", None),
            P("dp", None),
            P("dp", None),
            P(),
            P(),
            P(),
        ),
        out_specs=(
            P(("width", "dp"), None),
            P(("width", "dp"), None),
            P("dp", None),
            P("dp", None),
            P("dp", None),
            P("dp", None),
            P("dp", None),
            P("dp", None),
            P("dp", None),
            P("dp", None),
            P(),
            P(),
            P(),
        ),
        check_vma=False,
    )
```

```python
from functools import partial

import jax
import jax.numpy as jnp
from jax import lax
from jax.experimental import pallas as pl
from jax.experimental.layout import Layout, with_layout_constraint
from jax.experimental.pallas import tpu as pltpu
from jax.sharding import PartitionSpec as P

D = 2048
E = 4096
H = 64
P_SIZE = 64
N = 128
KCONV = 4
STRETCH = 256
K = 4352

NORM_EPS = 1e-05
ADAM_EPS = 1e-08
BETA_ONE = 0.5
BETA_TWO = 0.5
MATRIX_RATE = 0.02
MATRIX_DECAY = 0.1
PRECISE = lax.Precision.HIGHEST
BF = jnp.bfloat16
F32 = jnp.float32
LOW = -1e30
SHARED = 2 * N + H
BACK_PARTS = 1
FRONT_PARTS = 1


def small_table():
    rate_table = jnp.concatenate(
        [
            jnp.full((D,), 0.3, F32),
            jnp.full((E,), 0.3, F32),
            jnp.full((KCONV * K,), 0.2, F32),
            jnp.full((K,), 0.2, F32),
            jnp.full((H,), 0.3, F32),
            jnp.full((H,), 1.0, F32),
            jnp.full((H,), 0.3, F32),
        ]
    )
    decay_table = jnp.concatenate(
        [
            jnp.zeros((D + E,), F32),
            jnp.full((KCONV * K,), 0.1, F32),
            jnp.zeros((K + 3 * H,), F32),
        ]
    )
    return (rate_table, decay_table)


def unpack(small_params):
    offset = D + E
    conv_w = small_params[offset : offset + KCONV * K].reshape(KCONV, K)
    offset = offset + KCONV * K
    conv_b = small_params[offset : offset + K]
    offset = offset + K
    a_log = small_params[offset : offset + H]
    dt_bias = small_params[offset + H : offset + 2 * H]
    d_skip = small_params[offset + 2 * H : offset + 3 * H]
    return (small_params[:D], small_params[D : D + E], conv_w, conv_b, a_log, dt_bias, d_skip)


def row_places(lengths_row, row_count):
    seq_ends = jnp.cumsum(lengths_row)
    at = jnp.arange(row_count, dtype=jnp.int32)
    passed = seq_ends[None, :] <= at[:, None]
    begin = jnp.max(jnp.where(passed, seq_ends[None, :], 0), axis=1)
    finish = jnp.min(jnp.where(passed, row_count, seq_ends[None, :]), axis=1)
    return (at - begin, finish - 1 - at)


def adamw_step(weight, moment, second, grad, rate, decay, step_float):
    first_new = BETA_ONE * moment + (1.0 - BETA_ONE) * grad
    second_new = BETA_TWO * second + (1.0 - BETA_TWO) * grad * grad
    first_hat = first_new / (1.0 - jnp.power(BETA_ONE, step_float))
    second_hat = second_new / (1.0 - jnp.power(BETA_TWO, step_float))
    return (
        weight - rate * (first_hat / (jnp.sqrt(second_hat) + ADAM_EPS) + decay * weight),
        first_new,
        second_new,
    )


def sigmoid(v):
    return 1.0 / (1.0 + jnp.exp(-v))


def dot(a, b, dims):
    return lax.dot_general(
        a.astype(BF), b.astype(BF), (dims, ((), ())), preferred_element_type=F32
    )


def spread(columns, heads):
    return jnp.concatenate(
        [
            jnp.broadcast_to(columns[:, h : h + 1], (columns.shape[0], P_SIZE))
            for h in range(heads)
        ],
        axis=1,
    )


def head_sums(values, heads):
    lane = lax.broadcasted_iota(jnp.int32, (values.shape[0], 128), 1)
    total = jnp.zeros((values.shape[0], 128), F32)
    for h in range(heads):
        part = jnp.sum(values[:, h * P_SIZE : (h + 1) * P_SIZE], axis=1, keepdims=True)
        total = jnp.where(lane == h, part, total)
    return total


def convolve(buffer, weights, bias, place):
    total = bias + jnp.zeros((STRETCH, buffer.shape[1]), F32)
    for tap in range(KCONV):
        back = KCONV - 1 - tap
        rows = buffer[8 - back : 8 - back + STRETCH, :]
        if back:
            rows = jnp.where(place >= back, rows, 0.0)
        total = total + weights[tap : tap + 1, :] * rows
    return total


def block_terms(place, remain, dt_in, pdt):
    row = lax.broadcasted_iota(jnp.int32, (STRETCH, STRETCH), 0)
    col = lax.broadcasted_iota(jnp.int32, (STRETCH, STRETCH), 1)
    at = lax.broadcasted_iota(jnp.int32, (STRETCH, 1), 0)
    visible = (col <= row) & (col >= at - place)
    biased = dt_in + pdt[0:1, :]
    step = jnp.maximum(biased, 0.0) + jnp.log1p(jnp.exp(-jnp.abs(biased)))
    log_decay = step * pdt[1:2, :]
    lower = jnp.where(col <= row, 1.0, 0.0).astype(F32)
    cum = lax.dot_general(
        lower, log_decay, (((1,), (0,)), ((), ())), precision=PRECISE, preferred_element_type=F32
    )
    cum_t = jnp.transpose(cum)
    carrying = jnp.where(place >= at + 1, jnp.exp(cum), 0.0)
    tail_ok = remain >= STRETCH - 1 - at
    tail = jnp.exp(jnp.where(tail_ok, cum[STRETCH - 1 : STRETCH, :] - cum, LOW))
    return visible, biased, step, log_decay, cum, cum_t, carrying, tail


def forward_kernel(
    heads,
    gate_ref,
    x_ref,
    bc_ref,
    dt_ref,
    xprev_ref,
    bcprev_ref,
    place_ref,
    remain_ref,
    px_ref,
    pbc_ref,
    pdt_ref,
    state_in,
    *rest,
):
    zin_ref, mixed_ref, square_ref, states_ref, state, xbuf, bcbuf = rest[-7:]

    @pl.when(pl.program_id(0) == 0)
    def _():
        state[...] = state_in[...]

    xbuf[0:8, :] = xprev_ref[8:16, :].astype(F32)
    bcbuf[0:8, :] = bcprev_ref[8:16, :].astype(F32)
    place = place_ref[...]
    remain = remain_ref[...]
    xbuf[8 : 8 + STRETCH, :] = x_ref[...].astype(F32)
    bcbuf[8 : 8 + STRETCH, :] = bc_ref[...].astype(F32)
    conv_x = convolve(xbuf, px_ref[0:4, :], px_ref[4:5, :], place)
    conv_bc = convolve(bcbuf, pbc_ref[0:4, :], pbc_ref[4:5, :], place)
    x = conv_x * sigmoid(conv_x) * px_ref[7:8, :]
    act_bc = conv_bc * sigmoid(conv_bc)
    b_low = act_bc[:, :N].astype(BF)
    c_low = act_bc[:, N:].astype(BF)
    visible, _, step, _, cum, cum_t, carrying, tail = block_terms(
        place, remain, dt_ref[...].astype(F32), pdt_ref[...]
    )
    scaled = x * spread(step, heads)
    scaled_low = scaled.astype(BF)
    gram = dot(c_low, b_low, ((1,), (1,)))
    old = state[...]
    states_ref[0] = old
    across = dot(c_low, old, ((1,), (1,))) * spread(carrying, heads)
    parts = []
    for h in range(heads):
        decay = jnp.exp(jnp.where(visible, cum[:, h : h + 1] - cum_t[h : h + 1, :], LOW))
        parts.append(
            dot(gram * decay, scaled_low[:, h * P_SIZE : (h + 1) * P_SIZE], ((1,), (0,)))
        )
    mixed = jnp.concatenate(parts, axis=1) + across + px_ref[5:6, :] * x
    fresh = dot(scaled * spread(tail, heads), b_low, ((0,), (0,)))
    for h in range(heads):
        rows = slice(h * P_SIZE, (h + 1) * P_SIZE)
        state[rows, :] = (
            old[rows, :] * carrying[STRETCH - 1 : STRETCH, h : h + 1] + fresh[rows, :]
        )
    gate = gate_ref[...].astype(F32)
    gated = mixed * (gate * sigmoid(gate))
    mixed_ref[...] = mixed
    zin_ref[...] = (gated * px_ref[6:7, :]).astype(BF)
    square_ref[...] = jnp.sum(gated * gated, axis=1, keepdims=True)


def backward_kernel(
    heads,
    gate_ref,
    x_ref,
    bc_ref,
    dt_ref,
    xprev_ref,
    bcprev_ref,
    place_ref,
    remain_ref,
    mixed_ref,
    gout_ref,
    scale_ref,
    pull_ref,
    states_ref,
    px_ref,
    pbc_ref,
    pdt_ref,
    gstate_in,
    gx_in,
    gbc_in,
    gdt_in,
    *rest,
):
    gp_ref, low_ref, gstate, gx_ref, gbc_ref, gdt_ref, xbuf, bcbuf, gxbuf, gbcbuf = rest[-10:]
    width = x_ref.shape[1]

    @pl.when(pl.program_id(0) == 0)
    def _():
        gstate[...] = gstate_in[...]
        gxbuf[STRETCH : STRETCH + 8, :] = gx_in[8:16, :]
        gbcbuf[STRETCH : STRETCH + 8, :] = gbc_in[8:16, :]
        gx_ref[...] = gx_in[...]
        gbc_ref[...] = gbc_in[...]
        gdt_ref[...] = gdt_in[...]

    place = place_ref[...]
    remain = remain_ref[...]
    xbuf[0:8, :] = xprev_ref[8:16, :].astype(F32)
    bcbuf[0:8, :] = bcprev_ref[8:16, :].astype(F32)
    xbuf[8 : 8 + STRETCH, :] = x_ref[...].astype(F32)
    bcbuf[8 : 8 + STRETCH, :] = bc_ref[...].astype(F32)
    conv_x = convolve(xbuf, px_ref[0:4, :], px_ref[4:5, :], place)
    conv_bc = convolve(bcbuf, pbc_ref[0:4, :], pbc_ref[4:5, :], place)
    sig_x = sigmoid(conv_x)
    sig_bc = sigmoid(conv_bc)
    x = conv_x * sig_x * px_ref[7:8, :]
    act_bc = conv_bc * sig_bc
    b_low = act_bc[:, :N].astype(BF)
    c_low = act_bc[:, N:].astype(BF)
    visible, biased, step, log_decay, cum, cum_t, carrying, tail = block_terms(
        place, remain, dt_ref[...].astype(F32), pdt_ref[...]
    )

    gate = gate_ref[...].astype(F32)
    sig = sigmoid(gate)
    silu = gate * sig
    mixed = mixed_ref[...]
    gated = mixed * silu
    g_out = px_ref[6:7, :]
    scale = scale_ref[...]
    upstream = gout_ref[...]
    low_ref[...] = (gated * scale * g_out).astype(BF)
    g_gated = scale * g_out * upstream - gated * pull_ref[...]
    g_mixed = g_gated * silu
    gp_ref[:, 0:width] = (g_gated * mixed * (sig * (1.0 + gate * (1.0 - sig)))).astype(BF)

    step_wide = spread(step, heads)
    carry_wide = spread(carrying, heads)
    tail_wide = spread(tail, heads)
    scaled = x * step_wide
    scaled_low = scaled.astype(BF)
    g_low = g_mixed.astype(BF)
    old = states_ref[0]
    g_new = gstate[...]
    old_low = old.astype(BF)
    g_new_low = g_new.astype(BF)
    gram = dot(c_low, b_low, ((1,), (1,)))
    across = dot(c_low, old_low, ((1,), (1,)))
    returned = dot(b_low, g_new_low, ((1,), (1,))) * tail_wide
    g_carried = g_mixed * carry_wide
    g_carried_low = g_carried.astype(BF)
    tailed_low = (scaled * tail_wide).astype(BF)

    g_gram = jnp.zeros((STRETCH, STRETCH), F32)
    lane = lax.broadcasted_iota(jnp.int32, (STRETCH, 128), 1)
    row_sum = jnp.zeros((STRETCH, 128), F32)
    col_rows = []
    parts = []
    for h in range(heads):
        cols = slice(h * P_SIZE, (h + 1) * P_SIZE)
        decay = jnp.exp(jnp.where(visible, cum[:, h : h + 1] - cum_t[h : h + 1, :], LOW))
        mixing = gram * decay
        g_mixing = dot(g_low[:, cols], scaled_low[:, cols], ((1,), (1,)))
        parts.append(dot(mixing, g_low[:, cols], ((0,), (0,))))
        g_gram = g_gram + g_mixing * decay
        both = g_mixing * mixing
        row_sum = jnp.where(lane == h, jnp.sum(both, axis=1, keepdims=True), row_sum)
        col_rows.append(jnp.sum(both, axis=0, keepdims=True))
    col_rows.append(jnp.zeros((128 - heads, STRETCH), F32))
    col_sum = jnp.transpose(jnp.concatenate(col_rows, axis=0))
    g_scaled = jnp.concatenate(parts, axis=1) + returned
    into = head_sums(g_carried * across, heads)
    outof = head_sums(scaled * returned, heads)
    state_dot = jnp.zeros((1, 128), F32)
    lane_one = lax.broadcasted_iota(jnp.int32, (1, 128), 1)
    product = g_new * old
    for h in range(heads):
        total = jnp.sum(
            jnp.sum(product[h * P_SIZE : (h + 1) * P_SIZE, :], axis=0, keepdims=True),
            axis=1,
            keepdims=True,
        )
        state_dot = jnp.where(lane_one == h, total, state_dot)
    g_c = dot(g_gram, b_low, ((1,), (0,))) + dot(g_carried_low, old_low, ((1,), (0,)))
    g_b = dot(g_gram, c_low, ((0,), (0,))) + dot(tailed_low, g_new_low, ((1,), (0,)))
    g_fresh = dot(g_carried_low, c_low, ((0,), (0,)))
    for h in range(heads):
        rows = slice(h * P_SIZE, (h + 1) * P_SIZE)
        gstate[rows, :] = (
            g_new[rows, :] * carrying[STRETCH - 1 : STRETCH, h : h + 1] + g_fresh[rows, :]
        )
    row = lax.broadcasted_iota(jnp.int32, (STRETCH, STRETCH), 0)
    col = lax.broadcasted_iota(jnp.int32, (STRETCH, STRETCH), 1)
    upper = jnp.where(col >= row, 1.0, 0.0).astype(F32)
    g_cum = row_sum - col_sum + into - outof
    g_decay = lax.dot_general(
        upper, g_cum, (((1,), (0,)), ((), ())), precision=PRECISE, preferred_element_type=F32
    ) + (
        jnp.sum(outof, axis=0, keepdims=True)
        + carrying[STRETCH - 1 : STRETCH, :] * state_dot
    )
    g_step = head_sums(x * g_scaled, heads) + g_decay * pdt_ref[1:2, :]
    g_dt = g_step * sigmoid(biased)
    gdt_ref[0:1, :] += jnp.sum(g_dt, axis=0, keepdims=True)
    gdt_ref[1:2, :] += jnp.sum(g_decay * log_decay, axis=0, keepdims=True)
    g_x = px_ref[5:6, :] * g_mixed + step_wide * g_scaled
    g_conv_x = g_x * px_ref[7:8, :] * (sig_x * (1.0 + conv_x * (1.0 - sig_x)))
    g_act = jnp.concatenate([g_b, g_c], axis=1)
    g_conv_bc = g_act * (sig_bc * (1.0 + conv_bc * (1.0 - sig_bc)))
    gx_ref[4:5, :] += jnp.sum(g_conv_x, axis=0, keepdims=True)
    gx_ref[5:6, :] += jnp.sum(g_mixed * x, axis=0, keepdims=True)
    gx_ref[6:7, :] += jnp.sum(upstream * gated * scale, axis=0, keepdims=True)
    gbc_ref[4:5, :] += jnp.sum(g_conv_bc, axis=0, keepdims=True)
    gxbuf[0:STRETCH, :] = g_conv_x
    gbcbuf[0:STRETCH, :] = g_conv_bc
    g_in_x = jnp.zeros((STRETCH, width), F32)
    g_in_bc = jnp.zeros((STRETCH, 2 * N), F32)
    for tap in range(KCONV):
        back = KCONV - 1 - tap
        rows_x = xbuf[8 - back : 8 - back + STRETCH, :]
        rows_bc = bcbuf[8 - back : 8 - back + STRETCH, :]
        later_x = gxbuf[back : back + STRETCH, :]
        later_bc = gbcbuf[back : back + STRETCH, :]
        if back:
            rows_x = jnp.where(place >= back, rows_x, 0.0)
            rows_bc = jnp.where(place >= back, rows_bc, 0.0)
            later_x = jnp.where(remain >= back, later_x, 0.0)
            later_bc = jnp.where(remain >= back, later_bc, 0.0)
        gx_ref[tap : tap + 1, :] += jnp.sum(g_conv_x * rows_x, axis=0, keepdims=True)
        gbc_ref[tap : tap + 1, :] += jnp.sum(g_conv_bc * rows_bc, axis=0, keepdims=True)
        g_in_x = g_in_x + px_ref[tap : tap + 1, :] * later_x
        g_in_bc = g_in_bc + pbc_ref[tap : tap + 1, :] * later_bc
    gxbuf[STRETCH : STRETCH + 8, :] = g_conv_x[0:8, :]
    gbcbuf[STRETCH : STRETCH + 8, :] = g_conv_bc[0:8, :]
    gx_ref[8:16, :] = g_conv_x[0:8, :]
    gbc_ref[8:16, :] = g_conv_bc[0:8, :]
    gp_ref[:, width : 2 * width] = g_in_x.astype(BF)
    gp_ref[:, 2 * width : 2 * width + 2 * N] = g_in_bc.astype(BF)
    gp_ref[:, 2 * width + 2 * N : 2 * width + 2 * N + 128] = g_dt.astype(BF)


def run_forward(carried, first, count, projected, place, remain, px, pbc, pdt):
    total = projected.shape[0]
    width = px.shape[1]
    heads = width // P_SIZE
    row_spec = lambda w, c: pl.BlockSpec((STRETCH, w), lambda i: (first + i, c))
    prev_spec = lambda w, c: pl.BlockSpec(
        (16, w), lambda i: (jnp.maximum((first + i) * (STRETCH // 16) - 1, 0), c)
    )
    whole = lambda a: pl.BlockSpec(a.shape, lambda i: (0, 0))
    state = carried[0]
    filled = tuple(carried[1:])
    results = pl.pallas_call(
        partial(forward_kernel, heads),
        grid=(count,),
        in_specs=[
            row_spec(width, 0),
            row_spec(width, 1),
            row_spec(2 * N, width // N),
            row_spec(128, (2 * width + 2 * N) // 128),
            prev_spec(width, 1),
            prev_spec(2 * N, width // N),
            row_spec(1, 0),
            row_spec(1, 0),
            whole(px),
            whole(pbc),
            whole(pdt),
            whole(state),
        ]
        + [pl.BlockSpec(memory_space=pl.ANY)] * len(filled),
        out_specs=[
            row_spec(width, 0),
            row_spec(width, 0),
            row_spec(1, 0),
            pl.BlockSpec((1, width, N), lambda i: (first + i, 0, 0)),
            whole(state),
        ],
        out_shape=[
            jax.ShapeDtypeStruct((total, width), BF),
            jax.ShapeDtypeStruct((total, width), F32),
            jax.ShapeDtypeStruct((total, 1), F32),
            jax.ShapeDtypeStruct((total // STRETCH, width, N), F32),
            jax.ShapeDtypeStruct((width, N), F32),
        ],
        scratch_shapes=[
            pltpu.VMEM((STRETCH + 8, width), F32),
            pltpu.VMEM((STRETCH + 8, 2 * N), F32),
        ],
        input_output_aliases={12: 0, 13: 1, 14: 2, 15: 3} if filled else {},
        cost_estimate=pl.CostEstimate(
            flops=count * STRETCH * 256 * 20000,
            bytes_accessed=count * STRETCH * 5000,
            transcendentals=count * STRETCH * 1500,
        ),
        name="scan_forward",
    )(*((projected,) * 6 + (place, remain, px, pbc, pdt, state) + filled))
    return (results[4],) + tuple(results[:4])


def run_backward(carried, first, count, projected, rows_in, states, px, pbc, pdt):
    total = projected.shape[0]
    width = px.shape[1]
    heads = width // P_SIZE
    columns = projected.shape[1]
    rev = lambda i: first + count - 1 - i
    row_spec = lambda w, c: pl.BlockSpec((STRETCH, w), lambda i: (rev(i), c))
    prev_spec = lambda w, c: pl.BlockSpec(
        (16, w), lambda i: (jnp.maximum(rev(i) * (STRETCH // 16) - 1, 0), c)
    )
    whole = lambda a: pl.BlockSpec(a.shape, lambda i: (0, 0))
    fixed = lambda r, w: pl.BlockSpec((r, w), lambda i: (0, 0))
    place, remain, mixed, g_out_low, scale, pull = rows_in
    gstate, gx, gbc, gdt = carried[:4]
    filled = tuple(carried[4:])
    operands = (
        (projected,) * 6
        + (place, remain, mixed, g_out_low, scale, pull, states, px, pbc, pdt)
        + (gstate, gx, gbc, gdt)
        + filled
    )
    results = pl.pallas_call(
        partial(backward_kernel, heads),
        grid=(count,),
        in_specs=[
            row_spec(width, 0),
            row_spec(width, 1),
            row_spec(2 * N, width // N),
            row_spec(128, (2 * width + 2 * N) // 128),
            prev_spec(width, 1),
            prev_spec(2 * N, width // N),
            row_spec(1, 0),
            row_spec(1, 0),
            row_spec(width, 0),
            row_spec(width, 0),
            row_spec(1, 0),
            row_spec(1, 0),
            pl.BlockSpec((1, width, N), lambda i: (rev(i), 0, 0)),
            whole(px),
            whole(pbc),
            whole(pdt),
            whole(gstate),
            whole(gx),
            whole(gbc),
            whole(gdt),
        ]
        + [pl.BlockSpec(memory_space=pl.ANY)] * len(filled),
        out_specs=[
            row_spec(columns, 0),
            row_spec(width, 0),
            fixed(width, N),
            fixed(16, width),
            fixed(16, 2 * N),
            fixed(8, 128),
        ],
        out_shape=[
            jax.ShapeDtypeStruct((total, columns), BF),
            jax.ShapeDtypeStruct((total, width), BF),
            jax.ShapeDtypeStruct((width, N), F32),
            jax.ShapeDtypeStruct((16, width), F32),
            jax.ShapeDtypeStruct((16, 2 * N), F32),
            jax.ShapeDtypeStruct((8, 128), F32),
        ],
        scratch_shapes=[
            pltpu.VMEM((STRETCH + 8, width), F32),
            pltpu.VMEM((STRETCH + 8, 2 * N), F32),
            pltpu.VMEM((STRETCH + 8, width), F32),
            pltpu.VMEM((STRETCH + 8, 2 * N), F32),
        ],
        input_output_aliases={20: 0, 21: 1} if filled else {},
        cost_estimate=pl.CostEstimate(
            flops=count * STRETCH * 256 * 40000,
            bytes_accessed=count * STRETCH * 8000,
            transcendentals=count * STRETCH * 2000,
        ),
        name="scan_backward",
    )(*operands)
    return tuple(results[2:]) + tuple(results[:2])


def after(value, *others):
    return lax.optimization_barrier((value, others))[0]


def by_row(values):
    return with_layout_constraint(values, Layout(major_to_minor=(0, 1)))


def cuts(count, parts):
    edges = [count * i // parts for i in range(parts + 1)]
    return list(zip(edges[:-1], edges[1:]))


def ring_chips():
    return [(z * 2 + x) for x, z in [(0, 0), (0, 1), (0, 2), (0, 3), (1, 3), (1, 2), (1, 1), (1, 0)]]


def hop(values, steps):
    chips = ring_chips()
    count = len(chips)
    pairs = [
        (2 * chips[p] + core, 2 * chips[(p + steps) % count] + core)
        for p in range(count)
        for core in (0, 1)
    ]
    return lax.ppermute(values, "dp", pairs)


def swap(values):
    return lax.ppermute(values, "dp", [(i, i ^ 1) for i in range(lax.axis_size("dp"))])


def ring_place():
    here = lax.axis_index("dp")
    core = here % 2
    chip = here // 2
    spot = jnp.where(chip % 2 == 0, chip // 2, 7 - chip // 2)
    return core, spot


def ring_chip(spot):
    spot = spot % 8
    return jnp.where(spot < 4, spot * 2, (7 - spot) * 2 + 1)


class RingSum:
    def __init__(self, chunk, rows):
        self.chunk = chunk
        self.mid = rows // 2
        self.step = 4
        self.last = self.sent = ()
        self.ready = (chunk(4, ()),)

    def settle(self, others):
        self.last, self.ready, _ = lax.optimization_barrier((self.last, self.ready, others))

    def advance(self, *others):
        self.settle(others)
        mid = self.mid
        if self.step == 4:
            up, down = self.ready[0][:mid], self.ready[0][mid:]
        else:
            up, down = (value.astype(F32) for value in self.last)
            first, second = self.ready
            if self.step == 3:
                up = jnp.concatenate([first[:mid] + up, first[mid:]], axis=0)
                down = jnp.concatenate([second[:mid], second[mid:] + down], axis=0)
            else:
                up, down = first + up, second + down
        self.sent = lax.optimization_barrier((up.astype(BF), down.astype(BF)))
        up, down = self.sent
        self.last = (by_row(hop(by_row(up), 1)), by_row(hop(by_row(down), -1)))
        self.step -= 1
        self.ready = tuple(
            self.chunk(steps, self.sent)
            for steps in sorted({self.step, -self.step}, reverse=True)
        )

    def finish(self, others):
        self.settle(others)
        return self.ready[0] + self.last[0].astype(F32) + self.last[1].astype(F32)


class Scatter:
    def __init__(self, left, right, *gate):
        self.ring = lax.axis_size("dp") == 16
        self.last = self.sent = ()
        if not self.ring:
            full = jnp.dot(left, right, preferred_element_type=F32).astype(BF)
            self.done = lax.psum_scatter(full, "dp", scatter_dimension=0, tiled=True).astype(F32)
            return
        self.core, spot = ring_place()
        half = right.shape[1] // 2
        take = lambda c: lax.dynamic_slice_in_dim(right, c * half, half, 1)
        sides = ((left, take(self.core)), (swap(left), swap(take(1 - self.core))))
        sides = lax.optimization_barrier((sides, gate))[0]
        self.rows = rows = left.shape[0] // 8

        def chunk(steps, deps):
            start = ring_chip(spot + steps) * rows
            return by_row(
                sum(
                    jnp.dot(
                        lax.dynamic_slice_in_dim(after(side, deps), start, rows, 0),
                        weight,
                        preferred_element_type=F32,
                    )
                    for side, weight in sides
                )
            )

        self.sum = RingSum(chunk, rows)

    def advance(self, *others):
        if self.ring:
            self.sum.advance(*others)
            self.last, self.sent = self.sum.last, self.sum.sent

    def ready(self):
        return self.sum.ready if self.ring else ()

    def finish(self, *others):
        if not self.ring:
            return self.done
        done = self.sum.finish(others)
        own = self.rows // 2
        kept = lax.dynamic_slice_in_dim(done, self.core * own, own, 0)
        got = swap(lax.dynamic_slice_in_dim(done, (1 - self.core) * own, own, 0))
        first = self.core == 0
        return jnp.concatenate(
            [jnp.where(first, kept, got), jnp.where(first, got, kept)], axis=1
        )


def other_width(values):
    return lax.ppermute(values, "width", [(0, 1), (1, 0)])


def in_order(mine, other):
    first = lax.axis_index("width") == 0
    return jnp.where(first, mine, other), jnp.where(first, other, mine)


def same_core():
    return [[2 * chip + core for chip in range(8)] for core in (0, 1)]


def gather_blocks(block):
    if lax.axis_size("dp") != 16:
        return lax.all_gather(block, "dp")
    copies = jnp.broadcast_to(block[None], (8,) + block.shape)
    mine = lax.all_to_all(copies, "dp", 0, 0, axis_index_groups=same_core())
    theirs = swap(mine)
    first = lax.axis_index("dp") % 2 == 0
    pair = jnp.stack([jnp.where(first, mine, theirs), jnp.where(first, theirs, mine)], axis=1)
    return pair.reshape((16,) + block.shape)


def adamw_kernel(count, base_ref, weight_ref, moment_ref, second_ref, *refs):
    new_ref, first_ref, squares_ref, low_ref = refs[-4:]
    shape = weight_ref.shape
    grad = sum(ref[...].astype(F32).reshape(shape) for ref in refs[:count])
    base = base_ref[0, 0]
    weight = weight_ref[...]
    first = BETA_ONE * moment_ref[...] + (1.0 - BETA_ONE) * grad
    squares = BETA_TWO * second_ref[...] + (1.0 - BETA_TWO) * grad * grad
    new = weight - MATRIX_RATE * (
        (first / base) / (jnp.sqrt(squares / base) + ADAM_EPS) + MATRIX_DECAY * weight
    )
    new_ref[...] = new
    first_ref[...] = first
    squares_ref[...] = squares
    low_ref[...] = new.astype(BF)


def adamw_rows(base, weight, moment, second, grads, first, size, count, grad_spec, filled):
    columns = weight.shape[1]
    spec = pl.BlockSpec((size, columns), lambda i: (first // size + i, 0))
    used = 4 + len(grads)
    return pl.pallas_call(
        partial(adamw_kernel, len(grads)),
        grid=(count,),
        in_specs=[pl.BlockSpec(memory_space=pltpu.SMEM), spec, spec, spec]
        + [grad_spec] * len(grads)
        + [pl.BlockSpec(memory_space=pl.ANY)] * len(filled),
        out_specs=[spec] * 4,
        out_shape=[jax.ShapeDtypeStruct(weight.shape, F32)] * 3
        + [jax.ShapeDtypeStruct(weight.shape, BF)],
        input_output_aliases={used + i: i for i in range(len(filled))},
        cost_estimate=pl.CostEstimate(
            flops=count * columns * size * 10000,
            bytes_accessed=count * columns * size * 30,
            transcendentals=count * columns * size,
        ),
        name="adamw",
    )(base, weight, moment, second, *grads, *filled)


def tree_sum(values):
    if lax.axis_size("dp") != 16 or lax.axis_size("width") != 2:
        return lax.psum(values, ("width", "dp"))
    for bit in (1, 2, 4, 8):
        values = values + lax.ppermute(values, "dp", [(i, i ^ bit) for i in range(16)])
    return values + lax.ppermute(values, "width", [(0, 1), (1, 0)])


def pad_to(values, width, axis):
    missing = width - values.shape[axis]
    if missing == 0:
        return values
    pads = [(0, 0)] * values.ndim
    pads[axis] = (0, missing)
    return jnp.pad(values, pads)


def width_sum(values):
    if lax.axis_size("width") == 2:
        return values.astype(F32) + lax.ppermute(values, "width", [(0, 1), (1, 0)]).astype(F32)
    return jnp.sum(lax.all_gather(values, "width").astype(F32), axis=0)


def per_device(
    tokens,
    cotangent,
    lengths,
    levels,
    step_count,
    weight_in,
    moment_in,
    second_in,
    weight_out,
    moment_out,
    second_out,
    small_params,
    moment_small,
    second_small,
):
    dp = lax.axis_size("dp")
    here = lax.axis_index("dp")
    rows = tokens.shape[0]
    total = rows * dp
    units = E // dp
    own_heads = H // dp
    wide = max(units, 128)
    shard = weight_in.shape[0]

    inputs_f = tokens.astype(F32)
    root = lax.rsqrt(jnp.mean(inputs_f * inputs_f, axis=1, keepdims=True) + NORM_EPS)
    g_in, g_out, conv_w, conv_b, a_log, dt_bias, d_skip = unpack(small_params)
    normed_low = (inputs_f * root * g_in).astype(BF)
    weight_low = weight_in.T.astype(BF)
    normed_all = lax.all_gather(normed_low, "dp", axis=0, tiled=True)
    pairs = jnp.concatenate(
        [weight_low[:E].reshape(dp, units, shard), weight_low[E : 2 * E].reshape(dp, units, shard)],
        axis=1,
    )
    own_cols = lax.all_to_all(pairs, "dp", 0, 0).transpose(1, 0, 2).reshape(2 * units, D).T
    shared = gather_blocks(weight_low[2 * E :]).transpose(1, 0, 2).reshape(SHARED, D).T
    own_dt = lax.dynamic_slice_in_dim(shared, 2 * N + here * own_heads, own_heads, 1)
    weight_own = jnp.concatenate(
        [
            pad_to(own_cols[:, :units], wide, 1),
            pad_to(own_cols[:, units:], wide, 1),
            shared[:, : 2 * N],
            pad_to(own_dt, 128, 1),
        ],
        axis=1,
    )
    out_weight_low = by_row(pad_to(weight_out.astype(BF), wide, 0))

    live_units = jnp.right_shift(jnp.int32(E), lax.axis_size("width") - 1 - levels[0])
    live = live_units.astype(F32)
    place, remain = row_places(lengths[0], total)
    place = place[:, None]
    remain = remain[:, None]
    own = lambda v: lax.dynamic_slice_in_dim(v, here * units, units, v.ndim - 1)
    own_h = lambda v: lax.dynamic_slice_in_dim(v, here * own_heads, own_heads, 0)
    unit_mask = (here * units + jnp.arange(units, dtype=jnp.int32) < live_units).astype(F32)
    px = pad_to(
        jnp.concatenate(
            [
                own(conv_w[:, :E]),
                own(conv_b[:E])[None],
                jnp.repeat(own_h(d_skip), P_SIZE)[None],
                own(g_out)[None],
                unit_mask[None],
            ],
            axis=0,
        ),
        wide,
        1,
    )
    pbc = pad_to(jnp.concatenate([conv_w[:, E:], conv_b[None, E:]], axis=0), 8, 0)
    pdt = pad_to(
        pad_to(jnp.stack([own_h(dt_bias), -jnp.exp(own_h(a_log))]), 128, 1), 8, 0
    )

    cotangent_all = lax.all_gather(
        after(cotangent, normed_all, weight_own), "dp", axis=0, tiled=True
    )
    projected = jnp.dot(normed_all, weight_own, preferred_element_type=F32).astype(BF)
    carried = (jnp.zeros((wide, N), F32),)
    for begin, end in cuts(total // STRETCH, FRONT_PARTS):
        carried = run_forward(
            carried, begin, end - begin, projected, place, remain, px, pbc, pdt
        )
    _, zin, mixed, square, states = carried
    partial_out = jnp.dot(zin, out_weight_low, preferred_element_type=F32).astype(BF)
    summed_out = lax.psum_scatter(partial_out, "dp", scatter_dimension=0, tiled=True)
    g_out_low = lax.dot_general(
        cotangent_all, out_weight_low, (((1,), (1,)), ((), ())), preferred_element_type=F32
    )
    pull_part = jnp.sum(g_out_low * zin.astype(F32), axis=1)
    both = jnp.sum(lax.all_gather(jnp.stack([square[:, 0], pull_part]), "dp"), axis=0)
    scale = lax.rsqrt(both[0] / live + NORM_EPS)
    pull = scale * scale * scale / live * both[1]

    rows_in = (place, remain, mixed, g_out_low, scale[:, None], pull[:, None])
    carried = (
        jnp.zeros((wide, N), F32),
        jnp.zeros((16, wide), F32),
        jnp.zeros((16, 2 * N), F32),
        jnp.zeros((8, 128), F32),
    )
    for begin, end in reversed(cuts(total // STRETCH, BACK_PARTS)):
        carried = run_backward(
            carried, begin, end - begin, projected, rows_in, states, px, pbc, pdt
        )
    _, gx, gbc, gdt, g_projected, out_low = carried
    block_out = (
        inputs_f
        + summed_out.astype(F32)
        * lax.dynamic_slice_in_dim(scale, here * rows, rows, 0)[:, None]
    ).astype(BF)

    g_weight = lax.dot_general(
        g_projected, normed_all, (((0,), (0,)), ((), ())), preferred_element_type=F32
    ).astype(BF)
    g_heads = g_weight[2 * wide + 2 * N : 2 * wide + 2 * N + own_heads]
    g_shared = jnp.concatenate(
        [
            g_weight[2 * wide : 2 * wide + 2 * N],
            lax.dynamic_update_slice_in_dim(
                jnp.zeros((H, D), BF), g_heads, here * own_heads, 0
            ),
        ],
        axis=0,
    )
    g_both = jnp.stack([g_weight[:units], g_weight[wide : wide + units]])
    paired = lax.axis_size("width") == 2

    def to_owners(values):
        return lax.all_to_all(
            values.reshape(-1, dp, shard).transpose(1, 0, 2), "dp", 0, 0
        )

    def half(slot):
        return jnp.concatenate(
            [
                lax.dynamic_index_in_dim(g_both, slot, 0, False),
                lax.dynamic_slice_in_dim(g_shared, slot * (SHARED // 2), SHARED // 2, 0),
            ],
            axis=0,
        )

    inward = Scatter(g_projected, weight_own.T, g_weight)
    if paired:
        slot = lax.axis_index("width")
        g_kept = half(slot)
        g_got = other_width(half(1 - slot))
    inward.advance()
    g_weight_out = lax.dot_general(
        after(out_low, inward.sent),
        cotangent_all,
        (((0,), (0,)), ((), ())),
        preferred_element_type=F32,
    )[:units].astype(BF)
    inward.advance(g_weight_out)
    if paired:
        g_kept, g_got, _ = lax.optimization_barrier((g_kept, g_got, inward.sent))
        g_half = to_owners((g_kept.astype(F32) + g_got.astype(F32)).astype(BF))
        total_out = other_width(after(g_weight_out, inward.sent))
        inward.advance()
        inward.advance(total_out)
        total_out = g_weight_out.astype(F32) + total_out.astype(F32)
        g_half = after(g_half, inward.sent)
        g_shared = jnp.sum(g_half[:, units:].astype(F32), axis=0).astype(BF)
        g_half = g_half[:, :units]
        g_peer = other_width(g_half)
        g_apart = other_width(g_shared)
    else:
        inward.advance()
        inward.advance()
        total_out = width_sum(g_weight_out)
        g_pairs = width_sum(to_owners(g_both.reshape(-1, D)))
        g_gate, g_x = g_pairs[:, :units], g_pairs[:, units:]
        g_apart = lax.psum_scatter(
            g_shared.reshape(SHARED, dp, shard).transpose(1, 0, 2), "dp", scatter_dimension=0
        )
        g_apart = width_sum(g_apart)
    simple = paired and units % 128 == 0 and shard == 128
    step_float = step_count[0].astype(F32)
    new_out, mom_out, sec_out = adamw_step(
        weight_out,
        moment_out,
        second_out,
        after(total_out, inward.sent),
        MATRIX_RATE,
        MATRIX_DECAY,
        step_float,
    )
    if paired:
        g_normed = inward.finish(new_out, g_peer, g_apart)
        g_gate, g_x = in_order(g_half, g_peer)
        g_pairs = jnp.concatenate([g_gate, g_x], axis=0)
        g_apart = jnp.concatenate(in_order(g_shared, g_apart), axis=0)
    else:
        g_normed = inward.finish(new_out)
    if simple:
        base = (1.0 - jnp.power(BETA_ONE, step_float)).reshape(1, 1)
        own = (weight_in.T, moment_in.T, second_in.T)
        moved = adamw_rows(
            base,
            *own,
            (g_pairs,),
            0,
            4 * units,
            dp // 2,
            pl.BlockSpec((4, units, shard), lambda i: (i, 0, 0)),
            (),
        )
        results = adamw_rows(
            base,
            *own,
            (g_apart,),
            2 * E,
            H,
            SHARED // H,
            pl.BlockSpec((H, shard), lambda i: (i, 0)),
            tuple(moved),
        )
        new_in, mom_in, sec_in, low_in = (result.T for result in results)
    else:
        total_in = jnp.concatenate(
            [
                g_gate.transpose(2, 0, 1).reshape(shard, E),
                g_x.transpose(2, 0, 1).reshape(shard, E),
                g_apart.T,
            ],
            axis=1,
        ).astype(F32)
        new_in, mom_in, sec_in = adamw_step(
            weight_in, moment_in, second_in, total_in, MATRIX_RATE, MATRIX_DECAY, step_float
        )
        low_in = new_in.astype(BF)

    ratio = root * g_in
    lean = jnp.sum(g_in * g_normed * inputs_f, axis=1, keepdims=True)
    g_inputs = ratio * g_normed - inputs_f * (root * root * root / D * lean)
    grad_tokens = (cotangent.astype(F32) + g_inputs).astype(BF)
    g_g_in = jnp.sum(g_normed * inputs_f * root, axis=0)

    def placed(part, size):
        spots = jnp.zeros(part.shape[:-1] + (size,), F32)
        return lax.dynamic_update_slice_in_dim(
            spots, part, here * part.shape[-1], part.ndim - 1
        )

    conv_part = jnp.concatenate([placed(gx[:5, :units], E), gbc[:5]], axis=1)
    early = jnp.concatenate(
        [
            placed(gx[6, :units], E),
            conv_part.reshape(-1),
            placed(gdt[1, :own_heads], H),
            placed(gdt[0, :own_heads], H),
            placed(jnp.sum(gx[5, :units].reshape(own_heads, P_SIZE), axis=1), H),
        ]
    )
    total_small = tree_sum(jnp.concatenate([g_g_in, early]))
    rate_table, decay_table = small_table()
    new_small, mom_small, sec_small = adamw_step(
        small_params, moment_small, second_small, total_small, rate_table, decay_table, step_float
    )
    return (
        block_out,
        grad_tokens,
        new_in,
        mom_in,
        sec_in,
        low_in,
        new_out,
        mom_out,
        sec_out,
        new_out.astype(BF),
        new_small,
        mom_small,
        sec_small,
    )


def solution(mesh):
    return jax.shard_map(
        per_device,
        mesh=mesh,
        in_specs=(
            P(("width", "dp"), None),
            P(("width", "dp"), None),
            P("width", None),
            P("width"),
            P(),
            P("dp", None),
            P("dp", None),
            P("dp", None),
            P("dp", None),
            P("dp", None),
            P("dp", None),
            P(),
            P(),
            P(),
        ),
        out_specs=(
            P(("width", "dp"), None),
            P(("width", "dp"), None),
            P("dp", None),
            P("dp", None),
            P("dp", None),
            P("dp", None),
            P("dp", None),
            P("dp", None),
            P("dp", None),
            P("dp", None),
            P(),
            P(),
            P(),
        ),
        check_vma=False,
    )
```

```python
from functools import partial

import jax
import jax.numpy as jnp
from jax import lax
from jax.experimental import pallas as pl
from jax.experimental.layout import Layout, with_layout_constraint
from jax.experimental.pallas import tpu as pltpu
from jax.sharding import PartitionSpec as P

D = 2048
E = 4096
H = 64
P_SIZE = 64
N = 128
KCONV = 4
STRETCH = 256
K = 4352

NORM_EPS = 1e-05
ADAM_EPS = 1e-08
BETA_ONE = 0.5
BETA_TWO = 0.5
MATRIX_RATE = 0.02
MATRIX_DECAY = 0.1
PRECISE = lax.Precision.HIGHEST
BF = jnp.bfloat16
F32 = jnp.float32
LOW = -1e30
SHARED = 2 * N + H
BACK_PARTS = 1
FRONT_PARTS = 1


def small_table():
    rate_table = jnp.concatenate(
        [
            jnp.full((D,), 0.3, F32),
            jnp.full((E,), 0.3, F32),
            jnp.full((KCONV * K,), 0.2, F32),
            jnp.full((K,), 0.2, F32),
            jnp.full((H,), 0.3, F32),
            jnp.full((H,), 1.0, F32),
            jnp.full((H,), 0.3, F32),
        ]
    )
    decay_table = jnp.concatenate(
        [
            jnp.zeros((D + E,), F32),
            jnp.full((KCONV * K,), 0.1, F32),
            jnp.zeros((K + 3 * H,), F32),
        ]
    )
    return (rate_table, decay_table)


def unpack(small_params):
    offset = D + E
    conv_w = small_params[offset : offset + KCONV * K].reshape(KCONV, K)
    offset = offset + KCONV * K
    conv_b = small_params[offset : offset + K]
    offset = offset + K
    a_log = small_params[offset : offset + H]
    dt_bias = small_params[offset + H : offset + 2 * H]
    d_skip = small_params[offset + 2 * H : offset + 3 * H]
    return (small_params[:D], small_params[D : D + E], conv_w, conv_b, a_log, dt_bias, d_skip)


def row_places(lengths_row, row_count):
    seq_ends = jnp.cumsum(lengths_row)
    at = jnp.arange(row_count, dtype=jnp.int32)
    passed = seq_ends[None, :] <= at[:, None]
    begin = jnp.max(jnp.where(passed, seq_ends[None, :], 0), axis=1)
    finish = jnp.min(jnp.where(passed, row_count, seq_ends[None, :]), axis=1)
    return (at - begin, finish - 1 - at)


def adamw_step(weight, moment, second, grad, rate, decay, step_float):
    first_new = BETA_ONE * moment + (1.0 - BETA_ONE) * grad
    second_new = BETA_TWO * second + (1.0 - BETA_TWO) * grad * grad
    first_hat = first_new / (1.0 - jnp.power(BETA_ONE, step_float))
    second_hat = second_new / (1.0 - jnp.power(BETA_TWO, step_float))
    return (
        weight - rate * (first_hat / (jnp.sqrt(second_hat) + ADAM_EPS) + decay * weight),
        first_new,
        second_new,
    )


def sigmoid(v):
    return 1.0 / (1.0 + jnp.exp(-v))


def dot(a, b, dims):
    return lax.dot_general(
        a.astype(BF), b.astype(BF), (dims, ((), ())), preferred_element_type=F32
    )


def split(values, count):
    parts = []
    for _ in range(count):
        part = values.astype(BF)
        values = values - part.astype(F32)
        parts.append(part)
    return parts


def head_lanes(heads):
    row = lax.broadcasted_iota(jnp.int32, (128, heads * P_SIZE), 0)
    lane = lax.broadcasted_iota(jnp.int32, (128, heads * P_SIZE), 1)
    return jnp.where(lane // P_SIZE == row, 1.0, 0.0).astype(BF)


def spread(columns, lanes):
    return sum(dot(part, lanes, ((1,), (0,))) for part in split(columns, 2))


def head_sums(values, lanes):
    return sum(dot(part, lanes, ((1,), (1,))) for part in split(values, 2))


def running(mask, values):
    mask = jnp.where(mask, 1.0, 0.0).astype(BF)
    return sum(dot(mask, part, ((1,), (0,))) for part in split(values, 3))


def convolve(buffer, weights, bias, place):
    total = bias + jnp.zeros((STRETCH, buffer.shape[1]), F32)
    for tap in range(KCONV):
        back = KCONV - 1 - tap
        rows = buffer[8 - back : 8 - back + STRETCH, :]
        if back:
            rows = jnp.where(place >= back, rows, 0.0)
        total = total + weights[tap : tap + 1, :] * rows
    return total


def block_terms(place, remain, dt_in, pdt):
    row = lax.broadcasted_iota(jnp.int32, (STRETCH, STRETCH), 0)
    col = lax.broadcasted_iota(jnp.int32, (STRETCH, STRETCH), 1)
    at = lax.broadcasted_iota(jnp.int32, (STRETCH, 1), 0)
    biased = dt_in + pdt[0:1, :]
    step = jnp.maximum(biased, 0.0) + jnp.log1p(jnp.exp(-jnp.abs(biased)))
    log_decay = step * pdt[1:2, :]
    cum = running(col <= row, log_decay)
    cum_t = jnp.transpose(cum)
    carrying = jnp.where(place >= at + 1, jnp.exp(cum), 0.0)
    tail_ok = remain >= STRETCH - 1 - at
    tail = jnp.exp(jnp.where(tail_ok, cum[STRETCH - 1 : STRETCH, :] - cum, LOW))
    return row, col, biased, step, log_decay, cum, cum_t, carrying, tail


def forward_kernel(
    heads,
    gate_ref,
    x_ref,
    bc_ref,
    dt_ref,
    xprev_ref,
    bcprev_ref,
    place_ref,
    remain_ref,
    px_ref,
    pbc_ref,
    pdt_ref,
    state_in,
    *rest,
):
    zin_ref, mixed_ref, square_ref, states_ref, state, xbuf, bcbuf = rest[-7:]

    @pl.when(pl.program_id(0) == 0)
    def _():
        state[...] = state_in[...]

    xbuf[0:8, :] = xprev_ref[8:16, :].astype(F32)
    bcbuf[0:8, :] = bcprev_ref[8:16, :].astype(F32)
    place = place_ref[...]
    remain = remain_ref[...]
    xbuf[8 : 8 + STRETCH, :] = x_ref[...].astype(F32)
    bcbuf[8 : 8 + STRETCH, :] = bc_ref[...].astype(F32)
    conv_x = convolve(xbuf, px_ref[0:4, :], px_ref[4:5, :], place)
    conv_bc = convolve(bcbuf, pbc_ref[0:4, :], pbc_ref[4:5, :], place)
    x = conv_x * sigmoid(conv_x) * px_ref[7:8, :]
    act_bc = conv_bc * sigmoid(conv_bc)
    b_low = act_bc[:, :N].astype(BF)
    c_low = act_bc[:, N:].astype(BF)
    row, col, _, step, _, cum, cum_t, carrying, tail = block_terms(
        place, remain, dt_ref[...].astype(F32), pdt_ref[...]
    )
    visible = (col <= row) & (row - col <= place)
    lanes = head_lanes(heads)
    scaled = x * spread(step, lanes)
    scaled_low = scaled.astype(BF)
    gram = dot(c_low, b_low, ((1,), (1,)))
    old = state[...]
    states_ref[0] = old
    across = dot(c_low, old, ((1,), (1,))) * spread(carrying, lanes)
    parts = []
    for h in range(heads):
        decay = jnp.exp(jnp.where(visible, cum[:, h : h + 1] - cum_t[h : h + 1, :], LOW))
        parts.append(
            dot(gram * decay, scaled_low[:, h * P_SIZE : (h + 1) * P_SIZE], ((1,), (0,)))
        )
    mixed = jnp.concatenate(parts, axis=1) + across + px_ref[5:6, :] * x
    fresh = dot(scaled * spread(tail, lanes), b_low, ((0,), (0,)))
    for h in range(heads):
        rows = slice(h * P_SIZE, (h + 1) * P_SIZE)
        state[rows, :] = (
            old[rows, :] * carrying[STRETCH - 1 : STRETCH, h : h + 1] + fresh[rows, :]
        )
    gate = gate_ref[...].astype(F32)
    gated = mixed * (gate * sigmoid(gate))
    mixed_ref[...] = mixed
    zin_ref[...] = (gated * px_ref[6:7, :]).astype(BF)
    square_ref[...] = jnp.sum(gated * gated, axis=1, keepdims=True)


def backward_kernel(
    heads,
    gate_ref,
    x_ref,
    bc_ref,
    dt_ref,
    xprev_ref,
    bcprev_ref,
    place_ref,
    remain_ref,
    mixed_ref,
    gout_ref,
    scale_ref,
    pull_ref,
    states_ref,
    px_ref,
    pbc_ref,
    pdt_ref,
    gstate_in,
    gx_in,
    gbc_in,
    gdt_in,
    *rest,
):
    gp_ref, low_ref, gstate, gx_ref, gbc_ref, gdt_ref, xbuf, bcbuf, gxbuf, gbcbuf = rest[-10:]
    width = x_ref.shape[1]

    @pl.when(pl.program_id(0) == 0)
    def _():
        gstate[...] = gstate_in[...]
        gxbuf[STRETCH : STRETCH + 8, :] = gx_in[8:16, :]
        gbcbuf[STRETCH : STRETCH + 8, :] = gbc_in[8:16, :]
        gx_ref[...] = gx_in[...]
        gbc_ref[...] = gbc_in[...]
        gdt_ref[...] = gdt_in[...]

    place = place_ref[...]
    remain = remain_ref[...]
    xbuf[0:8, :] = xprev_ref[8:16, :].astype(F32)
    bcbuf[0:8, :] = bcprev_ref[8:16, :].astype(F32)
    xbuf[8 : 8 + STRETCH, :] = x_ref[...].astype(F32)
    bcbuf[8 : 8 + STRETCH, :] = bc_ref[...].astype(F32)
    conv_x = convolve(xbuf, px_ref[0:4, :], px_ref[4:5, :], place)
    conv_bc = convolve(bcbuf, pbc_ref[0:4, :], pbc_ref[4:5, :], place)
    sig_x = sigmoid(conv_x)
    sig_bc = sigmoid(conv_bc)
    x = conv_x * sig_x * px_ref[7:8, :]
    act_bc = conv_bc * sig_bc
    b_low = act_bc[:, :N].astype(BF)
    c_low = act_bc[:, N:].astype(BF)
    row, col, biased, step, log_decay, cum, cum_t, carrying, tail = block_terms(
        place, remain, dt_ref[...].astype(F32), pdt_ref[...]
    )
    visible = (col >= row) & (col - row <= remain)
    lanes = head_lanes(heads)

    gate = gate_ref[...].astype(F32)
    sig = sigmoid(gate)
    silu = gate * sig
    mixed = mixed_ref[...]
    gated = mixed * silu
    g_out = px_ref[6:7, :]
    scale = scale_ref[...]
    upstream = gout_ref[...]
    low_ref[...] = (gated * scale * g_out).astype(BF)
    g_gated = scale * g_out * upstream - gated * pull_ref[...]
    g_mixed = g_gated * silu
    gp_ref[:, 0:width] = (g_gated * mixed * (sig * (1.0 + gate * (1.0 - sig)))).astype(BF)

    step_wide = spread(step, lanes)
    carry_wide = spread(carrying, lanes)
    tail_wide = spread(tail, lanes)
    scaled = x * step_wide
    scaled_low = scaled.astype(BF)
    g_low = g_mixed.astype(BF)
    old = states_ref[0]
    g_new = gstate[...]
    old_low = old.astype(BF)
    g_new_low = g_new.astype(BF)
    gram = dot(b_low, c_low, ((1,), (1,)))
    across = dot(c_low, old_low, ((1,), (1,)))
    returned = dot(b_low, g_new_low, ((1,), (1,))) * tail_wide
    g_carried = g_mixed * carry_wide
    g_carried_low = g_carried.astype(BF)
    tailed_low = (scaled * tail_wide).astype(BF)

    g_gram = jnp.zeros((STRETCH, STRETCH), F32)
    lane = lax.broadcasted_iota(jnp.int32, (STRETCH, 128), 1)
    sources = jnp.zeros((STRETCH, 128), F32)
    target_rows = []
    parts = []
    for h in range(heads):
        cols = slice(h * P_SIZE, (h + 1) * P_SIZE)
        decay = jnp.exp(jnp.where(visible, cum_t[h : h + 1, :] - cum[:, h : h + 1], LOW))
        mixing = gram * decay
        g_mixing = dot(scaled_low[:, cols], g_low[:, cols], ((1,), (1,)))
        parts.append(dot(mixing, g_low[:, cols], ((1,), (0,))))
        g_gram = g_gram + g_mixing * decay
        both = g_mixing * mixing
        sources = jnp.where(lane == h, jnp.sum(both, axis=1, keepdims=True), sources)
        target_rows.append(jnp.sum(both, axis=0, keepdims=True))
    target_rows.append(jnp.zeros((128 - heads, STRETCH), F32))
    targets = jnp.transpose(jnp.concatenate(target_rows, axis=0))
    g_scaled = jnp.concatenate(parts, axis=1) + returned
    into = head_sums(g_carried * across, lanes)
    outof = head_sums(scaled * returned, lanes)
    state_dot = jnp.zeros((1, 128), F32)
    lane_one = lax.broadcasted_iota(jnp.int32, (1, 128), 1)
    product = g_new * old
    for h in range(heads):
        total = jnp.sum(
            jnp.sum(product[h * P_SIZE : (h + 1) * P_SIZE, :], axis=0, keepdims=True),
            axis=1,
            keepdims=True,
        )
        state_dot = jnp.where(lane_one == h, total, state_dot)
    g_c = dot(g_gram, b_low, ((0,), (0,))) + dot(g_carried_low, old_low, ((1,), (0,)))
    g_b = dot(g_gram, c_low, ((1,), (0,))) + dot(tailed_low, g_new_low, ((1,), (0,)))
    g_fresh = dot(g_carried_low, c_low, ((0,), (0,)))
    for h in range(heads):
        rows = slice(h * P_SIZE, (h + 1) * P_SIZE)
        gstate[rows, :] = (
            g_new[rows, :] * carrying[STRETCH - 1 : STRETCH, h : h + 1] + g_fresh[rows, :]
        )
    g_cum = targets - sources + into - outof
    g_decay = running(col >= row, g_cum) + (
        jnp.sum(outof, axis=0, keepdims=True)
        + carrying[STRETCH - 1 : STRETCH, :] * state_dot
    )
    g_step = head_sums(x * g_scaled, lanes) + g_decay * pdt_ref[1:2, :]
    g_dt = g_step * sigmoid(biased)
    gdt_ref[0:1, :] += jnp.sum(g_dt, axis=0, keepdims=True)
    gdt_ref[1:2, :] += jnp.sum(g_decay * log_decay, axis=0, keepdims=True)
    g_x = px_ref[5:6, :] * g_mixed + step_wide * g_scaled
    g_conv_x = g_x * px_ref[7:8, :] * (sig_x * (1.0 + conv_x * (1.0 - sig_x)))
    g_act = jnp.concatenate([g_b, g_c], axis=1)
    g_conv_bc = g_act * (sig_bc * (1.0 + conv_bc * (1.0 - sig_bc)))
    gx_ref[4:5, :] += jnp.sum(g_conv_x, axis=0, keepdims=True)
    gx_ref[5:6, :] += jnp.sum(g_mixed * x, axis=0, keepdims=True)
    gx_ref[6:7, :] += jnp.sum(upstream * gated * scale, axis=0, keepdims=True)
    gbc_ref[4:5, :] += jnp.sum(g_conv_bc, axis=0, keepdims=True)
    gxbuf[0:STRETCH, :] = g_conv_x
    gbcbuf[0:STRETCH, :] = g_conv_bc
    g_in_x = jnp.zeros((STRETCH, width), F32)
    g_in_bc = jnp.zeros((STRETCH, 2 * N), F32)
    for tap in range(KCONV):
        back = KCONV - 1 - tap
        rows_x = xbuf[8 - back : 8 - back + STRETCH, :]
        rows_bc = bcbuf[8 - back : 8 - back + STRETCH, :]
        later_x = gxbuf[back : back + STRETCH, :]
        later_bc = gbcbuf[back : back + STRETCH, :]
        if back:
            rows_x = jnp.where(place >= back, rows_x, 0.0)
            rows_bc = jnp.where(place >= back, rows_bc, 0.0)
            later_x = jnp.where(remain >= back, later_x, 0.0)
            later_bc = jnp.where(remain >= back, later_bc, 0.0)
        gx_ref[tap : tap + 1, :] += jnp.sum(g_conv_x * rows_x, axis=0, keepdims=True)
        gbc_ref[tap : tap + 1, :] += jnp.sum(g_conv_bc * rows_bc, axis=0, keepdims=True)
        g_in_x = g_in_x + px_ref[tap : tap + 1, :] * later_x
        g_in_bc = g_in_bc + pbc_ref[tap : tap + 1, :] * later_bc
    gxbuf[STRETCH : STRETCH + 8, :] = g_conv_x[0:8, :]
    gbcbuf[STRETCH : STRETCH + 8, :] = g_conv_bc[0:8, :]
    gx_ref[8:16, :] = g_conv_x[0:8, :]
    gbc_ref[8:16, :] = g_conv_bc[0:8, :]
    gp_ref[:, width : 2 * width] = g_in_x.astype(BF)
    gp_ref[:, 2 * width : 2 * width + 2 * N] = g_in_bc.astype(BF)
    gp_ref[:, 2 * width + 2 * N : 2 * width + 2 * N + 128] = g_dt.astype(BF)


def run_forward(carried, first, count, projected, place, remain, px, pbc, pdt):
    total = projected.shape[0]
    width = px.shape[1]
    heads = width // P_SIZE
    row_spec = lambda w, c: pl.BlockSpec((STRETCH, w), lambda i: (first + i, c))
    prev_spec = lambda w, c: pl.BlockSpec(
        (16, w), lambda i: (jnp.maximum((first + i) * (STRETCH // 16) - 1, 0), c)
    )
    whole = lambda a: pl.BlockSpec(a.shape, lambda i: (0, 0))
    state = carried[0]
    filled = tuple(carried[1:])
    results = pl.pallas_call(
        partial(forward_kernel, heads),
        grid=(count,),
        in_specs=[
            row_spec(width, 0),
            row_spec(width, 1),
            row_spec(2 * N, width // N),
            row_spec(128, (2 * width + 2 * N) // 128),
            prev_spec(width, 1),
            prev_spec(2 * N, width // N),
            row_spec(1, 0),
            row_spec(1, 0),
            whole(px),
            whole(pbc),
            whole(pdt),
            whole(state),
        ]
        + [pl.BlockSpec(memory_space=pl.ANY)] * len(filled),
        out_specs=[
            row_spec(width, 0),
            row_spec(width, 0),
            row_spec(1, 0),
            pl.BlockSpec((1, width, N), lambda i: (first + i, 0, 0)),
            whole(state),
        ],
        out_shape=[
            jax.ShapeDtypeStruct((total, width), BF),
            jax.ShapeDtypeStruct((total, width), F32),
            jax.ShapeDtypeStruct((total, 1), F32),
            jax.ShapeDtypeStruct((total // STRETCH, width, N), F32),
            jax.ShapeDtypeStruct((width, N), F32),
        ],
        scratch_shapes=[
            pltpu.VMEM((STRETCH + 8, width), F32),
            pltpu.VMEM((STRETCH + 8, 2 * N), F32),
        ],
        input_output_aliases={12: 0, 13: 1, 14: 2, 15: 3} if filled else {},
        cost_estimate=pl.CostEstimate(
            flops=count * STRETCH * 256 * 20000,
            bytes_accessed=count * STRETCH * 5000,
            transcendentals=count * STRETCH * 1500,
        ),
        name="scan_forward",
    )(*((projected,) * 6 + (place, remain, px, pbc, pdt, state) + filled))
    return (results[4],) + tuple(results[:4])


def run_backward(carried, first, count, projected, rows_in, states, px, pbc, pdt):
    total = projected.shape[0]
    width = px.shape[1]
    heads = width // P_SIZE
    columns = projected.shape[1]
    rev = lambda i: first + count - 1 - i
    row_spec = lambda w, c: pl.BlockSpec((STRETCH, w), lambda i: (rev(i), c))
    prev_spec = lambda w, c: pl.BlockSpec(
        (16, w), lambda i: (jnp.maximum(rev(i) * (STRETCH // 16) - 1, 0), c)
    )
    whole = lambda a: pl.BlockSpec(a.shape, lambda i: (0, 0))
    fixed = lambda r, w: pl.BlockSpec((r, w), lambda i: (0, 0))
    place, remain, mixed, g_out_low, scale, pull = rows_in
    gstate, gx, gbc, gdt = carried[:4]
    filled = tuple(carried[4:])
    operands = (
        (projected,) * 6
        + (place, remain, mixed, g_out_low, scale, pull, states, px, pbc, pdt)
        + (gstate, gx, gbc, gdt)
        + filled
    )
    results = pl.pallas_call(
        partial(backward_kernel, heads),
        grid=(count,),
        in_specs=[
            row_spec(width, 0),
            row_spec(width, 1),
            row_spec(2 * N, width // N),
            row_spec(128, (2 * width + 2 * N) // 128),
            prev_spec(width, 1),
            prev_spec(2 * N, width // N),
            row_spec(1, 0),
            row_spec(1, 0),
            row_spec(width, 0),
            row_spec(width, 0),
            row_spec(1, 0),
            row_spec(1, 0),
            pl.BlockSpec((1, width, N), lambda i: (rev(i), 0, 0)),
            whole(px),
            whole(pbc),
            whole(pdt),
            whole(gstate),
            whole(gx),
            whole(gbc),
            whole(gdt),
        ]
        + [pl.BlockSpec(memory_space=pl.ANY)] * len(filled),
        out_specs=[
            row_spec(columns, 0),
            row_spec(width, 0),
            fixed(width, N),
            fixed(16, width),
            fixed(16, 2 * N),
            fixed(8, 128),
        ],
        out_shape=[
            jax.ShapeDtypeStruct((total, columns), BF),
            jax.ShapeDtypeStruct((total, width), BF),
            jax.ShapeDtypeStruct((width, N), F32),
            jax.ShapeDtypeStruct((16, width), F32),
            jax.ShapeDtypeStruct((16, 2 * N), F32),
            jax.ShapeDtypeStruct((8, 128), F32),
        ],
        scratch_shapes=[
            pltpu.VMEM((STRETCH + 8, width), F32),
            pltpu.VMEM((STRETCH + 8, 2 * N), F32),
            pltpu.VMEM((STRETCH + 8, width), F32),
            pltpu.VMEM((STRETCH + 8, 2 * N), F32),
        ],
        input_output_aliases={20: 0, 21: 1} if filled else {},
        cost_estimate=pl.CostEstimate(
            flops=count * STRETCH * 256 * 40000,
            bytes_accessed=count * STRETCH * 8000,
            transcendentals=count * STRETCH * 2000,
        ),
        name="scan_backward",
    )(*operands)
    return tuple(results[2:]) + tuple(results[:2])


def after(value, *others):
    return lax.optimization_barrier((value, others))[0]


def by_row(values):
    return with_layout_constraint(values, Layout(major_to_minor=(0, 1)))


def cuts(count, parts):
    edges = [count * i // parts for i in range(parts + 1)]
    return list(zip(edges[:-1], edges[1:]))


def ring_chips():
    return [(z * 2 + x) for x, z in [(0, 0), (0, 1), (0, 2), (0, 3), (1, 3), (1, 2), (1, 1), (1, 0)]]


def hop(values, steps):
    chips = ring_chips()
    count = len(chips)
    pairs = [
        (2 * chips[p] + core, 2 * chips[(p + steps) % count] + core)
        for p in range(count)
        for core in (0, 1)
    ]
    return lax.ppermute(values, "dp", pairs)


def swap(values):
    return lax.ppermute(values, "dp", [(i, i ^ 1) for i in range(lax.axis_size("dp"))])


def ring_place():
    here = lax.axis_index("dp")
    core = here % 2
    chip = here // 2
    spot = jnp.where(chip % 2 == 0, chip // 2, 7 - chip // 2)
    return core, spot


def ring_chip(spot):
    spot = spot % 8
    return jnp.where(spot < 4, spot * 2, (7 - spot) * 2 + 1)


class RingSum:
    def __init__(self, chunk, rows):
        self.chunk = chunk
        self.mid = rows // 2
        self.step = 4
        self.last = self.sent = ()
        self.ready = (chunk(4, ()),)

    def settle(self, others):
        self.last, self.ready, _ = lax.optimization_barrier((self.last, self.ready, others))

    def advance(self, *others):
        self.settle(others)
        mid = self.mid
        if self.step == 4:
            up, down = self.ready[0][:mid], self.ready[0][mid:]
        else:
            up, down = (value.astype(F32) for value in self.last)
            first, second = self.ready
            if self.step == 3:
                up = jnp.concatenate([first[:mid] + up, first[mid:]], axis=0)
                down = jnp.concatenate([second[:mid], second[mid:] + down], axis=0)
            else:
                up, down = first + up, second + down
        self.sent = lax.optimization_barrier((up.astype(BF), down.astype(BF)))
        up, down = self.sent
        self.last = (by_row(hop(by_row(up), 1)), by_row(hop(by_row(down), -1)))
        self.step -= 1
        self.ready = tuple(
            self.chunk(steps, self.sent)
            for steps in sorted({self.step, -self.step}, reverse=True)
        )

    def finish(self, others):
        self.settle(others)
        return self.ready[0] + self.last[0].astype(F32) + self.last[1].astype(F32)


class Scatter:
    def __init__(self, left, right, *gate):
        self.ring = lax.axis_size("dp") == 16
        self.last = self.sent = ()
        if not self.ring:
            full = jnp.dot(left, right, preferred_element_type=F32).astype(BF)
            self.done = lax.psum_scatter(full, "dp", scatter_dimension=0, tiled=True).astype(F32)
            return
        self.core, spot = ring_place()
        half = right.shape[1] // 2
        take = lambda c: lax.dynamic_slice_in_dim(right, c * half, half, 1)
        sides = ((left, take(self.core)), (swap(left), swap(take(1 - self.core))))
        sides = lax.optimization_barrier((sides, gate))[0]
        self.rows = rows = left.shape[0] // 8

        def chunk(steps, deps):
            start = ring_chip(spot + steps) * rows
            return by_row(
                sum(
                    jnp.dot(
                        lax.dynamic_slice_in_dim(after(side, deps), start, rows, 0),
                        weight,
                        preferred_element_type=F32,
                    )
                    for side, weight in sides
                )
            )

        self.sum = RingSum(chunk, rows)

    def advance(self, *others):
        if self.ring:
            self.sum.advance(*others)
            self.last, self.sent = self.sum.last, self.sum.sent

    def ready(self):
        return self.sum.ready if self.ring else ()

    def finish(self, *others):
        if not self.ring:
            return self.done
        done = self.sum.finish(others)
        own = self.rows // 2
        kept = lax.dynamic_slice_in_dim(done, self.core * own, own, 0)
        got = swap(lax.dynamic_slice_in_dim(done, (1 - self.core) * own, own, 0))
        first = self.core == 0
        return jnp.concatenate(
            [jnp.where(first, kept, got), jnp.where(first, got, kept)], axis=1
        )


def other_width(values):
    return lax.ppermute(values, "width", [(0, 1), (1, 0)])


def in_order(mine, other):
    first = lax.axis_index("width") == 0
    return jnp.where(first, mine, other), jnp.where(first, other, mine)


def same_core():
    return [[2 * chip + core for chip in range(8)] for core in (0, 1)]


def gather_blocks(block):
    if lax.axis_size("dp") != 16:
        return lax.all_gather(block, "dp")
    copies = jnp.broadcast_to(block[None], (8,) + block.shape)
    mine = lax.all_to_all(copies, "dp", 0, 0, axis_index_groups=same_core())
    theirs = swap(mine)
    first = lax.axis_index("dp") % 2 == 0
    pair = jnp.stack([jnp.where(first, mine, theirs), jnp.where(first, theirs, mine)], axis=1)
    return pair.reshape((16,) + block.shape)


def adamw_kernel(first_ref, base_ref, weight_ref, moment_ref, second_ref, grad_ref, *refs):
    new_ref, first_moment_ref, squares_ref, low_ref = refs[-4:]
    grad = grad_ref[...].astype(F32).reshape(weight_ref.shape)
    base = base_ref[0, 0]
    weight = weight_ref[...]
    first = BETA_ONE * moment_ref[...] + (1.0 - BETA_ONE) * grad
    squares = BETA_TWO * second_ref[...] + (1.0 - BETA_TWO) * grad * grad
    new = weight - MATRIX_RATE * (
        (first / base) / (jnp.sqrt(squares / base) + ADAM_EPS) + MATRIX_DECAY * weight
    )
    new_ref[...] = new
    first_moment_ref[...] = first
    squares_ref[...] = squares
    low_ref[...] = new.astype(BF)


def adamw_rows(base, state, grad, first, size, filled):
    weight = state[0]
    columns = weight.shape[1]
    spec = pl.BlockSpec((size, columns), lambda i, at: (at[0] + i, 0))
    if grad.ndim == 3:
        units = grad.shape[1]
        count = grad.shape[0] * units // size
        grad_spec = pl.BlockSpec((size // units, units, columns), lambda i, at: (i, 0, 0))
    else:
        count = grad.shape[0] // size
        grad_spec = pl.BlockSpec((size, columns), lambda i, at: (i, 0))
    return tuple(
        pl.pallas_call(
            adamw_kernel,
            grid_spec=pltpu.PrefetchScalarGridSpec(
                num_scalar_prefetch=1,
                grid=(count,),
                in_specs=[pl.BlockSpec(memory_space=pltpu.SMEM), spec, spec, spec, grad_spec]
                + [pl.BlockSpec(memory_space=pl.ANY)] * len(filled),
                out_specs=[spec] * 4,
            ),
            out_shape=[jax.ShapeDtypeStruct(weight.shape, F32)] * 3
            + [jax.ShapeDtypeStruct(weight.shape, BF)],
            input_output_aliases={6 + i: i for i in range(len(filled))},
            cost_estimate=pl.CostEstimate(
                flops=count * columns * size * 10000,
                bytes_accessed=count * columns * size * 30,
                transcendentals=count * columns * size,
            ),
            name="adamw",
        )(jnp.reshape(first, (1,)).astype(jnp.int32), base, *state, grad, *filled)
    )


def tree_sum(values):
    if lax.axis_size("dp") != 16 or lax.axis_size("width") != 2:
        return lax.psum(values, ("width", "dp"))
    for low, high in ((1, 2), (4, 8)):
        near, far, across = (
            lax.ppermute(values, "dp", [(i, i ^ mask) for i in range(16)])
            for mask in (low, high, low ^ high)
        )
        values = (values + near) + (far + across)
    return values + lax.ppermute(values, "width", [(0, 1), (1, 0)])


def pad_to(values, width, axis):
    missing = width - values.shape[axis]
    if missing == 0:
        return values
    pads = [(0, 0)] * values.ndim
    pads[axis] = (0, missing)
    return jnp.pad(values, pads)


def width_sum(values):
    if lax.axis_size("width") == 2:
        return values.astype(F32) + lax.ppermute(values, "width", [(0, 1), (1, 0)]).astype(F32)
    return jnp.sum(lax.all_gather(values, "width").astype(F32), axis=0)


def per_device(
    tokens,
    cotangent,
    lengths,
    levels,
    step_count,
    weight_in,
    moment_in,
    second_in,
    weight_out,
    moment_out,
    second_out,
    small_params,
    moment_small,
    second_small,
):
    dp = lax.axis_size("dp")
    here = lax.axis_index("dp")
    rows = tokens.shape[0]
    total = rows * dp
    units = E // dp
    own_heads = H // dp
    wide = max(units, 128)
    shard = weight_in.shape[0]

    inputs_f = tokens.astype(F32)
    root = lax.rsqrt(jnp.mean(inputs_f * inputs_f, axis=1, keepdims=True) + NORM_EPS)
    g_in, g_out, conv_w, conv_b, a_log, dt_bias, d_skip = unpack(small_params)
    normed_low = (inputs_f * root * g_in).astype(BF)
    weight_low = weight_in.T.astype(BF)
    normed_all = lax.all_gather(normed_low, "dp", axis=0, tiled=True)
    pairs = jnp.concatenate(
        [weight_low[:E].reshape(dp, units, shard), weight_low[E : 2 * E].reshape(dp, units, shard)],
        axis=1,
    )
    own_cols = lax.all_to_all(pairs, "dp", 0, 0).transpose(1, 0, 2).reshape(2 * units, D).T
    shared = gather_blocks(weight_low[2 * E :]).transpose(1, 0, 2).reshape(SHARED, D).T
    own_dt = lax.dynamic_slice_in_dim(shared, 2 * N + here * own_heads, own_heads, 1)
    weight_own = jnp.concatenate(
        [
            pad_to(own_cols[:, :units], wide, 1),
            pad_to(own_cols[:, units:], wide, 1),
            shared[:, : 2 * N],
            pad_to(own_dt, 128, 1),
        ],
        axis=1,
    )
    out_weight_low = by_row(pad_to(weight_out.astype(BF), wide, 0))

    live_units = jnp.right_shift(jnp.int32(E), lax.axis_size("width") - 1 - levels[0])
    live = live_units.astype(F32)
    place, remain = row_places(lengths[0], total)
    place = place[:, None]
    remain = remain[:, None]
    own = lambda v: lax.dynamic_slice_in_dim(v, here * units, units, v.ndim - 1)
    own_h = lambda v: lax.dynamic_slice_in_dim(v, here * own_heads, own_heads, 0)
    unit_mask = (here * units + jnp.arange(units, dtype=jnp.int32) < live_units).astype(F32)
    px = pad_to(
        jnp.concatenate(
            [
                own(conv_w[:, :E]),
                own(conv_b[:E])[None],
                jnp.repeat(own_h(d_skip), P_SIZE)[None],
                own(g_out)[None],
                unit_mask[None],
            ],
            axis=0,
        ),
        wide,
        1,
    )
    pbc = pad_to(jnp.concatenate([conv_w[:, E:], conv_b[None, E:]], axis=0), 8, 0)
    pdt = pad_to(
        pad_to(jnp.stack([own_h(dt_bias), -jnp.exp(own_h(a_log))]), 128, 1), 8, 0
    )

    cotangent_all = lax.all_gather(
        after(cotangent, normed_all, weight_own), "dp", axis=0, tiled=True
    )
    projected = jnp.dot(normed_all, weight_own, preferred_element_type=F32).astype(BF)
    carried = (jnp.zeros((wide, N), F32),)
    for begin, end in cuts(total // STRETCH, FRONT_PARTS):
        carried = run_forward(
            carried, begin, end - begin, projected, place, remain, px, pbc, pdt
        )
    _, zin, mixed, square, states = carried
    partial_out = jnp.dot(zin, out_weight_low, preferred_element_type=F32).astype(BF)
    summed_out = lax.psum_scatter(partial_out, "dp", scatter_dimension=0, tiled=True)
    g_out_low = lax.dot_general(
        cotangent_all, out_weight_low, (((1,), (1,)), ((), ())), preferred_element_type=F32
    )
    pull_part = jnp.sum(g_out_low * zin.astype(F32), axis=1)
    both = jnp.sum(lax.all_gather(jnp.stack([square[:, 0], pull_part]), "dp"), axis=0)
    scale = lax.rsqrt(both[0] / live + NORM_EPS)
    pull = scale * scale * scale / live * both[1]

    rows_in = (place, remain, mixed, g_out_low, scale[:, None], pull[:, None])
    carried = (
        jnp.zeros((wide, N), F32),
        jnp.zeros((16, wide), F32),
        jnp.zeros((16, 2 * N), F32),
        jnp.zeros((8, 128), F32),
    )
    for begin, end in reversed(cuts(total // STRETCH, BACK_PARTS)):
        carried = run_backward(
            carried, begin, end - begin, projected, rows_in, states, px, pbc, pdt
        )
    _, gx, gbc, gdt, g_projected, out_low = carried
    block_out = (
        inputs_f
        + summed_out.astype(F32)
        * lax.dynamic_slice_in_dim(scale, here * rows, rows, 0)[:, None]
    ).astype(BF)

    g_weight = lax.dot_general(
        g_projected, normed_all, (((0,), (0,)), ((), ())), preferred_element_type=F32
    ).astype(BF)
    g_heads = g_weight[2 * wide + 2 * N : 2 * wide + 2 * N + own_heads]
    g_shared = jnp.concatenate(
        [
            g_weight[2 * wide : 2 * wide + 2 * N],
            lax.dynamic_update_slice_in_dim(
                jnp.zeros((H, D), BF), g_heads, here * own_heads, 0
            ),
        ],
        axis=0,
    )
    g_both = jnp.stack([g_weight[:units], g_weight[wide : wide + units]])
    paired = lax.axis_size("width") == 2

    def to_owners(values):
        return lax.all_to_all(
            values.reshape(-1, dp, shard).transpose(1, 0, 2), "dp", 0, 0
        )

    def half(slot):
        return jnp.concatenate(
            [
                lax.dynamic_index_in_dim(g_both, slot, 0, False),
                lax.dynamic_slice_in_dim(g_shared, slot * (SHARED // 2), SHARED // 2, 0),
            ],
            axis=0,
        )

    inward = Scatter(g_projected, weight_own.T, g_weight)
    if paired:
        slot = lax.axis_index("width")
        g_kept = half(slot)
        g_got = other_width(half(1 - slot))
    inward.advance()
    g_weight_out = lax.dot_general(
        after(out_low, inward.sent),
        cotangent_all,
        (((0,), (0,)), ((), ())),
        preferred_element_type=F32,
    )[:units].astype(BF)
    inward.advance(g_weight_out)
    if paired:
        g_kept, g_got, _ = lax.optimization_barrier((g_kept, g_got, inward.sent))
        g_half = to_owners((g_kept.astype(F32) + g_got.astype(F32)).astype(BF))
        total_out = other_width(after(g_weight_out, inward.sent))
        inward.advance()
        inward.advance(total_out)
        total_out = g_weight_out.astype(F32) + total_out.astype(F32)
        g_half = after(g_half, inward.sent)
        g_shared = jnp.sum(g_half[:, units:].astype(F32), axis=0).astype(BF)
        g_half = g_half[:, :units]
        g_peer = other_width(g_half)
        g_apart = other_width(g_shared)
    else:
        inward.advance()
        inward.advance()
        total_out = width_sum(g_weight_out)
        g_pairs = width_sum(to_owners(g_both.reshape(-1, D)))
        g_gate, g_x = g_pairs[:, :units], g_pairs[:, units:]
        g_apart = lax.psum_scatter(
            g_shared.reshape(SHARED, dp, shard).transpose(1, 0, 2), "dp", scatter_dimension=0
        )
        g_apart = width_sum(g_apart)
    simple = paired and units % 128 == 0 and shard == 128
    step_float = step_count[0].astype(F32)
    new_out, mom_out, sec_out = adamw_step(
        weight_out,
        moment_out,
        second_out,
        after(total_out, inward.sent),
        MATRIX_RATE,
        MATRIX_DECAY,
        step_float,
    )
    if simple:
        base = (1.0 - jnp.power(BETA_ONE, step_float)).reshape(1, 1)
        own = (weight_in.T, moment_in.T, second_in.T)
        size = 4 * units
        blocks = E // size
        moved = adamw_rows(base, own, after(g_half, inward.sent), slot * blocks, size, ())
        g_normed = inward.finish(new_out, g_peer, g_apart, moved)
    elif paired:
        g_normed = inward.finish(new_out, g_peer, g_apart)
    else:
        g_normed = inward.finish(new_out)
    if paired:
        g_apart = jnp.concatenate(in_order(g_shared, g_apart), axis=0)
    if simple:
        moved = adamw_rows(base, own, g_peer, (1 - slot) * blocks, size, moved)
        moved = adamw_rows(base, own, g_apart, 2 * E // H, H, moved)
        new_in, mom_in, sec_in, low_in = (result.T for result in moved)
    else:
        if paired:
            g_gate, g_x = in_order(g_half, g_peer)
        total_in = jnp.concatenate(
            [
                g_gate.transpose(2, 0, 1).reshape(shard, E),
                g_x.transpose(2, 0, 1).reshape(shard, E),
                g_apart.T,
            ],
            axis=1,
        ).astype(F32)
        new_in, mom_in, sec_in = adamw_step(
            weight_in, moment_in, second_in, total_in, MATRIX_RATE, MATRIX_DECAY, step_float
        )
        low_in = new_in.astype(BF)

    ratio = root * g_in
    lean = jnp.sum(g_in * g_normed * inputs_f, axis=1, keepdims=True)
    g_inputs = ratio * g_normed - inputs_f * (root * root * root / D * lean)
    grad_tokens = (cotangent.astype(F32) + g_inputs).astype(BF)
    g_g_in = jnp.sum(g_normed * inputs_f * root, axis=0)

    def placed(part, size):
        spots = jnp.zeros(part.shape[:-1] + (size,), F32)
        return lax.dynamic_update_slice_in_dim(
            spots, part, here * part.shape[-1], part.ndim - 1
        )

    conv_part = jnp.concatenate([placed(gx[:5, :units], E), gbc[:5]], axis=1)
    early = jnp.concatenate(
        [
            placed(gx[6, :units], E),
            conv_part.reshape(-1),
            placed(gdt[1, :own_heads], H),
            placed(gdt[0, :own_heads], H),
            placed(jnp.sum(gx[5, :units].reshape(own_heads, P_SIZE), axis=1), H),
        ]
    )
    total_small = tree_sum(jnp.concatenate([g_g_in, early]))
    rate_table, decay_table = small_table()
    new_small, mom_small, sec_small = adamw_step(
        small_params, moment_small, second_small, total_small, rate_table, decay_table, step_float
    )
    return (
        block_out,
        grad_tokens,
        new_in,
        mom_in,
        sec_in,
        low_in,
        new_out,
        mom_out,
        sec_out,
        new_out.astype(BF),
        new_small,
        mom_small,
        sec_small,
    )


def solution(mesh):
    return jax.shard_map(
        per_device,
        mesh=mesh,
        in_specs=(
            P(("width", "dp"), None),
            P(("width", "dp"), None),
            P("width", None),
            P("width"),
            P(),
            P("dp", None),
            P("dp", None),
            P("dp", None),
            P("dp", None),
            P("dp", None),
            P("dp", None),
            P(),
            P(),
            P(),
        ),
        out_specs=(
            P(("width", "dp"), None),
            P(("width", "dp"), None),
            P("dp", None),
            P("dp", None),
            P("dp", None),
            P("dp", None),
            P("dp", None),
            P("dp", None),
            P("dp", None),
            P("dp", None),
            P(),
            P(),
            P(),
        ),
        check_vma=False,
    )
```

```python
from functools import partial

import jax
import jax.numpy as jnp
from jax import lax
from jax.experimental import pallas as pl
from jax.experimental.layout import Layout, with_layout_constraint
from jax.experimental.pallas import tpu as pltpu
from jax.sharding import PartitionSpec as P

D = 2048
E = 4096
H = 64
P_SIZE = 64
N = 128
KCONV = 4
STRETCH = 256
K = 4352

NORM_EPS = 1e-05
ADAM_EPS = 1e-08
BETA_ONE = 0.5
BETA_TWO = 0.5
MATRIX_RATE = 0.02
MATRIX_DECAY = 0.1
PRECISE = lax.Precision.HIGHEST
BF = jnp.bfloat16
F32 = jnp.float32
LOW = -1e30
SHARED = 2 * N + H
BACK_PARTS = 1
FRONT_PARTS = 1


def small_table():
    rate_table = jnp.concatenate(
        [
            jnp.full((D,), 0.3, F32),
            jnp.full((E,), 0.3, F32),
            jnp.full((KCONV * K,), 0.2, F32),
            jnp.full((K,), 0.2, F32),
            jnp.full((H,), 0.3, F32),
            jnp.full((H,), 1.0, F32),
            jnp.full((H,), 0.3, F32),
        ]
    )
    decay_table = jnp.concatenate(
        [
            jnp.zeros((D + E,), F32),
            jnp.full((KCONV * K,), 0.1, F32),
            jnp.zeros((K + 3 * H,), F32),
        ]
    )
    return (rate_table, decay_table)


def unpack(small_params):
    offset = D + E
    conv_w = small_params[offset : offset + KCONV * K].reshape(KCONV, K)
    offset = offset + KCONV * K
    conv_b = small_params[offset : offset + K]
    offset = offset + K
    a_log = small_params[offset : offset + H]
    dt_bias = small_params[offset + H : offset + 2 * H]
    d_skip = small_params[offset + 2 * H : offset + 3 * H]
    return (small_params[:D], small_params[D : D + E], conv_w, conv_b, a_log, dt_bias, d_skip)


def row_places(lengths_row, row_count):
    seq_ends = jnp.cumsum(lengths_row)
    at = jnp.arange(row_count, dtype=jnp.int32)
    passed = seq_ends[None, :] <= at[:, None]
    begin = jnp.max(jnp.where(passed, seq_ends[None, :], 0), axis=1)
    finish = jnp.min(jnp.where(passed, row_count, seq_ends[None, :]), axis=1)
    return (at - begin, finish - 1 - at)


def adamw_step(weight, moment, second, grad, rate, decay, step_float):
    first_new = BETA_ONE * moment + (1.0 - BETA_ONE) * grad
    second_new = BETA_TWO * second + (1.0 - BETA_TWO) * grad * grad
    first_hat = first_new / (1.0 - jnp.power(BETA_ONE, step_float))
    second_hat = second_new / (1.0 - jnp.power(BETA_TWO, step_float))
    return (
        weight - rate * (first_hat / (jnp.sqrt(second_hat) + ADAM_EPS) + decay * weight),
        first_new,
        second_new,
    )


def sigmoid(v):
    return 1.0 / (1.0 + jnp.exp(-v))


def dot(a, b, dims):
    return lax.dot_general(
        a.astype(BF), b.astype(BF), (dims, ((), ())), preferred_element_type=F32
    )


def split(values, count):
    parts = []
    for _ in range(count):
        part = values.astype(BF)
        values = values - part.astype(F32)
        parts.append(part)
    return parts


def head_lanes(heads):
    row = lax.broadcasted_iota(jnp.int32, (128, heads * P_SIZE), 0)
    lane = lax.broadcasted_iota(jnp.int32, (128, heads * P_SIZE), 1)
    return jnp.where(lane // P_SIZE == row, 1.0, 0.0).astype(BF)


def spread(columns, lanes):
    return sum(dot(part, lanes, ((1,), (0,))) for part in split(columns, 2))


def head_sums(values, lanes):
    return sum(dot(part, lanes, ((1,), (1,))) for part in split(values, 2))


def running(mask, values):
    mask = jnp.where(mask, 1.0, 0.0).astype(BF)
    return sum(dot(mask, part, ((1,), (0,))) for part in split(values, 3))


def convolve(buffer, weights, bias, place):
    total = bias + jnp.zeros((STRETCH, buffer.shape[1]), F32)
    for tap in range(KCONV):
        back = KCONV - 1 - tap
        rows = buffer[8 - back : 8 - back + STRETCH, :]
        if back:
            rows = jnp.where(place >= back, rows, 0.0)
        total = total + weights[tap : tap + 1, :] * rows
    return total


def block_terms(place, remain, dt_in, pdt):
    row = lax.broadcasted_iota(jnp.int32, (STRETCH, STRETCH), 0)
    col = lax.broadcasted_iota(jnp.int32, (STRETCH, STRETCH), 1)
    at = lax.broadcasted_iota(jnp.int32, (STRETCH, 1), 0)
    biased = dt_in + pdt[0:1, :]
    step = jnp.maximum(biased, 0.0) + jnp.log1p(jnp.exp(-jnp.abs(biased)))
    log_decay = step * pdt[1:2, :]
    cum = running(col <= row, log_decay)
    cum_t = jnp.transpose(cum)
    carrying = jnp.where(place >= at + 1, jnp.exp(cum), 0.0)
    tail_ok = remain >= STRETCH - 1 - at
    tail = jnp.exp(jnp.where(tail_ok, cum[STRETCH - 1 : STRETCH, :] - cum, LOW))
    return row, col, biased, step, log_decay, cum, cum_t, carrying, tail


def forward_kernel(
    heads,
    gate_ref,
    x_ref,
    bc_ref,
    dt_ref,
    xprev_ref,
    bcprev_ref,
    place_ref,
    remain_ref,
    px_ref,
    pbc_ref,
    pdt_ref,
    state_in,
    *rest,
):
    zin_ref, mixed_ref, square_ref, states_ref, state, xbuf, bcbuf = rest[-7:]

    @pl.when(pl.program_id(0) == 0)
    def _():
        state[...] = state_in[...]

    xbuf[0:8, :] = xprev_ref[8:16, :].astype(F32)
    bcbuf[0:8, :] = bcprev_ref[8:16, :].astype(F32)
    place = place_ref[...]
    remain = remain_ref[...]
    xbuf[8 : 8 + STRETCH, :] = x_ref[...].astype(F32)
    bcbuf[8 : 8 + STRETCH, :] = bc_ref[...].astype(F32)
    conv_x = convolve(xbuf, px_ref[0:4, :], px_ref[4:5, :], place)
    conv_bc = convolve(bcbuf, pbc_ref[0:4, :], pbc_ref[4:5, :], place)
    x = conv_x * sigmoid(conv_x) * px_ref[7:8, :]
    act_bc = conv_bc * sigmoid(conv_bc)
    b_low = act_bc[:, :N].astype(BF)
    c_low = act_bc[:, N:].astype(BF)
    row, col, _, step, _, cum, cum_t, carrying, tail = block_terms(
        place, remain, dt_ref[...].astype(F32), pdt_ref[...]
    )
    visible = (col <= row) & (row - col <= place)
    lanes = head_lanes(heads)
    scaled = x * spread(step, lanes)
    scaled_low = scaled.astype(BF)
    gram = dot(c_low, b_low, ((1,), (1,)))
    old = state[...]
    states_ref[0] = old
    across = dot(c_low, old, ((1,), (1,))) * spread(carrying, lanes)
    parts = []
    for h in range(heads):
        decay = jnp.exp(jnp.where(visible, cum[:, h : h + 1] - cum_t[h : h + 1, :], LOW))
        parts.append(
            dot(gram * decay, scaled_low[:, h * P_SIZE : (h + 1) * P_SIZE], ((1,), (0,)))
        )
    mixed = jnp.concatenate(parts, axis=1) + across + px_ref[5:6, :] * x
    fresh = dot(scaled * spread(tail, lanes), b_low, ((0,), (0,)))
    for h in range(heads):
        rows = slice(h * P_SIZE, (h + 1) * P_SIZE)
        state[rows, :] = (
            old[rows, :] * carrying[STRETCH - 1 : STRETCH, h : h + 1] + fresh[rows, :]
        )
    gate = gate_ref[...].astype(F32)
    gated = mixed * (gate * sigmoid(gate))
    mixed_ref[...] = mixed
    zin_ref[...] = (gated * px_ref[6:7, :]).astype(BF)
    square_ref[...] = jnp.sum(gated * gated, axis=1, keepdims=True)


def backward_kernel(
    heads,
    gate_ref,
    x_ref,
    bc_ref,
    dt_ref,
    xprev_ref,
    bcprev_ref,
    place_ref,
    remain_ref,
    mixed_ref,
    gout_ref,
    scale_ref,
    pull_ref,
    states_ref,
    px_ref,
    pbc_ref,
    pdt_ref,
    gstate_in,
    gx_in,
    gbc_in,
    gdt_in,
    *rest,
):
    gp_ref, low_ref, gstate, gx_ref, gbc_ref, gdt_ref, xbuf, bcbuf, gxbuf, gbcbuf = rest[-10:]
    width = x_ref.shape[1]

    @pl.when(pl.program_id(0) == 0)
    def _():
        gstate[...] = gstate_in[...]
        gxbuf[STRETCH : STRETCH + 8, :] = gx_in[8:16, :]
        gbcbuf[STRETCH : STRETCH + 8, :] = gbc_in[8:16, :]
        gx_ref[...] = gx_in[...]
        gbc_ref[...] = gbc_in[...]
        gdt_ref[...] = gdt_in[...]

    place = place_ref[...]
    remain = remain_ref[...]
    xbuf[0:8, :] = xprev_ref[8:16, :].astype(F32)
    bcbuf[0:8, :] = bcprev_ref[8:16, :].astype(F32)
    xbuf[8 : 8 + STRETCH, :] = x_ref[...].astype(F32)
    bcbuf[8 : 8 + STRETCH, :] = bc_ref[...].astype(F32)
    conv_x = convolve(xbuf, px_ref[0:4, :], px_ref[4:5, :], place)
    conv_bc = convolve(bcbuf, pbc_ref[0:4, :], pbc_ref[4:5, :], place)
    sig_x = sigmoid(conv_x)
    sig_bc = sigmoid(conv_bc)
    x = conv_x * sig_x * px_ref[7:8, :]
    act_bc = conv_bc * sig_bc
    b_low = act_bc[:, :N].astype(BF)
    c_low = act_bc[:, N:].astype(BF)
    row, col, biased, step, log_decay, cum, cum_t, carrying, tail = block_terms(
        place, remain, dt_ref[...].astype(F32), pdt_ref[...]
    )
    visible = (col >= row) & (col - row <= remain)
    lanes = head_lanes(heads)

    gate = gate_ref[...].astype(F32)
    sig = sigmoid(gate)
    silu = gate * sig
    mixed = mixed_ref[...]
    gated = mixed * silu
    g_out = px_ref[6:7, :]
    scale = scale_ref[...]
    upstream = gout_ref[...]
    low_ref[...] = (gated * scale * g_out).astype(BF)
    g_gated = scale * g_out * upstream - gated * pull_ref[...]
    g_mixed = g_gated * silu
    gp_ref[:, 0:width] = (g_gated * mixed * (sig * (1.0 + gate * (1.0 - sig)))).astype(BF)

    step_wide = spread(step, lanes)
    carry_wide = spread(carrying, lanes)
    tail_wide = spread(tail, lanes)
    scaled = x * step_wide
    scaled_low = scaled.astype(BF)
    g_low = g_mixed.astype(BF)
    old = states_ref[0]
    g_new = gstate[...]
    old_low = old.astype(BF)
    g_new_low = g_new.astype(BF)
    gram = dot(b_low, c_low, ((1,), (1,)))
    across = dot(c_low, old_low, ((1,), (1,)))
    returned = dot(b_low, g_new_low, ((1,), (1,))) * tail_wide
    g_carried = g_mixed * carry_wide
    g_carried_low = g_carried.astype(BF)
    tailed_low = (scaled * tail_wide).astype(BF)

    g_gram = jnp.zeros((STRETCH, STRETCH), F32)
    lane = lax.broadcasted_iota(jnp.int32, (STRETCH, 128), 1)
    sources = jnp.zeros((STRETCH, 128), F32)
    target_rows = []
    parts = []
    for h in range(heads):
        cols = slice(h * P_SIZE, (h + 1) * P_SIZE)
        decay = jnp.exp(jnp.where(visible, cum_t[h : h + 1, :] - cum[:, h : h + 1], LOW))
        mixing = gram * decay
        g_mixing = dot(scaled_low[:, cols], g_low[:, cols], ((1,), (1,)))
        parts.append(dot(mixing, g_low[:, cols], ((1,), (0,))))
        g_gram = g_gram + g_mixing * decay
        both = g_mixing * mixing
        sources = jnp.where(lane == h, jnp.sum(both, axis=1, keepdims=True), sources)
        target_rows.append(jnp.sum(both, axis=0, keepdims=True))
    target_rows.append(jnp.zeros((128 - heads, STRETCH), F32))
    targets = jnp.transpose(jnp.concatenate(target_rows, axis=0))
    g_scaled = jnp.concatenate(parts, axis=1) + returned
    into = head_sums(g_carried * across, lanes)
    outof = head_sums(scaled * returned, lanes)
    state_dot = jnp.zeros((1, 128), F32)
    lane_one = lax.broadcasted_iota(jnp.int32, (1, 128), 1)
    product = g_new * old
    for h in range(heads):
        total = jnp.sum(
            jnp.sum(product[h * P_SIZE : (h + 1) * P_SIZE, :], axis=0, keepdims=True),
            axis=1,
            keepdims=True,
        )
        state_dot = jnp.where(lane_one == h, total, state_dot)
    g_c = dot(g_gram, b_low, ((0,), (0,))) + dot(g_carried_low, old_low, ((1,), (0,)))
    g_b = dot(g_gram, c_low, ((1,), (0,))) + dot(tailed_low, g_new_low, ((1,), (0,)))
    g_fresh = dot(g_carried_low, c_low, ((0,), (0,)))
    for h in range(heads):
        rows = slice(h * P_SIZE, (h + 1) * P_SIZE)
        gstate[rows, :] = (
            g_new[rows, :] * carrying[STRETCH - 1 : STRETCH, h : h + 1] + g_fresh[rows, :]
        )
    g_cum = targets - sources + into - outof
    g_decay = running(col >= row, g_cum) + (
        jnp.sum(outof, axis=0, keepdims=True)
        + carrying[STRETCH - 1 : STRETCH, :] * state_dot
    )
    g_step = head_sums(x * g_scaled, lanes) + g_decay * pdt_ref[1:2, :]
    g_dt = g_step * sigmoid(biased)
    gdt_ref[0:1, :] += jnp.sum(g_dt, axis=0, keepdims=True)
    gdt_ref[1:2, :] += jnp.sum(g_decay * log_decay, axis=0, keepdims=True)
    g_x = px_ref[5:6, :] * g_mixed + step_wide * g_scaled
    g_conv_x = g_x * px_ref[7:8, :] * (sig_x * (1.0 + conv_x * (1.0 - sig_x)))
    g_act = jnp.concatenate([g_b, g_c], axis=1)
    g_conv_bc = g_act * (sig_bc * (1.0 + conv_bc * (1.0 - sig_bc)))
    gx_ref[4:5, :] += jnp.sum(g_conv_x, axis=0, keepdims=True)
    gx_ref[5:6, :] += jnp.sum(g_mixed * x, axis=0, keepdims=True)
    gx_ref[6:7, :] += jnp.sum(upstream * gated * scale, axis=0, keepdims=True)
    gbc_ref[4:5, :] += jnp.sum(g_conv_bc, axis=0, keepdims=True)
    gxbuf[0:STRETCH, :] = g_conv_x
    gbcbuf[0:STRETCH, :] = g_conv_bc
    g_in_x = jnp.zeros((STRETCH, width), F32)
    g_in_bc = jnp.zeros((STRETCH, 2 * N), F32)
    for tap in range(KCONV):
        back = KCONV - 1 - tap
        rows_x = xbuf[8 - back : 8 - back + STRETCH, :]
        rows_bc = bcbuf[8 - back : 8 - back + STRETCH, :]
        later_x = gxbuf[back : back + STRETCH, :]
        later_bc = gbcbuf[back : back + STRETCH, :]
        if back:
            rows_x = jnp.where(place >= back, rows_x, 0.0)
            rows_bc = jnp.where(place >= back, rows_bc, 0.0)
            later_x = jnp.where(remain >= back, later_x, 0.0)
            later_bc = jnp.where(remain >= back, later_bc, 0.0)
        gx_ref[tap : tap + 1, :] += jnp.sum(g_conv_x * rows_x, axis=0, keepdims=True)
        gbc_ref[tap : tap + 1, :] += jnp.sum(g_conv_bc * rows_bc, axis=0, keepdims=True)
        g_in_x = g_in_x + px_ref[tap : tap + 1, :] * later_x
        g_in_bc = g_in_bc + pbc_ref[tap : tap + 1, :] * later_bc
    gxbuf[STRETCH : STRETCH + 8, :] = g_conv_x[0:8, :]
    gbcbuf[STRETCH : STRETCH + 8, :] = g_conv_bc[0:8, :]
    gx_ref[8:16, :] = g_conv_x[0:8, :]
    gbc_ref[8:16, :] = g_conv_bc[0:8, :]
    gp_ref[:, width : 2 * width] = g_in_x.astype(BF)
    gp_ref[:, 2 * width : 2 * width + 2 * N] = g_in_bc.astype(BF)
    gp_ref[:, 2 * width + 2 * N : 2 * width + 2 * N + 128] = g_dt.astype(BF)


def run_forward(carried, first, count, projected, place, remain, px, pbc, pdt):
    total = projected.shape[0]
    width = px.shape[1]
    heads = width // P_SIZE
    row_spec = lambda w, c: pl.BlockSpec((STRETCH, w), lambda i: (first + i, c))
    prev_spec = lambda w, c: pl.BlockSpec(
        (16, w), lambda i: (jnp.maximum((first + i) * (STRETCH // 16) - 1, 0), c)
    )
    whole = lambda a: pl.BlockSpec(a.shape, lambda i: (0, 0))
    state = carried[0]
    filled = tuple(carried[1:])
    results = pl.pallas_call(
        partial(forward_kernel, heads),
        grid=(count,),
        in_specs=[
            row_spec(width, 0),
            row_spec(width, 1),
            row_spec(2 * N, width // N),
            row_spec(128, (2 * width + 2 * N) // 128),
            prev_spec(width, 1),
            prev_spec(2 * N, width // N),
            row_spec(1, 0),
            row_spec(1, 0),
            whole(px),
            whole(pbc),
            whole(pdt),
            whole(state),
        ]
        + [pl.BlockSpec(memory_space=pl.ANY)] * len(filled),
        out_specs=[
            row_spec(width, 0),
            row_spec(width, 0),
            row_spec(1, 0),
            pl.BlockSpec((1, width, N), lambda i: (first + i, 0, 0)),
            whole(state),
        ],
        out_shape=[
            jax.ShapeDtypeStruct((total, width), BF),
            jax.ShapeDtypeStruct((total, width), F32),
            jax.ShapeDtypeStruct((total, 1), F32),
            jax.ShapeDtypeStruct((total // STRETCH, width, N), F32),
            jax.ShapeDtypeStruct((width, N), F32),
        ],
        scratch_shapes=[
            pltpu.VMEM((STRETCH + 8, width), F32),
            pltpu.VMEM((STRETCH + 8, 2 * N), F32),
        ],
        input_output_aliases={12: 0, 13: 1, 14: 2, 15: 3} if filled else {},
        cost_estimate=pl.CostEstimate(
            flops=count * STRETCH * 256 * 20000,
            bytes_accessed=count * STRETCH * 5000,
            transcendentals=count * STRETCH * 1500,
        ),
        name="scan_forward",
    )(*((projected,) * 6 + (place, remain, px, pbc, pdt, state) + filled))
    return (results[4],) + tuple(results[:4])


def run_backward(carried, first, count, projected, rows_in, states, px, pbc, pdt):
    total = projected.shape[0]
    width = px.shape[1]
    heads = width // P_SIZE
    columns = projected.shape[1]
    rev = lambda i: first + count - 1 - i
    row_spec = lambda w, c: pl.BlockSpec((STRETCH, w), lambda i: (rev(i), c))
    prev_spec = lambda w, c: pl.BlockSpec(
        (16, w), lambda i: (jnp.maximum(rev(i) * (STRETCH // 16) - 1, 0), c)
    )
    whole = lambda a: pl.BlockSpec(a.shape, lambda i: (0, 0))
    fixed = lambda r, w: pl.BlockSpec((r, w), lambda i: (0, 0))
    place, remain, mixed, g_out_low, scale, pull = rows_in
    gstate, gx, gbc, gdt = carried[:4]
    filled = tuple(carried[4:])
    operands = (
        (projected,) * 6
        + (place, remain, mixed, g_out_low, scale, pull, states, px, pbc, pdt)
        + (gstate, gx, gbc, gdt)
        + filled
    )
    results = pl.pallas_call(
        partial(backward_kernel, heads),
        grid=(count,),
        in_specs=[
            row_spec(width, 0),
            row_spec(width, 1),
            row_spec(2 * N, width // N),
            row_spec(128, (2 * width + 2 * N) // 128),
            prev_spec(width, 1),
            prev_spec(2 * N, width // N),
            row_spec(1, 0),
            row_spec(1, 0),
            row_spec(width, 0),
            row_spec(width, 0),
            row_spec(1, 0),
            row_spec(1, 0),
            pl.BlockSpec((1, width, N), lambda i: (rev(i), 0, 0)),
            whole(px),
            whole(pbc),
            whole(pdt),
            whole(gstate),
            whole(gx),
            whole(gbc),
            whole(gdt),
        ]
        + [pl.BlockSpec(memory_space=pl.ANY)] * len(filled),
        out_specs=[
            row_spec(columns, 0),
            row_spec(width, 0),
            fixed(width, N),
            fixed(16, width),
            fixed(16, 2 * N),
            fixed(8, 128),
        ],
        out_shape=[
            jax.ShapeDtypeStruct((total, columns), BF),
            jax.ShapeDtypeStruct((total, width), BF),
            jax.ShapeDtypeStruct((width, N), F32),
            jax.ShapeDtypeStruct((16, width), F32),
            jax.ShapeDtypeStruct((16, 2 * N), F32),
            jax.ShapeDtypeStruct((8, 128), F32),
        ],
        scratch_shapes=[
            pltpu.VMEM((STRETCH + 8, width), F32),
            pltpu.VMEM((STRETCH + 8, 2 * N), F32),
            pltpu.VMEM((STRETCH + 8, width), F32),
            pltpu.VMEM((STRETCH + 8, 2 * N), F32),
        ],
        input_output_aliases={20: 0, 21: 1} if filled else {},
        cost_estimate=pl.CostEstimate(
            flops=count * STRETCH * 256 * 40000,
            bytes_accessed=count * STRETCH * 8000,
            transcendentals=count * STRETCH * 2000,
        ),
        name="scan_backward",
    )(*operands)
    return tuple(results[2:]) + tuple(results[:2])


def after(value, *others):
    return lax.optimization_barrier((value, others))[0]


def by_row(values):
    return with_layout_constraint(values, Layout(major_to_minor=(0, 1)))


def cuts(count, parts):
    edges = [count * i // parts for i in range(parts + 1)]
    return list(zip(edges[:-1], edges[1:]))


def ring_chips():
    return [(z * 2 + x) for x, z in [(0, 0), (0, 1), (0, 2), (0, 3), (1, 3), (1, 2), (1, 1), (1, 0)]]


def hop(values, steps):
    chips = ring_chips()
    count = len(chips)
    pairs = [
        (2 * chips[p] + core, 2 * chips[(p + steps) % count] + core)
        for p in range(count)
        for core in (0, 1)
    ]
    return lax.ppermute(values, "dp", pairs)


def swap(values):
    return lax.ppermute(values, "dp", [(i, i ^ 1) for i in range(lax.axis_size("dp"))])


def ring_place():
    here = lax.axis_index("dp")
    core = here % 2
    chip = here // 2
    spot = jnp.where(chip % 2 == 0, chip // 2, 7 - chip // 2)
    return core, spot


def ring_chip(spot):
    spot = spot % 8
    return jnp.where(spot < 4, spot * 2, (7 - spot) * 2 + 1)


def absorb_kernel(count, by_rows, starts_ref, *refs):
    pieces = refs[:count]
    weight_ref = refs[count]
    kept_ref, product_ref, held = refs[-3:]
    for j in range(count):

        @pl.when(pl.program_id(0) == j)
        def _(j=j):
            held[...] = pieces[j][...]

    values = held[...]
    kept_ref[...] = values
    product_ref[...] = lax.dot_general(
        values,
        weight_ref[...],
        (((1,), (1 if by_rows else 0,)), ((), ())),
        preferred_element_type=F32,
    ).astype(product_ref.dtype)


def absorb(pieces, starts, total, filled, weight, by_rows, kind):
    size, depth = pieces[0].shape
    columns = weight.shape[0 if by_rows else 1]
    count = len(pieces)
    whole = lambda a: pl.BlockSpec(a.shape, lambda i, at: (0, 0))
    placed = lambda w: pl.BlockSpec((size, w), lambda i, at: (at[i], 0))
    return pl.pallas_call(
        partial(absorb_kernel, count, by_rows),
        grid_spec=pltpu.PrefetchScalarGridSpec(
            num_scalar_prefetch=1,
            grid=(count,),
            in_specs=[whole(piece) for piece in pieces]
            + [whole(weight)]
            + [pl.BlockSpec(memory_space=pl.ANY)] * len(filled),
            out_specs=[placed(depth), placed(columns)],
            scratch_shapes=[pltpu.VMEM((size, depth), BF)],
        ),
        out_shape=[
            jax.ShapeDtypeStruct((total, depth), BF),
            jax.ShapeDtypeStruct((total, columns), kind),
        ],
        input_output_aliases={count + 2: 0, count + 3: 1} if filled else {},
        cost_estimate=pl.CostEstimate(
            flops=40 * count * size * depth * columns,
            bytes_accessed=4 * count * size * depth + 2 * depth * columns,
            transcendentals=0,
        ),
        name="absorb_rows",
    )(starts, *pieces, weight, *filled)


class Gather:
    def __init__(self, values):
        self.rows = values.shape[0]
        self.core, self.spot = ring_place()
        self.last = (values, values)
        self.arrived = [((values, ring_chip(self.spot), 0),)]
        self.swapped = []
        self.sent = self.filled = ()

    def settle(self, *others):
        self.last, self.filled, _ = lax.optimization_barrier((self.last, self.filled, others))
        step = len(self.swapped)
        if step:
            offset = self.rows // 2 if step == 4 else 0
            self.arrived.append(
                (
                    (self.last[0], ring_chip(self.spot - step), 0),
                    (self.last[1], ring_chip(self.spot + step), offset),
                )
            )
        self.swapped.append([by_row(swap(by_row(piece))) for piece, _, _ in self.arrived[-1]])

    def advance(self):
        ahead, behind = self.last
        if len(self.swapped) == 4:
            ahead, behind = ahead[: self.rows // 2], behind[self.rows // 2 :]
        self.sent, self.swapped[-1] = lax.optimization_barrier(
            ((ahead, behind), self.swapped[-1])
        )
        ahead, behind = self.sent
        self.last = (by_row(hop(by_row(ahead), 1)), by_row(hop(by_row(behind), -1)))

    def take(self, weight, *hops):
        pieces, starts = [], []
        for k in hops:
            for (piece, chip, offset), other in zip(self.arrived[k], self.swapped[k]):
                for part, core in ((piece, self.core), (other, 1 - self.core)):
                    pieces.append(part)
                    starts.append(((2 * chip + core) * self.rows + offset) // piece.shape[0])
        pieces, _ = lax.optimization_barrier((pieces, self.sent))
        self.filled = tuple(
            absorb(
                pieces,
                jnp.stack(starts).astype(jnp.int32),
                16 * self.rows,
                self.filled,
                weight,
                False,
                BF,
            )
        )


class RingSum:
    def __init__(self, chunk, rows):
        self.chunk = chunk
        self.mid = rows // 2
        self.step = 4
        self.last = self.sent = ()
        self.ready = (chunk(4, ()),)

    def settle(self, others):
        self.last, self.ready, _ = lax.optimization_barrier((self.last, self.ready, others))

    def advance(self, *others):
        self.settle(others)
        mid = self.mid
        if self.step == 4:
            up, down = self.ready[0][:mid], self.ready[0][mid:]
        else:
            up, down = (value.astype(F32) for value in self.last)
            first, second = self.ready
            if self.step == 3:
                up = jnp.concatenate([first[:mid] + up, first[mid:]], axis=0)
                down = jnp.concatenate([second[:mid], second[mid:] + down], axis=0)
            else:
                up, down = first + up, second + down
        self.sent = lax.optimization_barrier((up.astype(BF), down.astype(BF)))
        up, down = self.sent
        self.last = (by_row(hop(by_row(up), 1)), by_row(hop(by_row(down), -1)))
        self.step -= 1
        self.ready = tuple(
            self.chunk(steps, self.sent)
            for steps in sorted({self.step, -self.step}, reverse=True)
        )

    def finish(self, others):
        self.settle(others)
        return self.ready[0] + self.last[0].astype(F32) + self.last[1].astype(F32)


class Scatter:
    def __init__(self, left, right, *gate):
        self.ring = lax.axis_size("dp") == 16
        self.last = self.sent = ()
        if not self.ring:
            full = jnp.dot(left, right, preferred_element_type=F32).astype(BF)
            self.done = lax.psum_scatter(full, "dp", scatter_dimension=0, tiled=True).astype(F32)
            return
        self.core, spot = ring_place()
        half = right.shape[1] // 2
        take = lambda c: lax.dynamic_slice_in_dim(right, c * half, half, 1)
        sides = ((left, take(self.core)), (swap(left), swap(take(1 - self.core))))
        sides = lax.optimization_barrier((sides, gate))[0]
        self.rows = rows = left.shape[0] // 8

        def chunk(steps, deps):
            start = ring_chip(spot + steps) * rows
            return by_row(
                sum(
                    jnp.dot(
                        lax.dynamic_slice_in_dim(after(side, deps), start, rows, 0),
                        weight,
                        preferred_element_type=F32,
                    )
                    for side, weight in sides
                )
            )

        self.sum = RingSum(chunk, rows)

    def advance(self, *others):
        if self.ring:
            self.sum.advance(*others)
            self.last, self.sent = self.sum.last, self.sum.sent

    def ready(self):
        return self.sum.ready if self.ring else ()

    def finish(self, *others):
        if not self.ring:
            return self.done
        done = self.sum.finish(others)
        own = self.rows // 2
        kept = lax.dynamic_slice_in_dim(done, self.core * own, own, 0)
        got = swap(lax.dynamic_slice_in_dim(done, (1 - self.core) * own, own, 0))
        first = self.core == 0
        return jnp.concatenate(
            [jnp.where(first, kept, got), jnp.where(first, got, kept)], axis=1
        )


def other_width(values):
    return lax.ppermute(values, "width", [(0, 1), (1, 0)])


def in_order(mine, other):
    first = lax.axis_index("width") == 0
    return jnp.where(first, mine, other), jnp.where(first, other, mine)


def weight_halves(weight_low, units):
    dp = lax.axis_size("dp")
    heads = weight_low[: 2 * E].reshape(2, dp, units, weight_low.shape[1])
    common = weight_low[2 * E :]
    if lax.axis_size("width") == 2:
        slot = lax.axis_index("width")
        heads = lax.dynamic_slice_in_dim(heads, slot, 1, 0)
        common = lax.dynamic_slice_in_dim(common, slot * (SHARED // 2), SHARED // 2, 0)
    return jnp.concatenate(
        [
            heads.transpose(1, 0, 2, 3).reshape(dp, -1, heads.shape[3]),
            jnp.broadcast_to(common[None], (dp,) + common.shape),
        ],
        axis=1,
    )


def join_weight(mine, units, wide, *gate):
    own_heads = units // P_SIZE
    if lax.axis_size("width") == 2:
        other = after(other_width(mine), gate)
        first, second = in_order(mine, other)
        gate_rows, x_rows = first[:units], second[:units]
        shared = jnp.concatenate([first[units:], second[units:]], axis=0)
    else:
        gate_rows, x_rows, shared = mine[:units], mine[units : 2 * units], mine[2 * units :]
    own_dt = lax.dynamic_slice_in_dim(
        shared, 2 * N + lax.axis_index("dp") * own_heads, own_heads, 0
    )
    return jnp.concatenate(
        [
            pad_to(gate_rows, wide, 0),
            pad_to(x_rows, wide, 0),
            shared[: 2 * N],
            pad_to(own_dt, 128, 0),
        ],
        axis=0,
    ).T


def adamw_kernel(first_ref, base_ref, weight_ref, moment_ref, second_ref, grad_ref, *refs):
    new_ref, first_moment_ref, squares_ref, low_ref = refs[-4:]
    grad = grad_ref[...].astype(F32).reshape(weight_ref.shape)
    base = base_ref[0, 0]
    weight = weight_ref[...]
    first = BETA_ONE * moment_ref[...] + (1.0 - BETA_ONE) * grad
    squares = BETA_TWO * second_ref[...] + (1.0 - BETA_TWO) * grad * grad
    new = weight - MATRIX_RATE * (
        (first / base) / (jnp.sqrt(squares / base) + ADAM_EPS) + MATRIX_DECAY * weight
    )
    new_ref[...] = new
    first_moment_ref[...] = first
    squares_ref[...] = squares
    low_ref[...] = new.astype(BF)


def adamw_rows(base, state, grad, first, size, filled):
    weight = state[0]
    columns = weight.shape[1]
    spec = pl.BlockSpec((size, columns), lambda i, at: (at[0] + i, 0))
    if grad.ndim == 3:
        units = grad.shape[1]
        count = grad.shape[0] * units // size
        grad_spec = pl.BlockSpec((size // units, units, columns), lambda i, at: (i, 0, 0))
    else:
        count = grad.shape[0] // size
        grad_spec = pl.BlockSpec((size, columns), lambda i, at: (i, 0))
    return tuple(
        pl.pallas_call(
            adamw_kernel,
            grid_spec=pltpu.PrefetchScalarGridSpec(
                num_scalar_prefetch=1,
                grid=(count,),
                in_specs=[pl.BlockSpec(memory_space=pltpu.SMEM), spec, spec, spec, grad_spec]
                + [pl.BlockSpec(memory_space=pl.ANY)] * len(filled),
                out_specs=[spec] * 4,
            ),
            out_shape=[jax.ShapeDtypeStruct(weight.shape, F32)] * 3
            + [jax.ShapeDtypeStruct(weight.shape, BF)],
            input_output_aliases={6 + i: i for i in range(len(filled))},
            cost_estimate=pl.CostEstimate(
                flops=count * columns * size * 10000,
                bytes_accessed=count * columns * size * 30,
                transcendentals=count * columns * size,
            ),
            name="adamw",
        )(jnp.reshape(first, (1,)).astype(jnp.int32), base, *state, grad, *filled)
    )


def tree_sum(values):
    if lax.axis_size("dp") != 16 or lax.axis_size("width") != 2:
        return lax.psum(values, ("width", "dp"))
    for low, high in ((1, 2), (4, 8)):
        near, far, across = (
            lax.ppermute(values, "dp", [(i, i ^ mask) for i in range(16)])
            for mask in (low, high, low ^ high)
        )
        values = (values + near) + (far + across)
    return values + lax.ppermute(values, "width", [(0, 1), (1, 0)])


def pad_to(values, width, axis):
    missing = width - values.shape[axis]
    if missing == 0:
        return values
    pads = [(0, 0)] * values.ndim
    pads[axis] = (0, missing)
    return jnp.pad(values, pads)


def width_sum(values):
    if lax.axis_size("width") == 2:
        return values.astype(F32) + lax.ppermute(values, "width", [(0, 1), (1, 0)]).astype(F32)
    return jnp.sum(lax.all_gather(values, "width").astype(F32), axis=0)


def per_device(
    tokens,
    cotangent,
    lengths,
    levels,
    step_count,
    weight_in,
    moment_in,
    second_in,
    weight_out,
    moment_out,
    second_out,
    small_params,
    moment_small,
    second_small,
):
    dp = lax.axis_size("dp")
    here = lax.axis_index("dp")
    rows = tokens.shape[0]
    total = rows * dp
    units = E // dp
    own_heads = H // dp
    wide = max(units, 128)
    shard = weight_in.shape[0]

    inputs_f = tokens.astype(F32)
    root = lax.rsqrt(jnp.mean(inputs_f * inputs_f, axis=1, keepdims=True) + NORM_EPS)
    g_in, g_out, conv_w, conv_b, a_log, dt_bias, d_skip = unpack(small_params)
    normed_low = (inputs_f * root * g_in).astype(BF)
    weight_low = weight_in.T.astype(BF)
    ring = dp == 16
    if ring:
        gather = Gather(by_row(normed_low))
        gather.settle()
        gather.advance()
    else:
        normed_all = lax.all_gather(normed_low, "dp", axis=0, tiled=True)
    mine = lax.all_to_all(weight_halves(weight_low, units), "dp", 0, 0)
    mine = mine.transpose(1, 0, 2).reshape(-1, D)
    out_weight_low = by_row(pad_to(weight_out.astype(BF), wide, 0))

    live_units = jnp.right_shift(jnp.int32(E), lax.axis_size("width") - 1 - levels[0])
    live = live_units.astype(F32)
    place, remain = row_places(lengths[0], total)
    place = place[:, None]
    remain = remain[:, None]
    own = lambda v: lax.dynamic_slice_in_dim(v, here * units, units, v.ndim - 1)
    own_h = lambda v: lax.dynamic_slice_in_dim(v, here * own_heads, own_heads, 0)
    unit_mask = (here * units + jnp.arange(units, dtype=jnp.int32) < live_units).astype(F32)
    px = pad_to(
        jnp.concatenate(
            [
                own(conv_w[:, :E]),
                own(conv_b[:E])[None],
                jnp.repeat(own_h(d_skip), P_SIZE)[None],
                own(g_out)[None],
                unit_mask[None],
            ],
            axis=0,
        ),
        wide,
        1,
    )
    pbc = pad_to(jnp.concatenate([conv_w[:, E:], conv_b[None, E:]], axis=0), 8, 0)
    pdt = pad_to(
        pad_to(jnp.stack([own_h(dt_bias), -jnp.exp(own_h(a_log))]), 128, 1), 8, 0
    )

    if ring:
        gather.settle(mine, place, remain)
        gather.advance()
        mine = after(mine, gather.sent)
        released = after(cotangent, gather.sent)
        gather.settle()
        gather.advance()
        weight_own = by_row(join_weight(mine, units, wide, gather.sent))
        gather.take(weight_own, 0, 1)
        gather.take(weight_own, 2)
        gather.settle()
        gather.advance()
        gather.take(weight_own, 3)
        gather.settle()
        gather.sent = ()
        gather.take(weight_own, 4)
        normed_all, projected = gather.filled
    else:
        weight_own = join_weight(mine, units, wide)
        released = after(cotangent, normed_all, weight_own)
        projected = jnp.dot(normed_all, weight_own, preferred_element_type=F32).astype(BF)
    cotangent_all = lax.all_gather(released, "dp", axis=0, tiled=True)
    carried = (jnp.zeros((wide, N), F32),)
    for begin, end in cuts(total // STRETCH, FRONT_PARTS):
        carried = run_forward(
            carried, begin, end - begin, projected, place, remain, px, pbc, pdt
        )
    _, zin, mixed, square, states = carried
    partial_out = jnp.dot(zin, out_weight_low, preferred_element_type=F32).astype(BF)
    summed_out = lax.psum_scatter(partial_out, "dp", scatter_dimension=0, tiled=True)
    g_out_low = lax.dot_general(
        cotangent_all, out_weight_low, (((1,), (1,)), ((), ())), preferred_element_type=F32
    )
    pull_part = jnp.sum(g_out_low * zin.astype(F32), axis=1)
    both = jnp.sum(lax.all_gather(jnp.stack([square[:, 0], pull_part]), "dp"), axis=0)
    scale = lax.rsqrt(both[0] / live + NORM_EPS)
    pull = scale * scale * scale / live * both[1]

    rows_in = (place, remain, mixed, g_out_low, scale[:, None], pull[:, None])
    carried = (
        jnp.zeros((wide, N), F32),
        jnp.zeros((16, wide), F32),
        jnp.zeros((16, 2 * N), F32),
        jnp.zeros((8, 128), F32),
    )
    for begin, end in reversed(cuts(total // STRETCH, BACK_PARTS)):
        carried = run_backward(
            carried, begin, end - begin, projected, rows_in, states, px, pbc, pdt
        )
    _, gx, gbc, gdt, g_projected, out_low = carried
    block_out = (
        inputs_f
        + summed_out.astype(F32)
        * lax.dynamic_slice_in_dim(scale, here * rows, rows, 0)[:, None]
    ).astype(BF)

    g_weight = lax.dot_general(
        g_projected, normed_all, (((0,), (0,)), ((), ())), preferred_element_type=F32
    ).astype(BF)
    g_heads = g_weight[2 * wide + 2 * N : 2 * wide + 2 * N + own_heads]
    g_shared = jnp.concatenate(
        [
            g_weight[2 * wide : 2 * wide + 2 * N],
            lax.dynamic_update_slice_in_dim(
                jnp.zeros((H, D), BF), g_heads, here * own_heads, 0
            ),
        ],
        axis=0,
    )
    g_both = jnp.stack([g_weight[:units], g_weight[wide : wide + units]])
    paired = lax.axis_size("width") == 2

    def to_owners(values):
        return lax.all_to_all(
            values.reshape(-1, dp, shard).transpose(1, 0, 2), "dp", 0, 0
        )

    def half(slot):
        return jnp.concatenate(
            [
                lax.dynamic_index_in_dim(g_both, slot, 0, False),
                lax.dynamic_slice_in_dim(g_shared, slot * (SHARED // 2), SHARED // 2, 0),
            ],
            axis=0,
        )

    inward = Scatter(g_projected, weight_own.T, g_weight)
    if paired:
        slot = lax.axis_index("width")
        g_kept = half(slot)
        g_got = other_width(half(1 - slot))
    inward.advance()
    g_weight_out = lax.dot_general(
        after(out_low, inward.sent),
        cotangent_all,
        (((0,), (0,)), ((), ())),
        preferred_element_type=F32,
    )[:units].astype(BF)
    inward.advance(g_weight_out)
    if paired:
        g_kept, g_got, _ = lax.optimization_barrier((g_kept, g_got, inward.sent))
        g_half = to_owners((g_kept.astype(F32) + g_got.astype(F32)).astype(BF))
        total_out = other_width(after(g_weight_out, inward.sent))
        inward.advance()
        inward.advance(total_out)
        total_out = g_weight_out.astype(F32) + total_out.astype(F32)
        g_half = after(g_half, inward.sent)
        g_shared = jnp.sum(g_half[:, units:].astype(F32), axis=0).astype(BF)
        g_half = g_half[:, :units]
        g_peer = other_width(g_half)
        g_apart = other_width(g_shared)
    else:
        inward.advance()
        inward.advance()
        total_out = width_sum(g_weight_out)
        g_pairs = width_sum(to_owners(g_both.reshape(-1, D)))
        g_gate, g_x = g_pairs[:, :units], g_pairs[:, units:]
        g_apart = lax.psum_scatter(
            g_shared.reshape(SHARED, dp, shard).transpose(1, 0, 2), "dp", scatter_dimension=0
        )
        g_apart = width_sum(g_apart)
    simple = paired and units % 128 == 0 and shard == 128
    step_float = step_count[0].astype(F32)
    new_out, mom_out, sec_out = adamw_step(
        weight_out,
        moment_out,
        second_out,
        after(total_out, inward.sent),
        MATRIX_RATE,
        MATRIX_DECAY,
        step_float,
    )
    if simple:
        base = (1.0 - jnp.power(BETA_ONE, step_float)).reshape(1, 1)
        own = (weight_in.T, moment_in.T, second_in.T)
        size = 4 * units
        blocks = E // size
        moved = adamw_rows(base, own, after(g_half, inward.sent), slot * blocks, size, ())
        g_normed = inward.finish(new_out, g_peer, g_apart, moved)
    elif paired:
        g_normed = inward.finish(new_out, g_peer, g_apart)
    else:
        g_normed = inward.finish(new_out)
    if paired:
        g_apart = jnp.concatenate(in_order(g_shared, g_apart), axis=0)
    if simple:
        moved = adamw_rows(base, own, g_peer, (1 - slot) * blocks, size, moved)
        moved = adamw_rows(base, own, g_apart, 2 * E // H, H, moved)
        new_in, mom_in, sec_in, low_in = (result.T for result in moved)
    else:
        if paired:
            g_gate, g_x = in_order(g_half, g_peer)
        total_in = jnp.concatenate(
            [
                g_gate.transpose(2, 0, 1).reshape(shard, E),
                g_x.transpose(2, 0, 1).reshape(shard, E),
                g_apart.T,
            ],
            axis=1,
        ).astype(F32)
        new_in, mom_in, sec_in = adamw_step(
            weight_in, moment_in, second_in, total_in, MATRIX_RATE, MATRIX_DECAY, step_float
        )
        low_in = new_in.astype(BF)

    ratio = root * g_in
    lean = jnp.sum(g_in * g_normed * inputs_f, axis=1, keepdims=True)
    g_inputs = ratio * g_normed - inputs_f * (root * root * root / D * lean)
    grad_tokens = (cotangent.astype(F32) + g_inputs).astype(BF)
    g_g_in = jnp.sum(g_normed * inputs_f * root, axis=0)

    def placed(part, size):
        spots = jnp.zeros(part.shape[:-1] + (size,), F32)
        return lax.dynamic_update_slice_in_dim(
            spots, part, here * part.shape[-1], part.ndim - 1
        )

    conv_part = jnp.concatenate([placed(gx[:5, :units], E), gbc[:5]], axis=1)
    early = jnp.concatenate(
        [
            placed(gx[6, :units], E),
            conv_part.reshape(-1),
            placed(gdt[1, :own_heads], H),
            placed(gdt[0, :own_heads], H),
            placed(jnp.sum(gx[5, :units].reshape(own_heads, P_SIZE), axis=1), H),
        ]
    )
    total_small = tree_sum(jnp.concatenate([g_g_in, early]))
    rate_table, decay_table = small_table()
    new_small, mom_small, sec_small = adamw_step(
        small_params, moment_small, second_small, total_small, rate_table, decay_table, step_float
    )
    return (
        block_out,
        grad_tokens,
        new_in,
        mom_in,
        sec_in,
        low_in,
        new_out,
        mom_out,
        sec_out,
        new_out.astype(BF),
        new_small,
        mom_small,
        sec_small,
    )


def solution(mesh):
    return jax.shard_map(
        per_device,
        mesh=mesh,
        in_specs=(
            P(("width", "dp"), None),
            P(("width", "dp"), None),
            P("width", None),
            P("width"),
            P(),
            P("dp", None),
            P("dp", None),
            P("dp", None),
            P("dp", None),
            P("dp", None),
            P("dp", None),
            P(),
            P(),
            P(),
        ),
        out_specs=(
            P(("width", "dp"), None),
            P(("width", "dp"), None),
            P("dp", None),
            P("dp", None),
            P("dp", None),
            P("dp", None),
            P("dp", None),
            P("dp", None),
            P("dp", None),
            P("dp", None),
            P(),
            P(),
            P(),
        ),
        check_vma=False,
    )
```

```python
from functools import partial

import jax
import jax.numpy as jnp
from jax import lax
from jax.experimental import pallas as pl
from jax.experimental.layout import Layout, with_layout_constraint
from jax.experimental.pallas import tpu as pltpu
from jax.sharding import PartitionSpec as P

D = 2048
E = 4096
H = 64
P_SIZE = 64
N = 128
KCONV = 4
STRETCH = 256
K = 4352

NORM_EPS = 1e-05
ADAM_EPS = 1e-08
BETA_ONE = 0.5
BETA_TWO = 0.5
MATRIX_RATE = 0.02
MATRIX_DECAY = 0.1
PRECISE = lax.Precision.HIGHEST
BF = jnp.bfloat16
F32 = jnp.float32
LOW = -1e30
SHARED = 2 * N + H
BACK_PARTS = 1
FRONT_PARTS = 1


def small_table():
    rate_table = jnp.concatenate(
        [
            jnp.full((D,), 0.3, F32),
            jnp.full((E,), 0.3, F32),
            jnp.full((KCONV * K,), 0.2, F32),
            jnp.full((K,), 0.2, F32),
            jnp.full((H,), 0.3, F32),
            jnp.full((H,), 1.0, F32),
            jnp.full((H,), 0.3, F32),
        ]
    )
    decay_table = jnp.concatenate(
        [
            jnp.zeros((D + E,), F32),
            jnp.full((KCONV * K,), 0.1, F32),
            jnp.zeros((K + 3 * H,), F32),
        ]
    )
    return (rate_table, decay_table)


def unpack(small_params):
    offset = D + E
    conv_w = small_params[offset : offset + KCONV * K].reshape(KCONV, K)
    offset = offset + KCONV * K
    conv_b = small_params[offset : offset + K]
    offset = offset + K
    a_log = small_params[offset : offset + H]
    dt_bias = small_params[offset + H : offset + 2 * H]
    d_skip = small_params[offset + 2 * H : offset + 3 * H]
    return (small_params[:D], small_params[D : D + E], conv_w, conv_b, a_log, dt_bias, d_skip)


def row_places(lengths_row, row_count):
    seq_ends = jnp.cumsum(lengths_row)
    at = jnp.arange(row_count, dtype=jnp.int32)
    passed = seq_ends[None, :] <= at[:, None]
    begin = jnp.max(jnp.where(passed, seq_ends[None, :], 0), axis=1)
    finish = jnp.min(jnp.where(passed, row_count, seq_ends[None, :]), axis=1)
    return (at - begin, finish - 1 - at)


def adamw_step(weight, moment, second, grad, rate, decay, step_float):
    first_new = BETA_ONE * moment + (1.0 - BETA_ONE) * grad
    second_new = BETA_TWO * second + (1.0 - BETA_TWO) * grad * grad
    first_hat = first_new / (1.0 - jnp.power(BETA_ONE, step_float))
    second_hat = second_new / (1.0 - jnp.power(BETA_TWO, step_float))
    return (
        weight - rate * (first_hat / (jnp.sqrt(second_hat) + ADAM_EPS) + decay * weight),
        first_new,
        second_new,
    )


def sigmoid(v):
    return 1.0 / (1.0 + jnp.exp(-v))


def dot(a, b, dims):
    return lax.dot_general(
        a.astype(BF), b.astype(BF), (dims, ((), ())), preferred_element_type=F32
    )


def split(values, count):
    parts = []
    for _ in range(count):
        part = values.astype(BF)
        values = values - part.astype(F32)
        parts.append(part)
    return parts


def head_lanes(heads):
    row = lax.broadcasted_iota(jnp.int32, (128, heads * P_SIZE), 0)
    lane = lax.broadcasted_iota(jnp.int32, (128, heads * P_SIZE), 1)
    return jnp.where(lane // P_SIZE == row, 1.0, 0.0).astype(BF)


def spread(columns, lanes):
    return sum(dot(part, lanes, ((1,), (0,))) for part in split(columns, 2))


def head_sums(values, lanes):
    return sum(dot(part, lanes, ((1,), (1,))) for part in split(values, 2))


def running(mask, values):
    mask = jnp.where(mask, 1.0, 0.0).astype(BF)
    return sum(dot(mask, part, ((1,), (0,))) for part in split(values, 3))


def convolve(buffer, weights, bias, place):
    total = bias + jnp.zeros((STRETCH, buffer.shape[1]), F32)
    for tap in range(KCONV):
        back = KCONV - 1 - tap
        rows = buffer[8 - back : 8 - back + STRETCH, :]
        if back:
            rows = jnp.where(place >= back, rows, 0.0)
        total = total + weights[tap : tap + 1, :] * rows
    return total


def block_terms(place, remain, dt_in, pdt):
    row = lax.broadcasted_iota(jnp.int32, (STRETCH, STRETCH), 0)
    col = lax.broadcasted_iota(jnp.int32, (STRETCH, STRETCH), 1)
    at = lax.broadcasted_iota(jnp.int32, (STRETCH, 1), 0)
    biased = dt_in + pdt[0:1, :]
    step = jnp.maximum(biased, 0.0) + jnp.log1p(jnp.exp(-jnp.abs(biased)))
    log_decay = step * pdt[1:2, :]
    cum = running(col <= row, log_decay)
    cum_t = jnp.transpose(cum)
    carrying = jnp.where(place >= at + 1, jnp.exp(cum), 0.0)
    tail_ok = remain >= STRETCH - 1 - at
    tail = jnp.exp(jnp.where(tail_ok, cum[STRETCH - 1 : STRETCH, :] - cum, LOW))
    return row, col, biased, step, log_decay, cum, cum_t, carrying, tail


def forward_kernel(
    heads,
    gate_ref,
    x_ref,
    bc_ref,
    dt_ref,
    xprev_ref,
    bcprev_ref,
    place_ref,
    remain_ref,
    px_ref,
    pbc_ref,
    pdt_ref,
    state_in,
    *rest,
):
    zin_ref, mixed_ref, square_ref, states_ref, state, xbuf, bcbuf = rest[-7:]

    @pl.when(pl.program_id(0) == 0)
    def _():
        state[...] = state_in[...]

    xbuf[0:8, :] = xprev_ref[8:16, :].astype(F32)
    bcbuf[0:8, :] = bcprev_ref[8:16, :].astype(F32)
    place = place_ref[...]
    remain = remain_ref[...]
    xbuf[8 : 8 + STRETCH, :] = x_ref[...].astype(F32)
    bcbuf[8 : 8 + STRETCH, :] = bc_ref[...].astype(F32)
    conv_x = convolve(xbuf, px_ref[0:4, :], px_ref[4:5, :], place)
    conv_bc = convolve(bcbuf, pbc_ref[0:4, :], pbc_ref[4:5, :], place)
    x = conv_x * sigmoid(conv_x) * px_ref[7:8, :]
    act_bc = conv_bc * sigmoid(conv_bc)
    b_low = act_bc[:, :N].astype(BF)
    c_low = act_bc[:, N:].astype(BF)
    row, col, _, step, _, cum, cum_t, carrying, tail = block_terms(
        place, remain, dt_ref[...].astype(F32), pdt_ref[...]
    )
    visible = (col <= row) & (row - col <= place)
    lanes = head_lanes(heads)
    scaled = x * spread(step, lanes)
    scaled_low = scaled.astype(BF)
    gram = dot(c_low, b_low, ((1,), (1,)))
    old = state[...]
    states_ref[0] = old
    across = dot(c_low, old, ((1,), (1,))) * spread(carrying, lanes)
    parts = []
    for h in range(heads):
        decay = jnp.exp(jnp.where(visible, cum[:, h : h + 1] - cum_t[h : h + 1, :], LOW))
        parts.append(
            dot(gram * decay, scaled_low[:, h * P_SIZE : (h + 1) * P_SIZE], ((1,), (0,)))
        )
    mixed = jnp.concatenate(parts, axis=1) + across + px_ref[5:6, :] * x
    fresh = dot(scaled * spread(tail, lanes), b_low, ((0,), (0,)))
    for h in range(heads):
        rows = slice(h * P_SIZE, (h + 1) * P_SIZE)
        state[rows, :] = (
            old[rows, :] * carrying[STRETCH - 1 : STRETCH, h : h + 1] + fresh[rows, :]
        )
    gate = gate_ref[...].astype(F32)
    gated = mixed * (gate * sigmoid(gate))
    mixed_ref[...] = mixed
    zin_ref[...] = (gated * px_ref[6:7, :]).astype(BF)
    ones = jnp.ones((8, gated.shape[1]), BF)
    square_ref[...] = sum(dot(ones, part, ((1,), (1,))) for part in split(gated * gated, 2))


def backward_kernel(
    heads,
    gate_ref,
    x_ref,
    bc_ref,
    dt_ref,
    xprev_ref,
    bcprev_ref,
    place_ref,
    remain_ref,
    mixed_ref,
    gout_ref,
    sums_ref,
    live_ref,
    states_ref,
    px_ref,
    pbc_ref,
    pdt_ref,
    gstate_in,
    gx_in,
    gbc_in,
    gdt_in,
    *rest,
):
    gp_ref, low_ref, gstate, gx_ref, gbc_ref, gdt_ref, xbuf, bcbuf, gxbuf, gbcbuf = rest[-10:]
    width = x_ref.shape[1]

    @pl.when(pl.program_id(0) == 0)
    def _():
        gstate[...] = gstate_in[...]
        gxbuf[STRETCH : STRETCH + 8, :] = gx_in[8:16, :]
        gbcbuf[STRETCH : STRETCH + 8, :] = gbc_in[8:16, :]
        gx_ref[...] = gx_in[...]
        gbc_ref[...] = gbc_in[...]
        gdt_ref[...] = gdt_in[...]

    place = place_ref[...]
    remain = remain_ref[...]
    xbuf[0:8, :] = xprev_ref[8:16, :].astype(F32)
    bcbuf[0:8, :] = bcprev_ref[8:16, :].astype(F32)
    xbuf[8 : 8 + STRETCH, :] = x_ref[...].astype(F32)
    bcbuf[8 : 8 + STRETCH, :] = bc_ref[...].astype(F32)
    conv_x = convolve(xbuf, px_ref[0:4, :], px_ref[4:5, :], place)
    conv_bc = convolve(bcbuf, pbc_ref[0:4, :], pbc_ref[4:5, :], place)
    sig_x = sigmoid(conv_x)
    sig_bc = sigmoid(conv_bc)
    x = conv_x * sig_x * px_ref[7:8, :]
    act_bc = conv_bc * sig_bc
    b_low = act_bc[:, :N].astype(BF)
    c_low = act_bc[:, N:].astype(BF)
    row, col, biased, step, log_decay, cum, cum_t, carrying, tail = block_terms(
        place, remain, dt_ref[...].astype(F32), pdt_ref[...]
    )
    visible = (col >= row) & (col - row <= remain)
    lanes = head_lanes(heads)

    gate = gate_ref[...].astype(F32)
    sig = sigmoid(gate)
    silu = gate * sig
    mixed = mixed_ref[...]
    gated = mixed * silu
    g_out = px_ref[6:7, :]
    sums = jnp.transpose(
        jnp.concatenate([sums_ref[...], jnp.zeros((120, STRETCH), F32)], axis=0)
    )
    live = live_ref[0, 0]
    scale = lax.rsqrt(sums[:, 0:1] / live + NORM_EPS)
    pull = scale * scale * scale / live * sums[:, 1:2]
    upstream = gout_ref[...]
    low_ref[...] = (gated * scale * g_out).astype(BF)
    g_gated = scale * g_out * upstream - gated * pull
    g_mixed = g_gated * silu
    gp_ref[:, 0:width] = (g_gated * mixed * (sig * (1.0 + gate * (1.0 - sig)))).astype(BF)

    step_wide = spread(step, lanes)
    carry_wide = spread(carrying, lanes)
    tail_wide = spread(tail, lanes)
    scaled = x * step_wide
    scaled_low = scaled.astype(BF)
    g_low = g_mixed.astype(BF)
    old = states_ref[0]
    g_new = gstate[...]
    old_low = old.astype(BF)
    g_new_low = g_new.astype(BF)
    gram = dot(b_low, c_low, ((1,), (1,)))
    across = dot(c_low, old_low, ((1,), (1,)))
    returned = dot(b_low, g_new_low, ((1,), (1,))) * tail_wide
    g_carried = g_mixed * carry_wide
    g_carried_low = g_carried.astype(BF)
    tailed_low = (scaled * tail_wide).astype(BF)

    g_gram = jnp.zeros((STRETCH, STRETCH), F32)
    lane = lax.broadcasted_iota(jnp.int32, (STRETCH, 128), 1)
    sources = jnp.zeros((STRETCH, 128), F32)
    target_rows = []
    parts = []
    for h in range(heads):
        cols = slice(h * P_SIZE, (h + 1) * P_SIZE)
        decay = jnp.exp(jnp.where(visible, cum_t[h : h + 1, :] - cum[:, h : h + 1], LOW))
        mixing = gram * decay
        g_mixing = dot(scaled_low[:, cols], g_low[:, cols], ((1,), (1,)))
        parts.append(dot(mixing, g_low[:, cols], ((1,), (0,))))
        g_gram = g_gram + g_mixing * decay
        both = g_mixing * mixing
        sources = jnp.where(lane == h, jnp.sum(both, axis=1, keepdims=True), sources)
        target_rows.append(jnp.sum(both, axis=0, keepdims=True))
    target_rows.append(jnp.zeros((128 - heads, STRETCH), F32))
    targets = jnp.transpose(jnp.concatenate(target_rows, axis=0))
    g_scaled = jnp.concatenate(parts, axis=1) + returned
    into = head_sums(g_carried * across, lanes)
    outof = head_sums(scaled * returned, lanes)
    state_dot = jnp.zeros((1, 128), F32)
    lane_one = lax.broadcasted_iota(jnp.int32, (1, 128), 1)
    product = g_new * old
    for h in range(heads):
        total = jnp.sum(
            jnp.sum(product[h * P_SIZE : (h + 1) * P_SIZE, :], axis=0, keepdims=True),
            axis=1,
            keepdims=True,
        )
        state_dot = jnp.where(lane_one == h, total, state_dot)
    g_c = dot(g_gram, b_low, ((0,), (0,))) + dot(g_carried_low, old_low, ((1,), (0,)))
    g_b = dot(g_gram, c_low, ((1,), (0,))) + dot(tailed_low, g_new_low, ((1,), (0,)))
    g_fresh = dot(g_carried_low, c_low, ((0,), (0,)))
    for h in range(heads):
        rows = slice(h * P_SIZE, (h + 1) * P_SIZE)
        gstate[rows, :] = (
            g_new[rows, :] * carrying[STRETCH - 1 : STRETCH, h : h + 1] + g_fresh[rows, :]
        )
    g_cum = targets - sources + into - outof
    g_decay = running(col >= row, g_cum) + (
        jnp.sum(outof, axis=0, keepdims=True)
        + carrying[STRETCH - 1 : STRETCH, :] * state_dot
    )
    g_step = head_sums(x * g_scaled, lanes) + g_decay * pdt_ref[1:2, :]
    g_dt = g_step * sigmoid(biased)
    gdt_ref[0:1, :] += jnp.sum(g_dt, axis=0, keepdims=True)
    gdt_ref[1:2, :] += jnp.sum(g_decay * log_decay, axis=0, keepdims=True)
    g_x = px_ref[5:6, :] * g_mixed + step_wide * g_scaled
    g_conv_x = g_x * px_ref[7:8, :] * (sig_x * (1.0 + conv_x * (1.0 - sig_x)))
    g_act = jnp.concatenate([g_b, g_c], axis=1)
    g_conv_bc = g_act * (sig_bc * (1.0 + conv_bc * (1.0 - sig_bc)))
    gx_ref[4:5, :] += jnp.sum(g_conv_x, axis=0, keepdims=True)
    gx_ref[5:6, :] += jnp.sum(g_mixed * x, axis=0, keepdims=True)
    gx_ref[6:7, :] += jnp.sum(upstream * gated * scale, axis=0, keepdims=True)
    gbc_ref[4:5, :] += jnp.sum(g_conv_bc, axis=0, keepdims=True)
    gxbuf[0:STRETCH, :] = g_conv_x
    gbcbuf[0:STRETCH, :] = g_conv_bc
    g_in_x = jnp.zeros((STRETCH, width), F32)
    g_in_bc = jnp.zeros((STRETCH, 2 * N), F32)
    for tap in range(KCONV):
        back = KCONV - 1 - tap
        rows_x = xbuf[8 - back : 8 - back + STRETCH, :]
        rows_bc = bcbuf[8 - back : 8 - back + STRETCH, :]
        later_x = gxbuf[back : back + STRETCH, :]
        later_bc = gbcbuf[back : back + STRETCH, :]
        if back:
            rows_x = jnp.where(place >= back, rows_x, 0.0)
            rows_bc = jnp.where(place >= back, rows_bc, 0.0)
            later_x = jnp.where(remain >= back, later_x, 0.0)
            later_bc = jnp.where(remain >= back, later_bc, 0.0)
        gx_ref[tap : tap + 1, :] += jnp.sum(g_conv_x * rows_x, axis=0, keepdims=True)
        gbc_ref[tap : tap + 1, :] += jnp.sum(g_conv_bc * rows_bc, axis=0, keepdims=True)
        g_in_x = g_in_x + px_ref[tap : tap + 1, :] * later_x
        g_in_bc = g_in_bc + pbc_ref[tap : tap + 1, :] * later_bc
    gxbuf[STRETCH : STRETCH + 8, :] = g_conv_x[0:8, :]
    gbcbuf[STRETCH : STRETCH + 8, :] = g_conv_bc[0:8, :]
    gx_ref[8:16, :] = g_conv_x[0:8, :]
    gbc_ref[8:16, :] = g_conv_bc[0:8, :]
    gp_ref[:, width : 2 * width] = g_in_x.astype(BF)
    gp_ref[:, 2 * width : 2 * width + 2 * N] = g_in_bc.astype(BF)
    gp_ref[:, 2 * width + 2 * N : 2 * width + 2 * N + 128] = g_dt.astype(BF)


def run_forward(carried, first, count, projected, place, remain, px, pbc, pdt):
    total = projected.shape[0]
    width = px.shape[1]
    heads = width // P_SIZE
    row_spec = lambda w, c: pl.BlockSpec((STRETCH, w), lambda i: (first + i, c))
    prev_spec = lambda w, c: pl.BlockSpec(
        (16, w), lambda i: (jnp.maximum((first + i) * (STRETCH // 16) - 1, 0), c)
    )
    whole = lambda a: pl.BlockSpec(a.shape, lambda i: (0, 0))
    state = carried[0]
    filled = tuple(carried[1:])
    results = pl.pallas_call(
        partial(forward_kernel, heads),
        grid=(count,),
        in_specs=[
            row_spec(width, 0),
            row_spec(width, 1),
            row_spec(2 * N, width // N),
            row_spec(128, (2 * width + 2 * N) // 128),
            prev_spec(width, 1),
            prev_spec(2 * N, width // N),
            row_spec(1, 0),
            row_spec(1, 0),
            whole(px),
            whole(pbc),
            whole(pdt),
            whole(state),
        ]
        + [pl.BlockSpec(memory_space=pl.ANY)] * len(filled),
        out_specs=[
            row_spec(width, 0),
            row_spec(width, 0),
            pl.BlockSpec((8, STRETCH), lambda i: (0, first + i)),
            pl.BlockSpec((1, width, N), lambda i: (first + i, 0, 0)),
            whole(state),
        ],
        out_shape=[
            jax.ShapeDtypeStruct((total, width), BF),
            jax.ShapeDtypeStruct((total, width), F32),
            jax.ShapeDtypeStruct((8, total), F32),
            jax.ShapeDtypeStruct((total // STRETCH, width, N), F32),
            jax.ShapeDtypeStruct((width, N), F32),
        ],
        scratch_shapes=[
            pltpu.VMEM((STRETCH + 8, width), F32),
            pltpu.VMEM((STRETCH + 8, 2 * N), F32),
        ],
        input_output_aliases={12: 0, 13: 1, 14: 2, 15: 3} if filled else {},
        cost_estimate=pl.CostEstimate(
            flops=count * STRETCH * 256 * 20000,
            bytes_accessed=count * STRETCH * 5000,
            transcendentals=count * STRETCH * 1500,
        ),
        name="scan_forward",
    )(*((projected,) * 6 + (place, remain, px, pbc, pdt, state) + filled))
    return (results[4],) + tuple(results[:4])


def run_backward(carried, first, count, projected, rows_in, states, px, pbc, pdt):
    total = projected.shape[0]
    width = px.shape[1]
    heads = width // P_SIZE
    columns = projected.shape[1]
    rev = lambda i: first + count - 1 - i
    row_spec = lambda w, c: pl.BlockSpec((STRETCH, w), lambda i: (rev(i), c))
    prev_spec = lambda w, c: pl.BlockSpec(
        (16, w), lambda i: (jnp.maximum(rev(i) * (STRETCH // 16) - 1, 0), c)
    )
    whole = lambda a: pl.BlockSpec(a.shape, lambda i: (0, 0))
    fixed = lambda r, w: pl.BlockSpec((r, w), lambda i: (0, 0))
    place, remain, mixed, g_out_low, sums, live = rows_in
    gstate, gx, gbc, gdt = carried[:4]
    filled = tuple(carried[4:])
    operands = (
        (projected,) * 6
        + (place, remain, mixed, g_out_low, sums, live, states, px, pbc, pdt)
        + (gstate, gx, gbc, gdt)
        + filled
    )
    results = pl.pallas_call(
        partial(backward_kernel, heads),
        grid=(count,),
        in_specs=[
            row_spec(width, 0),
            row_spec(width, 1),
            row_spec(2 * N, width // N),
            row_spec(128, (2 * width + 2 * N) // 128),
            prev_spec(width, 1),
            prev_spec(2 * N, width // N),
            row_spec(1, 0),
            row_spec(1, 0),
            row_spec(width, 0),
            row_spec(width, 0),
            pl.BlockSpec((8, STRETCH), lambda i: (0, rev(i))),
            pl.BlockSpec(memory_space=pltpu.SMEM),
            pl.BlockSpec((1, width, N), lambda i: (rev(i), 0, 0)),
            whole(px),
            whole(pbc),
            whole(pdt),
            whole(gstate),
            whole(gx),
            whole(gbc),
            whole(gdt),
        ]
        + [pl.BlockSpec(memory_space=pl.ANY)] * len(filled),
        out_specs=[
            row_spec(columns, 0),
            row_spec(width, 0),
            fixed(width, N),
            fixed(16, width),
            fixed(16, 2 * N),
            fixed(8, 128),
        ],
        out_shape=[
            jax.ShapeDtypeStruct((total, columns), BF),
            jax.ShapeDtypeStruct((total, width), BF),
            jax.ShapeDtypeStruct((width, N), F32),
            jax.ShapeDtypeStruct((16, width), F32),
            jax.ShapeDtypeStruct((16, 2 * N), F32),
            jax.ShapeDtypeStruct((8, 128), F32),
        ],
        scratch_shapes=[
            pltpu.VMEM((STRETCH + 8, width), F32),
            pltpu.VMEM((STRETCH + 8, 2 * N), F32),
            pltpu.VMEM((STRETCH + 8, width), F32),
            pltpu.VMEM((STRETCH + 8, 2 * N), F32),
        ],
        input_output_aliases={20: 0, 21: 1} if filled else {},
        cost_estimate=pl.CostEstimate(
            flops=count * STRETCH * 256 * 40000,
            bytes_accessed=count * STRETCH * 8000,
            transcendentals=count * STRETCH * 2000,
        ),
        name="scan_backward",
    )(*operands)
    return tuple(results[2:]) + tuple(results[:2])


def after(value, *others):
    return lax.optimization_barrier((value, others))[0]


def by_row(values):
    return with_layout_constraint(values, Layout(major_to_minor=(0, 1)))


def cuts(count, parts):
    edges = [count * i // parts for i in range(parts + 1)]
    return list(zip(edges[:-1], edges[1:]))


def ring_chips():
    return [(z * 2 + x) for x, z in [(0, 0), (0, 1), (0, 2), (0, 3), (1, 3), (1, 2), (1, 1), (1, 0)]]


def hop(values, steps):
    chips = ring_chips()
    count = len(chips)
    pairs = [
        (2 * chips[p] + core, 2 * chips[(p + steps) % count] + core)
        for p in range(count)
        for core in (0, 1)
    ]
    return lax.ppermute(values, "dp", pairs)


def swap(values):
    return lax.ppermute(values, "dp", [(i, i ^ 1) for i in range(lax.axis_size("dp"))])


def ring_place():
    here = lax.axis_index("dp")
    core = here % 2
    chip = here // 2
    spot = jnp.where(chip % 2 == 0, chip // 2, 7 - chip // 2)
    return core, spot


def ring_chip(spot):
    spot = spot % 8
    return jnp.where(spot < 4, spot * 2, (7 - spot) * 2 + 1)


def absorb_kernel(count, by_rows, starts_ref, *refs):
    pieces = refs[:count]
    weight_ref = refs[count]
    kept_ref, product_ref, held = refs[-3:]
    for j in range(count):

        @pl.when(pl.program_id(0) == j)
        def _(j=j):
            held[...] = pieces[j][...]

    values = held[...]
    kept_ref[...] = values
    product_ref[...] = lax.dot_general(
        values,
        weight_ref[...],
        (((1,), (1 if by_rows else 0,)), ((), ())),
        preferred_element_type=F32,
    ).astype(product_ref.dtype)


def absorb(pieces, starts, total, filled, weight, by_rows, kind):
    size, depth = pieces[0].shape
    columns = weight.shape[0 if by_rows else 1]
    count = len(pieces)
    whole = lambda a: pl.BlockSpec(a.shape, lambda i, at: (0, 0))
    placed = lambda w: pl.BlockSpec((size, w), lambda i, at: (at[i], 0))
    return pl.pallas_call(
        partial(absorb_kernel, count, by_rows),
        grid_spec=pltpu.PrefetchScalarGridSpec(
            num_scalar_prefetch=1,
            grid=(count,),
            in_specs=[whole(piece) for piece in pieces]
            + [whole(weight)]
            + [pl.BlockSpec(memory_space=pl.ANY)] * len(filled),
            out_specs=[placed(depth), placed(columns)],
            scratch_shapes=[pltpu.VMEM((size, depth), BF)],
        ),
        out_shape=[
            jax.ShapeDtypeStruct((total, depth), BF),
            jax.ShapeDtypeStruct((total, columns), kind),
        ],
        input_output_aliases={count + 2: 0, count + 3: 1} if filled else {},
        cost_estimate=pl.CostEstimate(
            flops=40 * count * size * depth * columns,
            bytes_accessed=4 * count * size * depth + 2 * depth * columns,
            transcendentals=0,
        ),
        name="absorb_rows",
    )(starts, *pieces, weight, *filled)


class Gather:
    def __init__(self, values):
        self.rows = values.shape[0]
        self.core, self.spot = ring_place()
        self.last = (values, values)
        self.arrived = [((values, ring_chip(self.spot), 0),)]
        self.swapped = []
        self.sent = self.filled = ()

    def settle(self, *others):
        self.last, self.filled, _ = lax.optimization_barrier((self.last, self.filled, others))
        step = len(self.swapped)
        if step:
            offset = self.rows // 2 if step == 4 else 0
            self.arrived.append(
                (
                    (self.last[0], ring_chip(self.spot - step), 0),
                    (self.last[1], ring_chip(self.spot + step), offset),
                )
            )
        self.swapped.append([by_row(swap(by_row(piece))) for piece, _, _ in self.arrived[-1]])

    def advance(self):
        ahead, behind = self.last
        if len(self.swapped) == 4:
            ahead, behind = ahead[: self.rows // 2], behind[self.rows // 2 :]
        self.sent, self.swapped[-1] = lax.optimization_barrier(
            ((ahead, behind), self.swapped[-1])
        )
        ahead, behind = self.sent
        self.last = (by_row(hop(by_row(ahead), 1)), by_row(hop(by_row(behind), -1)))

    def take(self, weight, *hops):
        pieces, starts = [], []
        for k in hops:
            for (piece, chip, offset), other in zip(self.arrived[k], self.swapped[k]):
                for part, core in ((piece, self.core), (other, 1 - self.core)):
                    pieces.append(part)
                    starts.append(((2 * chip + core) * self.rows + offset) // piece.shape[0])
        pieces, _ = lax.optimization_barrier((pieces, self.sent))
        self.filled = tuple(
            absorb(
                pieces,
                jnp.stack(starts).astype(jnp.int32),
                16 * self.rows,
                self.filled,
                weight,
                False,
                BF,
            )
        )


class RingSum:
    def __init__(self, chunk, rows):
        self.chunk = chunk
        self.mid = rows // 2
        self.step = 4
        self.last = self.sent = ()
        self.ready = (chunk(4, ()),)

    def settle(self, others):
        self.last, self.ready, _ = lax.optimization_barrier((self.last, self.ready, others))

    def advance(self, *others):
        self.settle(others)
        mid = self.mid
        if self.step == 4:
            up, down = self.ready[0][:mid], self.ready[0][mid:]
        else:
            up, down = (value.astype(F32) for value in self.last)
            first, second = self.ready
            if self.step == 3:
                up = jnp.concatenate([first[:mid] + up, first[mid:]], axis=0)
                down = jnp.concatenate([second[:mid], second[mid:] + down], axis=0)
            else:
                up, down = first + up, second + down
        self.sent = lax.optimization_barrier((up.astype(BF), down.astype(BF)))
        up, down = self.sent
        self.last = (by_row(hop(by_row(up), 1)), by_row(hop(by_row(down), -1)))
        self.step -= 1
        self.ready = tuple(
            self.chunk(steps, self.sent)
            for steps in sorted({self.step, -self.step}, reverse=True)
        )

    def finish(self, others):
        self.settle(others)
        return self.ready[0] + self.last[0].astype(F32) + self.last[1].astype(F32)


def column_halves(weight):
    if lax.axis_size("dp") != 16:
        return ()
    core = lax.axis_index("dp") % 2
    half = weight.shape[1] // 2
    take = lambda c: lax.dynamic_slice_in_dim(weight, c * half, half, 1)
    return lax.optimization_barrier((take(core), swap(take(1 - core))))


class Scatter:
    def __init__(self, left, right, halves, *gate):
        self.ring = lax.axis_size("dp") == 16
        self.last = self.sent = ()
        if not self.ring:
            full = jnp.dot(left, right, preferred_element_type=F32).astype(BF)
            self.done = lax.psum_scatter(full, "dp", scatter_dimension=0, tiled=True).astype(F32)
            return
        self.core, spot = ring_place()
        sides = ((left, halves[0]), (swap(left), halves[1]))
        sides = lax.optimization_barrier((sides, gate))[0]
        self.rows = rows = left.shape[0] // 8

        def chunk(steps, deps):
            start = ring_chip(spot + steps) * rows
            return by_row(
                sum(
                    jnp.dot(
                        lax.dynamic_slice_in_dim(after(side, deps), start, rows, 0),
                        weight,
                        preferred_element_type=F32,
                    )
                    for side, weight in sides
                )
            )

        self.sum = RingSum(chunk, rows)

    def advance(self, *others):
        if self.ring:
            self.sum.advance(*others)
            self.last, self.sent = self.sum.last, self.sum.sent

    def ready(self):
        return self.sum.ready if self.ring else ()

    def finish(self, *others):
        if not self.ring:
            return self.done
        done = self.sum.finish(others)
        own = self.rows // 2
        kept = lax.dynamic_slice_in_dim(done, self.core * own, own, 0)
        got = swap(lax.dynamic_slice_in_dim(done, (1 - self.core) * own, own, 0))
        first = self.core == 0
        return jnp.concatenate(
            [jnp.where(first, kept, got), jnp.where(first, got, kept)], axis=1
        )


def other_width(values):
    return lax.ppermute(values, "width", [(0, 1), (1, 0)])


def in_order(mine, other):
    first = lax.axis_index("width") == 0
    return jnp.where(first, mine, other), jnp.where(first, other, mine)


def weight_halves(weight_low, units):
    dp = lax.axis_size("dp")
    heads = weight_low[: 2 * E].reshape(2, dp, units, weight_low.shape[1])
    common = weight_low[2 * E :]
    if lax.axis_size("width") == 2:
        slot = lax.axis_index("width")
        heads = lax.dynamic_slice_in_dim(heads, slot, 1, 0)
        common = lax.dynamic_slice_in_dim(common, slot * (SHARED // 2), SHARED // 2, 0)
    return jnp.concatenate(
        [
            heads.transpose(1, 0, 2, 3).reshape(dp, -1, heads.shape[3]),
            jnp.broadcast_to(common[None], (dp,) + common.shape),
        ],
        axis=1,
    )


def join_weight(mine, units, wide, *gate):
    own_heads = units // P_SIZE
    if lax.axis_size("width") == 2:
        other = after(other_width(mine), gate)
        first, second = in_order(mine, other)
        gate_rows, x_rows = first[:units], second[:units]
        shared = jnp.concatenate([first[units:], second[units:]], axis=0)
    else:
        gate_rows, x_rows, shared = mine[:units], mine[units : 2 * units], mine[2 * units :]
    own_dt = lax.dynamic_slice_in_dim(
        shared, 2 * N + lax.axis_index("dp") * own_heads, own_heads, 0
    )
    return jnp.concatenate(
        [
            pad_to(gate_rows, wide, 0),
            pad_to(x_rows, wide, 0),
            shared[: 2 * N],
            pad_to(own_dt, 128, 0),
        ],
        axis=0,
    ).T


def adamw_kernel(first_ref, base_ref, weight_ref, moment_ref, second_ref, grad_ref, *refs):
    new_ref, first_moment_ref, squares_ref, low_ref = refs[-4:]
    grad = grad_ref[...].astype(F32).reshape(weight_ref.shape)
    base = base_ref[0, 0]
    weight = weight_ref[...]
    first = BETA_ONE * moment_ref[...] + (1.0 - BETA_ONE) * grad
    squares = BETA_TWO * second_ref[...] + (1.0 - BETA_TWO) * grad * grad
    new = weight - MATRIX_RATE * (
        (first / base) / (jnp.sqrt(squares / base) + ADAM_EPS) + MATRIX_DECAY * weight
    )
    new_ref[...] = new
    first_moment_ref[...] = first
    squares_ref[...] = squares
    low_ref[...] = new.astype(BF)


def adamw_rows(base, state, grad, first, size, filled):
    weight = state[0]
    columns = weight.shape[1]
    spec = pl.BlockSpec((size, columns), lambda i, at: (at[0] + i, 0))
    if grad.ndim == 3:
        units = grad.shape[1]
        count = grad.shape[0] * units // size
        grad_spec = pl.BlockSpec((size // units, units, columns), lambda i, at: (i, 0, 0))
    else:
        count = grad.shape[0] // size
        grad_spec = pl.BlockSpec((size, columns), lambda i, at: (i, 0))
    return tuple(
        pl.pallas_call(
            adamw_kernel,
            grid_spec=pltpu.PrefetchScalarGridSpec(
                num_scalar_prefetch=1,
                grid=(count,),
                in_specs=[pl.BlockSpec(memory_space=pltpu.SMEM), spec, spec, spec, grad_spec]
                + [pl.BlockSpec(memory_space=pl.ANY)] * len(filled),
                out_specs=[spec] * 4,
            ),
            out_shape=[jax.ShapeDtypeStruct(weight.shape, F32)] * 3
            + [jax.ShapeDtypeStruct(weight.shape, BF)],
            input_output_aliases={6 + i: i for i in range(len(filled))},
            cost_estimate=pl.CostEstimate(
                flops=count * columns * size * 10000,
                bytes_accessed=count * columns * size * 30,
                transcendentals=count * columns * size,
            ),
            name="adamw",
        )(jnp.reshape(first, (1,)).astype(jnp.int32), base, *state, grad, *filled)
    )


def stepwise():
    return lax.axis_size("dp") == 16 and lax.axis_size("width") == 2


def quad_sum(values, low, high):
    near, far, across = (
        lax.ppermute(values, "dp", [(i, i ^ mask) for i in range(16)])
        for mask in (low, high, low ^ high)
    )
    return (values + near) + (far + across)


def tree_sum(values):
    if not stepwise():
        return lax.psum(values, ("width", "dp"))
    values = quad_sum(quad_sum(values, 1, 2), 4, 8)
    return values + other_width(values)


def pad_to(values, width, axis):
    missing = width - values.shape[axis]
    if missing == 0:
        return values
    pads = [(0, 0)] * values.ndim
    pads[axis] = (0, missing)
    return jnp.pad(values, pads)


def width_sum(values):
    if lax.axis_size("width") == 2:
        return values.astype(F32) + lax.ppermute(values, "width", [(0, 1), (1, 0)]).astype(F32)
    return jnp.sum(lax.all_gather(values, "width").astype(F32), axis=0)


def per_device(
    tokens,
    cotangent,
    lengths,
    levels,
    step_count,
    weight_in,
    moment_in,
    second_in,
    weight_out,
    moment_out,
    second_out,
    small_params,
    moment_small,
    second_small,
):
    dp = lax.axis_size("dp")
    here = lax.axis_index("dp")
    rows = tokens.shape[0]
    total = rows * dp
    units = E // dp
    own_heads = H // dp
    wide = max(units, 128)
    shard = weight_in.shape[0]

    inputs_f = tokens.astype(F32)
    root = lax.rsqrt(jnp.mean(inputs_f * inputs_f, axis=1, keepdims=True) + NORM_EPS)
    g_in, g_out, conv_w, conv_b, a_log, dt_bias, d_skip = unpack(small_params)
    normed_low = (inputs_f * root * g_in).astype(BF)
    weight_low = weight_in.T.astype(BF)
    ring = dp == 16
    if ring:
        gather = Gather(by_row(normed_low))
        gather.settle()
        gather.advance()
    else:
        normed_all = lax.all_gather(normed_low, "dp", axis=0, tiled=True)
    mine = lax.all_to_all(weight_halves(weight_low, units), "dp", 0, 0)
    mine = mine.transpose(1, 0, 2).reshape(-1, D)
    out_weight_low = by_row(pad_to(weight_out.astype(BF), wide, 0))

    live_units = jnp.right_shift(jnp.int32(E), lax.axis_size("width") - 1 - levels[0])
    live = live_units.astype(F32)
    place, remain = row_places(lengths[0], total)
    place = place[:, None]
    remain = remain[:, None]
    own = lambda v: lax.dynamic_slice_in_dim(v, here * units, units, v.ndim - 1)
    own_h = lambda v: lax.dynamic_slice_in_dim(v, here * own_heads, own_heads, 0)
    unit_mask = (here * units + jnp.arange(units, dtype=jnp.int32) < live_units).astype(F32)
    px = pad_to(
        jnp.concatenate(
            [
                own(conv_w[:, :E]),
                own(conv_b[:E])[None],
                jnp.repeat(own_h(d_skip), P_SIZE)[None],
                own(g_out)[None],
                unit_mask[None],
            ],
            axis=0,
        ),
        wide,
        1,
    )
    pbc = pad_to(jnp.concatenate([conv_w[:, E:], conv_b[None, E:]], axis=0), 8, 0)
    pdt = pad_to(
        pad_to(jnp.stack([own_h(dt_bias), -jnp.exp(own_h(a_log))]), 128, 1), 8, 0
    )

    if ring:
        gather.settle(mine, place, remain)
        gather.advance()
        mine = after(mine, gather.sent)
        released = after(cotangent, gather.sent)
        gather.settle()
        gather.advance()
        weight_own = by_row(join_weight(mine, units, wide, gather.sent))
        gather.take(weight_own, 0, 1)
        gather.take(weight_own, 2)
        gather.settle()
        gather.advance()
        gather.take(weight_own, 3)
        gather.settle()
        gather.sent = ()
        gather.take(weight_own, 4)
        normed_all, projected = gather.filled
    else:
        weight_own = join_weight(mine, units, wide)
        released = after(cotangent, normed_all, weight_own)
        projected = jnp.dot(normed_all, weight_own, preferred_element_type=F32).astype(BF)
    cotangent_all = lax.all_gather(released, "dp", axis=0, tiled=True)
    carried = (jnp.zeros((wide, N), F32),)
    for begin, end in cuts(total // STRETCH, FRONT_PARTS):
        carried = run_forward(
            carried, begin, end - begin, projected, place, remain, px, pbc, pdt
        )
    _, zin, mixed, square, states = carried
    partial_out = jnp.dot(zin, out_weight_low, preferred_element_type=F32).astype(BF)
    summed_out = lax.psum_scatter(partial_out, "dp", scatter_dimension=0, tiled=True)
    g_out_low = lax.dot_general(
        cotangent_all, out_weight_low, (((1,), (1,)), ((), ())), preferred_element_type=F32
    )
    pull_part = jnp.sum(g_out_low * zin.astype(F32), axis=1)
    both = jnp.sum(lax.all_gather(jnp.stack([square[0], pull_part]), "dp"), axis=0)
    rows_in = (place, remain, mixed, g_out_low, pad_to(both, 8, 0), live.reshape(1, 1))
    scale = lax.rsqrt(lax.dynamic_slice_in_dim(both[0], here * rows, rows, 0) / live + NORM_EPS)
    carried = (
        jnp.zeros((wide, N), F32),
        jnp.zeros((16, wide), F32),
        jnp.zeros((16, 2 * N), F32),
        jnp.zeros((8, 128), F32),
    )
    halves = column_halves(weight_own.T)
    for begin, end in reversed(cuts(total // STRETCH, BACK_PARTS)):
        carried = run_backward(
            (after(carried[0], halves),) + carried[1:], begin, end - begin, projected, rows_in, states, px, pbc, pdt
        )
    _, gx, gbc, gdt, g_projected, out_low = carried
    block_out = (
        inputs_f
        + summed_out.astype(F32)
        * scale[:, None]
    ).astype(BF)

    def placed(part, size):
        spots = jnp.zeros(part.shape[:-1] + (size,), F32)
        return lax.dynamic_update_slice_in_dim(
            spots, part, here * part.shape[-1], part.ndim - 1
        )

    conv_part = jnp.concatenate([placed(gx[:5, :units], E), gbc[:5]], axis=1)
    early = jnp.concatenate(
        [
            placed(gx[6, :units], E),
            conv_part.reshape(-1),
            placed(gdt[1, :own_heads], H),
            placed(gdt[0, :own_heads], H),
            placed(jnp.sum(gx[5, :units].reshape(own_heads, P_SIZE), axis=1), H),
        ]
    )
    g_weight = lax.dot_general(
        g_projected, normed_all, (((0,), (0,)), ((), ())), preferred_element_type=F32
    ).astype(BF)
    g_heads = g_weight[2 * wide + 2 * N : 2 * wide + 2 * N + own_heads]
    g_shared = jnp.concatenate(
        [
            g_weight[2 * wide : 2 * wide + 2 * N],
            lax.dynamic_update_slice_in_dim(
                jnp.zeros((H, D), BF), g_heads, here * own_heads, 0
            ),
        ],
        axis=0,
    )
    g_both = jnp.stack([g_weight[:units], g_weight[wide : wide + units]])
    paired = lax.axis_size("width") == 2

    def to_owners(values):
        return lax.all_to_all(
            values.reshape(-1, dp, shard).transpose(1, 0, 2), "dp", 0, 0
        )

    def half(slot):
        return jnp.concatenate(
            [
                lax.dynamic_index_in_dim(g_both, slot, 0, False),
                lax.dynamic_slice_in_dim(g_shared, slot * (SHARED // 2), SHARED // 2, 0),
            ],
            axis=0,
        )

    if stepwise():
        early = quad_sum(early, 1, 2)
    inward = Scatter(g_projected, weight_own.T, halves, g_weight)
    if paired:
        slot = lax.axis_index("width")
        g_kept = half(slot)
        g_got = other_width(half(1 - slot))
    inward.advance()
    g_weight_out = lax.dot_general(
        after(out_low, inward.sent),
        cotangent_all,
        (((0,), (0,)), ((), ())),
        preferred_element_type=F32,
    )[:units].astype(BF)
    if stepwise():
        inward.advance(g_weight_out)
    else:
        inward.advance(g_weight_out)
    if paired:
        g_kept, g_got, _ = lax.optimization_barrier((g_kept, g_got, inward.sent))
        g_half = to_owners((g_kept.astype(F32) + g_got.astype(F32)).astype(BF))
        total_out = other_width(after(g_weight_out, inward.sent))
        inward.advance()
        inward.advance(total_out)
        if stepwise():
            early = quad_sum(after(early, inward.ready()), 4, 8)
        total_out = g_weight_out.astype(F32) + total_out.astype(F32)
        g_half = after(g_half, inward.sent)
        g_shared = jnp.sum(g_half[:, units:].astype(F32), axis=0).astype(BF)
        g_half = g_half[:, :units]
        g_peer = other_width(g_half)
        g_apart = other_width(g_shared)
    else:
        inward.advance()
        inward.advance()
        total_out = width_sum(g_weight_out)
        g_pairs = width_sum(to_owners(g_both.reshape(-1, D)))
        g_gate, g_x = g_pairs[:, :units], g_pairs[:, units:]
        g_apart = lax.psum_scatter(
            g_shared.reshape(SHARED, dp, shard).transpose(1, 0, 2), "dp", scatter_dimension=0
        )
        g_apart = width_sum(g_apart)
    simple = paired and units % 128 == 0 and shard == 128
    step_float = step_count[0].astype(F32)
    new_out, mom_out, sec_out = adamw_step(
        weight_out,
        moment_out,
        second_out,
        after(total_out, inward.sent),
        MATRIX_RATE,
        MATRIX_DECAY,
        step_float,
    )
    if simple:
        base = (1.0 - jnp.power(BETA_ONE, step_float)).reshape(1, 1)
        own = (weight_in.T, moment_in.T, second_in.T)
        size = 4 * units
        blocks = E // size
        moved = adamw_rows(base, own, after(g_half, inward.sent), slot * blocks, size, ())
        g_normed = inward.finish(new_out, g_peer, g_apart, moved)
    elif paired:
        g_normed = inward.finish(new_out, g_peer, g_apart)
    else:
        g_normed = inward.finish(new_out)
    if paired:
        g_apart = jnp.concatenate(in_order(g_shared, g_apart), axis=0)
    if simple:
        moved = adamw_rows(base, own, g_peer, (1 - slot) * blocks, size, moved)
        moved = adamw_rows(base, own, g_apart, 2 * E // H, H, moved)
        new_in, mom_in, sec_in, low_in = (result.T for result in moved)
    else:
        if paired:
            g_gate, g_x = in_order(g_half, g_peer)
        total_in = jnp.concatenate(
            [
                g_gate.transpose(2, 0, 1).reshape(shard, E),
                g_x.transpose(2, 0, 1).reshape(shard, E),
                g_apart.T,
            ],
            axis=1,
        ).astype(F32)
        new_in, mom_in, sec_in = adamw_step(
            weight_in, moment_in, second_in, total_in, MATRIX_RATE, MATRIX_DECAY, step_float
        )
        low_in = new_in.astype(BF)

    ratio = root * g_in
    lean = jnp.sum(g_in * g_normed * inputs_f, axis=1, keepdims=True)
    g_inputs = ratio * g_normed - inputs_f * (root * root * root / D * lean)
    grad_tokens = (cotangent.astype(F32) + g_inputs).astype(BF)
    g_g_in = jnp.sum(g_normed * inputs_f * root, axis=0)

    if stepwise():
        small = quad_sum(quad_sum(g_g_in, 1, 2), 4, 8)
        total_small = jnp.concatenate([small, early])
        total_small = total_small + other_width(total_small)
    else:
        total_small = tree_sum(jnp.concatenate([g_g_in, early]))
    rate_table, decay_table = small_table()
    new_small, mom_small, sec_small = adamw_step(
        small_params, moment_small, second_small, total_small, rate_table, decay_table, step_float
    )
    return (
        block_out,
        grad_tokens,
        new_in,
        mom_in,
        sec_in,
        low_in,
        new_out,
        mom_out,
        sec_out,
        new_out.astype(BF),
        new_small,
        mom_small,
        sec_small,
    )


def solution(mesh):
    return jax.shard_map(
        per_device,
        mesh=mesh,
        in_specs=(
            P(("width", "dp"), None),
            P(("width", "dp"), None),
            P("width", None),
            P("width"),
            P(),
            P("dp", None),
            P("dp", None),
            P("dp", None),
            P("dp", None),
            P("dp", None),
            P("dp", None),
            P(),
            P(),
            P(),
        ),
        out_specs=(
            P(("width", "dp"), None),
            P(("width", "dp"), None),
            P("dp", None),
            P("dp", None),
            P("dp", None),
            P("dp", None),
            P("dp", None),
            P("dp", None),
            P("dp", None),
            P("dp", None),
            P(),
            P(),
            P(),
        ),
        check_vma=False,
    )
```

```python
from functools import partial

import jax
import jax.numpy as jnp
from jax import lax
from jax.experimental import pallas as pl
from jax.experimental.layout import Layout, with_layout_constraint
from jax.experimental.pallas import tpu as pltpu
from jax.sharding import PartitionSpec as P

D = 2048
E = 4096
H = 64
P_SIZE = 64
N = 128
KCONV = 4
STRETCH = 256
K = 4352

NORM_EPS = 1e-05
ADAM_EPS = 1e-08
BETA_ONE = 0.5
BETA_TWO = 0.5
MATRIX_RATE = 0.02
MATRIX_DECAY = 0.1
PRECISE = lax.Precision.HIGHEST
BF = jnp.bfloat16
F32 = jnp.float32
LOW = -1e30
SHARED = 2 * N + H
BACK_PARTS = 1
FRONT_PARTS = 1


def small_table():
    rate_table = jnp.concatenate(
        [
            jnp.full((D,), 0.3, F32),
            jnp.full((E,), 0.3, F32),
            jnp.full((KCONV * K,), 0.2, F32),
            jnp.full((K,), 0.2, F32),
            jnp.full((H,), 0.3, F32),
            jnp.full((H,), 1.0, F32),
            jnp.full((H,), 0.3, F32),
        ]
    )
    decay_table = jnp.concatenate(
        [
            jnp.zeros((D + E,), F32),
            jnp.full((KCONV * K,), 0.1, F32),
            jnp.zeros((K + 3 * H,), F32),
        ]
    )
    return (rate_table, decay_table)


def unpack(small_params):
    offset = D + E
    conv_w = small_params[offset : offset + KCONV * K].reshape(KCONV, K)
    offset = offset + KCONV * K
    conv_b = small_params[offset : offset + K]
    offset = offset + K
    a_log = small_params[offset : offset + H]
    dt_bias = small_params[offset + H : offset + 2 * H]
    d_skip = small_params[offset + 2 * H : offset + 3 * H]
    return (small_params[:D], small_params[D : D + E], conv_w, conv_b, a_log, dt_bias, d_skip)


def row_places(lengths_row, row_count):
    seq_ends = jnp.cumsum(lengths_row)
    at = jnp.arange(row_count, dtype=jnp.int32)
    passed = seq_ends[None, :] <= at[:, None]
    begin = jnp.max(jnp.where(passed, seq_ends[None, :], 0), axis=1)
    finish = jnp.min(jnp.where(passed, row_count, seq_ends[None, :]), axis=1)
    return (at - begin, finish - 1 - at)


def adamw_step(weight, moment, second, grad, rate, decay, step_float):
    first_new = BETA_ONE * moment + (1.0 - BETA_ONE) * grad
    second_new = BETA_TWO * second + (1.0 - BETA_TWO) * grad * grad
    first_hat = first_new / (1.0 - jnp.power(BETA_ONE, step_float))
    second_hat = second_new / (1.0 - jnp.power(BETA_TWO, step_float))
    return (
        weight - rate * (first_hat / (jnp.sqrt(second_hat) + ADAM_EPS) + decay * weight),
        first_new,
        second_new,
    )


def sigmoid(v):
    return 1.0 / (1.0 + jnp.exp(-v))


def dot(a, b, dims):
    return lax.dot_general(
        a.astype(BF), b.astype(BF), (dims, ((), ())), preferred_element_type=F32
    )


def split(values, count):
    parts = []
    for _ in range(count):
        part = values.astype(BF)
        values = values - part.astype(F32)
        parts.append(part)
    return parts


def head_lanes(heads):
    row = lax.broadcasted_iota(jnp.int32, (128, heads * P_SIZE), 0)
    lane = lax.broadcasted_iota(jnp.int32, (128, heads * P_SIZE), 1)
    return jnp.where(lane // P_SIZE == row, 1.0, 0.0).astype(BF)


def spread(columns, lanes):
    return sum(dot(part, lanes, ((1,), (0,))) for part in split(columns, 2))


def head_sums(values, lanes):
    return sum(dot(part, lanes, ((1,), (1,))) for part in split(values, 2))


def running(mask, values):
    mask = jnp.where(mask, 1.0, 0.0).astype(BF)
    return sum(dot(mask, part, ((1,), (0,))) for part in split(values, 3))


def convolve(buffer, weights, bias, place):
    total = bias + jnp.zeros((STRETCH, buffer.shape[1]), F32)
    for tap in range(KCONV):
        back = KCONV - 1 - tap
        rows = buffer[8 - back : 8 - back + STRETCH, :]
        if back:
            rows = jnp.where(place >= back, rows, 0.0)
        total = total + weights[tap : tap + 1, :] * rows
    return total


def block_terms(place, remain, dt_in, pdt):
    row = lax.broadcasted_iota(jnp.int32, (STRETCH, STRETCH), 0)
    col = lax.broadcasted_iota(jnp.int32, (STRETCH, STRETCH), 1)
    at = lax.broadcasted_iota(jnp.int32, (STRETCH, 1), 0)
    biased = dt_in + pdt[0:1, :]
    step = jnp.maximum(biased, 0.0) + jnp.log1p(jnp.exp(-jnp.abs(biased)))
    log_decay = step * pdt[1:2, :]
    cum = running(col <= row, log_decay)
    cum_t = jnp.transpose(cum)
    carrying = jnp.where(place >= at + 1, jnp.exp(cum), 0.0)
    tail_ok = remain >= STRETCH - 1 - at
    tail = jnp.exp(jnp.where(tail_ok, cum[STRETCH - 1 : STRETCH, :] - cum, LOW))
    return row, col, biased, step, log_decay, cum, cum_t, carrying, tail


def forward_kernel(
    heads,
    gate_ref,
    x_ref,
    bc_ref,
    dt_ref,
    xprev_ref,
    bcprev_ref,
    place_ref,
    remain_ref,
    px_ref,
    pbc_ref,
    pdt_ref,
    state_in,
    *rest,
):
    zin_ref, mixed_ref, square_ref, states_ref, state, xbuf, bcbuf = rest[-7:]

    @pl.when(pl.program_id(0) == 0)
    def _():
        state[...] = state_in[...]

    xbuf[0:8, :] = xprev_ref[8:16, :].astype(F32)
    bcbuf[0:8, :] = bcprev_ref[8:16, :].astype(F32)
    place = place_ref[...]
    remain = remain_ref[...]
    xbuf[8 : 8 + STRETCH, :] = x_ref[...].astype(F32)
    bcbuf[8 : 8 + STRETCH, :] = bc_ref[...].astype(F32)
    conv_x = convolve(xbuf, px_ref[0:4, :], px_ref[4:5, :], place)
    conv_bc = convolve(bcbuf, pbc_ref[0:4, :], pbc_ref[4:5, :], place)
    x = conv_x * sigmoid(conv_x) * px_ref[7:8, :]
    act_bc = conv_bc * sigmoid(conv_bc)
    b_low = act_bc[:, :N].astype(BF)
    c_low = act_bc[:, N:].astype(BF)
    row, col, _, step, _, cum, cum_t, carrying, tail = block_terms(
        place, remain, dt_ref[...].astype(F32), pdt_ref[...]
    )
    visible = (col <= row) & (row - col <= place)
    lanes = head_lanes(heads)
    scaled = x * spread(step, lanes)
    scaled_low = scaled.astype(BF)
    gram = dot(c_low, b_low, ((1,), (1,)))
    old = state[...]
    states_ref[0] = old
    across = dot(c_low, old, ((1,), (1,))) * spread(carrying, lanes)
    parts = []
    for h in range(heads):
        decay = jnp.exp(jnp.where(visible, cum[:, h : h + 1] - cum_t[h : h + 1, :], LOW))
        parts.append(
            dot(gram * decay, scaled_low[:, h * P_SIZE : (h + 1) * P_SIZE], ((1,), (0,)))
        )
    mixed = jnp.concatenate(parts, axis=1) + across + px_ref[5:6, :] * x
    fresh = dot(scaled * spread(tail, lanes), b_low, ((0,), (0,)))
    for h in range(heads):
        rows = slice(h * P_SIZE, (h + 1) * P_SIZE)
        state[rows, :] = (
            old[rows, :] * carrying[STRETCH - 1 : STRETCH, h : h + 1] + fresh[rows, :]
        )
    gate = gate_ref[...].astype(F32)
    gated = mixed * (gate * sigmoid(gate))
    mixed_ref[...] = mixed
    zin_ref[...] = (gated * px_ref[6:7, :]).astype(BF)
    ones = jnp.ones((8, gated.shape[1]), BF)
    square_ref[...] = sum(dot(ones, part, ((1,), (1,))) for part in split(gated * gated, 2))


def backward_kernel(
    heads,
    gate_ref,
    x_ref,
    bc_ref,
    dt_ref,
    xprev_ref,
    bcprev_ref,
    place_ref,
    remain_ref,
    mixed_ref,
    gout_ref,
    sums_ref,
    live_ref,
    states_ref,
    px_ref,
    pbc_ref,
    pdt_ref,
    gstate_in,
    gx_in,
    gbc_in,
    gdt_in,
    *rest,
):
    gp_ref, low_ref, gstate, gx_ref, gbc_ref, gdt_ref, xbuf, bcbuf, gxbuf, gbcbuf = rest[-10:]
    width = x_ref.shape[1]

    @pl.when(pl.program_id(0) == 0)
    def _():
        gstate[...] = gstate_in[...]
        gxbuf[STRETCH : STRETCH + 8, :] = gx_in[8:16, :]
        gbcbuf[STRETCH : STRETCH + 8, :] = gbc_in[8:16, :]
        gx_ref[...] = gx_in[...]
        gbc_ref[...] = gbc_in[...]
        gdt_ref[...] = gdt_in[...]

    place = place_ref[...]
    remain = remain_ref[...]
    xbuf[0:8, :] = xprev_ref[8:16, :].astype(F32)
    bcbuf[0:8, :] = bcprev_ref[8:16, :].astype(F32)
    xbuf[8 : 8 + STRETCH, :] = x_ref[...].astype(F32)
    bcbuf[8 : 8 + STRETCH, :] = bc_ref[...].astype(F32)
    conv_x = convolve(xbuf, px_ref[0:4, :], px_ref[4:5, :], place)
    conv_bc = convolve(bcbuf, pbc_ref[0:4, :], pbc_ref[4:5, :], place)
    sig_x = sigmoid(conv_x)
    sig_bc = sigmoid(conv_bc)
    x = conv_x * sig_x * px_ref[7:8, :]
    act_bc = conv_bc * sig_bc
    b_low = act_bc[:, :N].astype(BF)
    c_low = act_bc[:, N:].astype(BF)
    row, col, biased, step, log_decay, cum, cum_t, carrying, tail = block_terms(
        place, remain, dt_ref[...].astype(F32), pdt_ref[...]
    )
    visible = (col >= row) & (col - row <= remain)
    lanes = head_lanes(heads)

    gate = gate_ref[...].astype(F32)
    sig = sigmoid(gate)
    silu = gate * sig
    mixed = mixed_ref[...]
    gated = mixed * silu
    g_out = px_ref[6:7, :]
    sums = jnp.transpose(
        jnp.concatenate([sums_ref[...], jnp.zeros((120, STRETCH), F32)], axis=0)
    )
    live = live_ref[0, 0]
    scale = lax.rsqrt(sums[:, 0:1] / live + NORM_EPS)
    pull = scale * scale * scale / live * sums[:, 1:2]
    upstream = gout_ref[...]
    low_ref[...] = (gated * scale * g_out).astype(BF)
    g_gated = scale * g_out * upstream - gated * pull
    g_mixed = g_gated * silu
    gp_ref[:, 0:width] = (g_gated * mixed * (sig * (1.0 + gate * (1.0 - sig)))).astype(BF)

    step_wide = spread(step, lanes)
    carry_wide = spread(carrying, lanes)
    tail_wide = spread(tail, lanes)
    scaled = x * step_wide
    scaled_low = scaled.astype(BF)
    g_low = g_mixed.astype(BF)
    old = states_ref[0]
    g_new = gstate[...]
    old_low = old.astype(BF)
    g_new_low = g_new.astype(BF)
    gram = dot(b_low, c_low, ((1,), (1,)))
    across = dot(c_low, old_low, ((1,), (1,)))
    returned = dot(b_low, g_new_low, ((1,), (1,))) * tail_wide
    g_carried = g_mixed * carry_wide
    g_carried_low = g_carried.astype(BF)
    tailed_low = (scaled * tail_wide).astype(BF)

    g_gram = jnp.zeros((STRETCH, STRETCH), F32)
    lane = lax.broadcasted_iota(jnp.int32, (STRETCH, 128), 1)
    sources = jnp.zeros((STRETCH, 128), F32)
    target_rows = []
    parts = []
    for h in range(heads):
        cols = slice(h * P_SIZE, (h + 1) * P_SIZE)
        decay = jnp.exp(jnp.where(visible, cum_t[h : h + 1, :] - cum[:, h : h + 1], LOW))
        mixing = gram * decay
        g_mixing = dot(scaled_low[:, cols], g_low[:, cols], ((1,), (1,)))
        parts.append(dot(mixing, g_low[:, cols], ((1,), (0,))))
        g_gram = g_gram + g_mixing * decay
        both = g_mixing * mixing
        sources = jnp.where(lane == h, jnp.sum(both, axis=1, keepdims=True), sources)
        target_rows.append(jnp.sum(both, axis=0, keepdims=True))
    target_rows.append(jnp.zeros((128 - heads, STRETCH), F32))
    targets = jnp.transpose(jnp.concatenate(target_rows, axis=0))
    g_scaled = jnp.concatenate(parts, axis=1) + returned
    into = head_sums(g_carried * across, lanes)
    outof = head_sums(scaled * returned, lanes)
    state_dot = jnp.zeros((1, 128), F32)
    lane_one = lax.broadcasted_iota(jnp.int32, (1, 128), 1)
    product = g_new * old
    for h in range(heads):
        total = jnp.sum(
            jnp.sum(product[h * P_SIZE : (h + 1) * P_SIZE, :], axis=0, keepdims=True),
            axis=1,
            keepdims=True,
        )
        state_dot = jnp.where(lane_one == h, total, state_dot)
    g_c = dot(g_gram, b_low, ((0,), (0,))) + dot(g_carried_low, old_low, ((1,), (0,)))
    g_b = dot(g_gram, c_low, ((1,), (0,))) + dot(tailed_low, g_new_low, ((1,), (0,)))
    g_fresh = dot(g_carried_low, c_low, ((0,), (0,)))
    for h in range(heads):
        rows = slice(h * P_SIZE, (h + 1) * P_SIZE)
        gstate[rows, :] = (
            g_new[rows, :] * carrying[STRETCH - 1 : STRETCH, h : h + 1] + g_fresh[rows, :]
        )
    g_cum = targets - sources + into - outof
    g_decay = running(col >= row, g_cum) + (
        jnp.sum(outof, axis=0, keepdims=True)
        + carrying[STRETCH - 1 : STRETCH, :] * state_dot
    )
    g_step = head_sums(x * g_scaled, lanes) + g_decay * pdt_ref[1:2, :]
    g_dt = g_step * sigmoid(biased)
    gdt_ref[0:1, :] += jnp.sum(g_dt, axis=0, keepdims=True)
    gdt_ref[1:2, :] += jnp.sum(g_decay * log_decay, axis=0, keepdims=True)
    g_x = px_ref[5:6, :] * g_mixed + step_wide * g_scaled
    g_conv_x = g_x * px_ref[7:8, :] * (sig_x * (1.0 + conv_x * (1.0 - sig_x)))
    g_act = jnp.concatenate([g_b, g_c], axis=1)
    g_conv_bc = g_act * (sig_bc * (1.0 + conv_bc * (1.0 - sig_bc)))
    gx_ref[4:5, :] += jnp.sum(g_conv_x, axis=0, keepdims=True)
    gx_ref[5:6, :] += jnp.sum(g_mixed * x, axis=0, keepdims=True)
    gx_ref[6:7, :] += jnp.sum(upstream * gated * scale, axis=0, keepdims=True)
    gbc_ref[4:5, :] += jnp.sum(g_conv_bc, axis=0, keepdims=True)
    gxbuf[0:STRETCH, :] = g_conv_x
    gbcbuf[0:STRETCH, :] = g_conv_bc
    g_in_x = jnp.zeros((STRETCH, width), F32)
    g_in_bc = jnp.zeros((STRETCH, 2 * N), F32)
    for tap in range(KCONV):
        back = KCONV - 1 - tap
        rows_x = xbuf[8 - back : 8 - back + STRETCH, :]
        rows_bc = bcbuf[8 - back : 8 - back + STRETCH, :]
        later_x = gxbuf[back : back + STRETCH, :]
        later_bc = gbcbuf[back : back + STRETCH, :]
        if back:
            rows_x = jnp.where(place >= back, rows_x, 0.0)
            rows_bc = jnp.where(place >= back, rows_bc, 0.0)
            later_x = jnp.where(remain >= back, later_x, 0.0)
            later_bc = jnp.where(remain >= back, later_bc, 0.0)
        gx_ref[tap : tap + 1, :] += jnp.sum(g_conv_x * rows_x, axis=0, keepdims=True)
        gbc_ref[tap : tap + 1, :] += jnp.sum(g_conv_bc * rows_bc, axis=0, keepdims=True)
        g_in_x = g_in_x + px_ref[tap : tap + 1, :] * later_x
        g_in_bc = g_in_bc + pbc_ref[tap : tap + 1, :] * later_bc
    gxbuf[STRETCH : STRETCH + 8, :] = g_conv_x[0:8, :]
    gbcbuf[STRETCH : STRETCH + 8, :] = g_conv_bc[0:8, :]
    gx_ref[8:16, :] = g_conv_x[0:8, :]
    gbc_ref[8:16, :] = g_conv_bc[0:8, :]
    gp_ref[:, width : 2 * width] = g_in_x.astype(BF)
    gp_ref[:, 2 * width : 2 * width + 2 * N] = g_in_bc.astype(BF)
    gp_ref[:, 2 * width + 2 * N : 2 * width + 2 * N + 128] = g_dt.astype(BF)


def run_forward(carried, first, count, projected, place, remain, px, pbc, pdt):
    total = projected.shape[0]
    width = px.shape[1]
    heads = width // P_SIZE
    row_spec = lambda w, c: pl.BlockSpec((STRETCH, w), lambda i: (first + i, c))
    prev_spec = lambda w, c: pl.BlockSpec(
        (16, w), lambda i: (jnp.maximum((first + i) * (STRETCH // 16) - 1, 0), c)
    )
    whole = lambda a: pl.BlockSpec(a.shape, lambda i: (0, 0))
    state = carried[0]
    filled = tuple(carried[1:])
    results = pl.pallas_call(
        partial(forward_kernel, heads),
        grid=(count,),
        in_specs=[
            row_spec(width, 0),
            row_spec(width, 1),
            row_spec(2 * N, width // N),
            row_spec(128, (2 * width + 2 * N) // 128),
            prev_spec(width, 1),
            prev_spec(2 * N, width // N),
            row_spec(1, 0),
            row_spec(1, 0),
            whole(px),
            whole(pbc),
            whole(pdt),
            whole(state),
        ]
        + [pl.BlockSpec(memory_space=pl.ANY)] * len(filled),
        out_specs=[
            row_spec(width, 0),
            row_spec(width, 0),
            pl.BlockSpec((8, STRETCH), lambda i: (0, first + i)),
            pl.BlockSpec((1, width, N), lambda i: (first + i, 0, 0)),
            whole(state),
        ],
        out_shape=[
            jax.ShapeDtypeStruct((total, width), BF),
            jax.ShapeDtypeStruct((total, width), F32),
            jax.ShapeDtypeStruct((8, total), F32),
            jax.ShapeDtypeStruct((total // STRETCH, width, N), F32),
            jax.ShapeDtypeStruct((width, N), F32),
        ],
        scratch_shapes=[
            pltpu.VMEM((STRETCH + 8, width), F32),
            pltpu.VMEM((STRETCH + 8, 2 * N), F32),
        ],
        input_output_aliases={12: 0, 13: 1, 14: 2, 15: 3} if filled else {},
        cost_estimate=pl.CostEstimate(
            flops=count * STRETCH * 256 * 20000,
            bytes_accessed=count * STRETCH * 5000,
            transcendentals=count * STRETCH * 1500,
        ),
        name="scan_forward",
    )(*((projected,) * 6 + (place, remain, px, pbc, pdt, state) + filled))
    return (results[4],) + tuple(results[:4])


def run_backward(carried, first, count, projected, rows_in, states, px, pbc, pdt):
    total = projected.shape[0]
    width = px.shape[1]
    heads = width // P_SIZE
    columns = projected.shape[1]
    rev = lambda i: first + count - 1 - i
    row_spec = lambda w, c: pl.BlockSpec((STRETCH, w), lambda i: (rev(i), c))
    prev_spec = lambda w, c: pl.BlockSpec(
        (16, w), lambda i: (jnp.maximum(rev(i) * (STRETCH // 16) - 1, 0), c)
    )
    whole = lambda a: pl.BlockSpec(a.shape, lambda i: (0, 0))
    fixed = lambda r, w: pl.BlockSpec((r, w), lambda i: (0, 0))
    place, remain, mixed, g_out_low, sums, live = rows_in
    gstate, gx, gbc, gdt = carried[:4]
    filled = tuple(carried[4:])
    operands = (
        (projected,) * 6
        + (place, remain, mixed, g_out_low, sums, live, states, px, pbc, pdt)
        + (gstate, gx, gbc, gdt)
        + filled
    )
    results = pl.pallas_call(
        partial(backward_kernel, heads),
        grid=(count,),
        in_specs=[
            row_spec(width, 0),
            row_spec(width, 1),
            row_spec(2 * N, width // N),
            row_spec(128, (2 * width + 2 * N) // 128),
            prev_spec(width, 1),
            prev_spec(2 * N, width // N),
            row_spec(1, 0),
            row_spec(1, 0),
            row_spec(width, 0),
            row_spec(width, 0),
            pl.BlockSpec((8, STRETCH), lambda i: (0, rev(i))),
            pl.BlockSpec(memory_space=pltpu.SMEM),
            pl.BlockSpec((1, width, N), lambda i: (rev(i), 0, 0)),
            whole(px),
            whole(pbc),
            whole(pdt),
            whole(gstate),
            whole(gx),
            whole(gbc),
            whole(gdt),
        ]
        + [pl.BlockSpec(memory_space=pl.ANY)] * len(filled),
        out_specs=[
            row_spec(columns, 0),
            row_spec(width, 0),
            fixed(width, N),
            fixed(16, width),
            fixed(16, 2 * N),
            fixed(8, 128),
        ],
        out_shape=[
            jax.ShapeDtypeStruct((total, columns), BF),
            jax.ShapeDtypeStruct((total, width), BF),
            jax.ShapeDtypeStruct((width, N), F32),
            jax.ShapeDtypeStruct((16, width), F32),
            jax.ShapeDtypeStruct((16, 2 * N), F32),
            jax.ShapeDtypeStruct((8, 128), F32),
        ],
        scratch_shapes=[
            pltpu.VMEM((STRETCH + 8, width), F32),
            pltpu.VMEM((STRETCH + 8, 2 * N), F32),
            pltpu.VMEM((STRETCH + 8, width), F32),
            pltpu.VMEM((STRETCH + 8, 2 * N), F32),
        ],
        input_output_aliases={20: 0, 21: 1} if filled else {},
        cost_estimate=pl.CostEstimate(
            flops=count * STRETCH * 256 * 40000,
            bytes_accessed=count * STRETCH * 8000,
            transcendentals=count * STRETCH * 2000,
        ),
        name="scan_backward",
    )(*operands)
    return tuple(results[2:]) + tuple(results[:2])


def after(value, *others):
    return lax.optimization_barrier((value, others))[0]


def by_row(values):
    return with_layout_constraint(values, Layout(major_to_minor=(0, 1)))


def cuts(count, parts):
    edges = [count * i // parts for i in range(parts + 1)]
    return list(zip(edges[:-1], edges[1:]))


def ring_chips():
    return [(z * 2 + x) for x, z in [(0, 0), (0, 1), (0, 2), (0, 3), (1, 3), (1, 2), (1, 1), (1, 0)]]


def hop(values, steps):
    chips = ring_chips()
    count = len(chips)
    pairs = [
        (2 * chips[p] + core, 2 * chips[(p + steps) % count] + core)
        for p in range(count)
        for core in (0, 1)
    ]
    return lax.ppermute(values, "dp", pairs)


def swap(values):
    return lax.ppermute(values, "dp", [(i, i ^ 1) for i in range(lax.axis_size("dp"))])


def ring_place():
    here = lax.axis_index("dp")
    core = here % 2
    chip = here // 2
    spot = jnp.where(chip % 2 == 0, chip // 2, 7 - chip // 2)
    return core, spot


def ring_chip(spot):
    spot = spot % 8
    return jnp.where(spot < 4, spot * 2, (7 - spot) * 2 + 1)


def absorb_kernel(count, by_rows, starts_ref, *refs):
    pieces = refs[:count]
    weight_ref = refs[count]
    kept_ref, product_ref, held = refs[-3:]
    for j in range(count):

        @pl.when(pl.program_id(0) == j)
        def _(j=j):
            held[...] = pieces[j][...]

    values = held[...]
    kept_ref[...] = values
    product_ref[...] = lax.dot_general(
        values,
        weight_ref[...],
        (((1,), (1 if by_rows else 0,)), ((), ())),
        preferred_element_type=F32,
    ).astype(product_ref.dtype)


def absorb(pieces, starts, total, filled, weight, by_rows, kind):
    size, depth = pieces[0].shape
    columns = weight.shape[0 if by_rows else 1]
    count = len(pieces)
    whole = lambda a: pl.BlockSpec(a.shape, lambda i, at: (0, 0))
    placed = lambda w: pl.BlockSpec((size, w), lambda i, at: (at[i], 0))
    return pl.pallas_call(
        partial(absorb_kernel, count, by_rows),
        grid_spec=pltpu.PrefetchScalarGridSpec(
            num_scalar_prefetch=1,
            grid=(count,),
            in_specs=[whole(piece) for piece in pieces]
            + [whole(weight)]
            + [pl.BlockSpec(memory_space=pl.ANY)] * len(filled),
            out_specs=[placed(depth), placed(columns)],
            scratch_shapes=[pltpu.VMEM((size, depth), BF)],
        ),
        out_shape=[
            jax.ShapeDtypeStruct((total, depth), BF),
            jax.ShapeDtypeStruct((total, columns), kind),
        ],
        input_output_aliases={count + 2: 0, count + 3: 1} if filled else {},
        cost_estimate=pl.CostEstimate(
            flops=40 * count * size * depth * columns,
            bytes_accessed=4 * count * size * depth + 2 * depth * columns,
            transcendentals=0,
        ),
        name="absorb_rows",
    )(starts, *pieces, weight, *filled)


class Gather:
    def __init__(self, values):
        self.rows = values.shape[0]
        self.core, self.spot = ring_place()
        self.last = (values, values)
        self.arrived = [((values, ring_chip(self.spot), 0),)]
        self.swapped = []
        self.sent = self.filled = ()

    def settle(self, *others):
        self.last, self.filled, _ = lax.optimization_barrier((self.last, self.filled, others))
        step = len(self.swapped)
        if step:
            offset = self.rows // 2 if step == 4 else 0
            self.arrived.append(
                (
                    (self.last[0], ring_chip(self.spot - step), 0),
                    (self.last[1], ring_chip(self.spot + step), offset),
                )
            )
        self.swapped.append([by_row(swap(by_row(piece))) for piece, _, _ in self.arrived[-1]])

    def advance(self):
        ahead, behind = self.last
        if len(self.swapped) == 4:
            ahead, behind = ahead[: self.rows // 2], behind[self.rows // 2 :]
        self.sent, self.swapped[-1] = lax.optimization_barrier(
            ((ahead, behind), self.swapped[-1])
        )
        ahead, behind = self.sent
        self.last = (by_row(hop(by_row(ahead), 1)), by_row(hop(by_row(behind), -1)))

    def take(self, weight, *hops):
        pieces, starts = [], []
        for k in hops:
            for (piece, chip, offset), other in zip(self.arrived[k], self.swapped[k]):
                for part, core in ((piece, self.core), (other, 1 - self.core)):
                    pieces.append(part)
                    starts.append(((2 * chip + core) * self.rows + offset) // piece.shape[0])
        pieces, _ = lax.optimization_barrier((pieces, self.sent))
        self.filled = tuple(
            absorb(
                pieces,
                jnp.stack(starts).astype(jnp.int32),
                16 * self.rows,
                self.filled,
                weight,
                False,
                BF,
            )
        )


class RingSum:
    def __init__(self, chunk, rows):
        self.chunk = chunk
        self.mid = rows // 2
        self.step = 4
        self.last = self.sent = ()
        self.ready = (chunk(4, ()),)

    def settle(self, others):
        self.last, self.ready, _ = lax.optimization_barrier((self.last, self.ready, others))

    def advance(self, *others):
        self.settle(others)
        mid = self.mid
        if self.step == 4:
            up, down = self.ready[0][:mid], self.ready[0][mid:]
        else:
            up, down = (value.astype(F32) for value in self.last)
            first, second = self.ready
            if self.step == 3:
                up = jnp.concatenate([first[:mid] + up, first[mid:]], axis=0)
                down = jnp.concatenate([second[:mid], second[mid:] + down], axis=0)
            else:
                up, down = first + up, second + down
        self.sent = lax.optimization_barrier((up.astype(BF), down.astype(BF)))
        up, down = self.sent
        self.last = (by_row(hop(by_row(up), 1)), by_row(hop(by_row(down), -1)))
        self.step -= 1
        self.ready = tuple(
            self.chunk(steps, self.sent)
            for steps in sorted({self.step, -self.step}, reverse=True)
        )

    def finish(self, others):
        self.settle(others)
        return self.ready[0] + self.last[0].astype(F32) + self.last[1].astype(F32)


def column_halves(weight):
    if lax.axis_size("dp") != 16:
        return ()
    core = lax.axis_index("dp") % 2
    half = weight.shape[1] // 2
    take = lambda c: lax.dynamic_slice_in_dim(weight, c * half, half, 1)
    return lax.optimization_barrier((take(core), swap(take(1 - core))))


class Scatter:
    def __init__(self, left, right, halves, *gate):
        self.ring = lax.axis_size("dp") == 16
        self.last = self.sent = ()
        if not self.ring:
            full = jnp.dot(left, right, preferred_element_type=F32).astype(BF)
            self.done = lax.psum_scatter(full, "dp", scatter_dimension=0, tiled=True).astype(F32)
            return
        self.core, spot = ring_place()
        sides = ((left, halves[0]), (swap(left), halves[1]))
        sides = lax.optimization_barrier((sides, gate))[0]
        self.rows = rows = left.shape[0] // 8

        def chunk(steps, deps):
            start = ring_chip(spot + steps) * rows
            return by_row(
                sum(
                    jnp.dot(
                        lax.dynamic_slice_in_dim(after(side, deps), start, rows, 0),
                        weight,
                        preferred_element_type=F32,
                    )
                    for side, weight in sides
                )
            )

        self.sum = RingSum(chunk, rows)

    def advance(self, *others):
        if self.ring:
            self.sum.advance(*others)
            self.last, self.sent = self.sum.last, self.sum.sent

    def ready(self):
        return self.sum.ready if self.ring else ()

    def finish(self, *others):
        if not self.ring:
            return self.done
        done = self.sum.finish(others)
        own = self.rows // 2
        kept = lax.dynamic_slice_in_dim(done, self.core * own, own, 0)
        got = swap(lax.dynamic_slice_in_dim(done, (1 - self.core) * own, own, 0))
        first = self.core == 0
        return jnp.concatenate(
            [jnp.where(first, kept, got), jnp.where(first, got, kept)], axis=1
        )


def other_width(values):
    return lax.ppermute(values, "width", [(0, 1), (1, 0)])


def in_order(mine, other):
    first = lax.axis_index("width") == 0
    return jnp.where(first, mine, other), jnp.where(first, other, mine)


def weight_halves(weight_low, units):
    dp = lax.axis_size("dp")
    heads = weight_low[: 2 * E].reshape(2, dp, units, weight_low.shape[1])
    common = weight_low[2 * E :]
    if lax.axis_size("width") == 2:
        slot = lax.axis_index("width")
        heads = lax.dynamic_slice_in_dim(heads, slot, 1, 0)
        common = lax.dynamic_slice_in_dim(common, slot * (SHARED // 2), SHARED // 2, 0)
    return jnp.concatenate(
        [
            heads.transpose(1, 0, 2, 3).reshape(dp, -1, heads.shape[3]),
            jnp.broadcast_to(common[None], (dp,) + common.shape),
        ],
        axis=1,
    )


def join_weight(mine, units, wide, *gate):
    own_heads = units // P_SIZE
    if lax.axis_size("width") == 2:
        other = after(other_width(mine), gate)
        first, second = in_order(mine, other)
        gate_rows, x_rows = first[:units], second[:units]
        shared = jnp.concatenate([first[units:], second[units:]], axis=0)
    else:
        gate_rows, x_rows, shared = mine[:units], mine[units : 2 * units], mine[2 * units :]
    own_dt = lax.dynamic_slice_in_dim(
        shared, 2 * N + lax.axis_index("dp") * own_heads, own_heads, 0
    )
    return jnp.concatenate(
        [
            pad_to(gate_rows, wide, 0),
            pad_to(x_rows, wide, 0),
            shared[: 2 * N],
            pad_to(own_dt, 128, 0),
        ],
        axis=0,
    ).T


def adamw_kernel(first_ref, base_ref, weight_ref, moment_ref, second_ref, grad_ref, *refs):
    new_ref, first_moment_ref, squares_ref, low_ref = refs[-4:]
    grad = grad_ref[...].astype(F32).reshape(weight_ref.shape)
    base = base_ref[0, 0]
    weight = weight_ref[...]
    first = BETA_ONE * moment_ref[...] + (1.0 - BETA_ONE) * grad
    squares = BETA_TWO * second_ref[...] + (1.0 - BETA_TWO) * grad * grad
    new = weight - MATRIX_RATE * (
        (first / base) / (jnp.sqrt(squares / base) + ADAM_EPS) + MATRIX_DECAY * weight
    )
    new_ref[...] = new
    first_moment_ref[...] = first
    squares_ref[...] = squares
    low_ref[...] = new.astype(BF)


def adamw_rows(base, state, grad, first, size, filled):
    weight = state[0]
    columns = weight.shape[1]
    spec = pl.BlockSpec((size, columns), lambda i, at: (at[0] + i, 0))
    if grad.ndim == 3:
        units = grad.shape[1]
        count = grad.shape[0] * units // size
        grad_spec = pl.BlockSpec((size // units, units, columns), lambda i, at: (i, 0, 0))
    else:
        count = grad.shape[0] // size
        grad_spec = pl.BlockSpec((size, columns), lambda i, at: (i, 0))
    return tuple(
        pl.pallas_call(
            adamw_kernel,
            grid_spec=pltpu.PrefetchScalarGridSpec(
                num_scalar_prefetch=1,
                grid=(count,),
                in_specs=[pl.BlockSpec(memory_space=pltpu.SMEM), spec, spec, spec, grad_spec]
                + [pl.BlockSpec(memory_space=pl.ANY)] * len(filled),
                out_specs=[spec] * 4,
            ),
            out_shape=[jax.ShapeDtypeStruct(weight.shape, F32)] * 3
            + [jax.ShapeDtypeStruct(weight.shape, BF)],
            input_output_aliases={6 + i: i for i in range(len(filled))},
            cost_estimate=pl.CostEstimate(
                flops=count * columns * size * 10000,
                bytes_accessed=count * columns * size * 30,
                transcendentals=count * columns * size,
            ),
            name="adamw",
        )(jnp.reshape(first, (1,)).astype(jnp.int32), base, *state, grad, *filled)
    )


def stepwise():
    return lax.axis_size("dp") == 16 and lax.axis_size("width") == 2


def quad_sum(values, low, high):
    near, far, across = (
        lax.ppermute(values, "dp", [(i, i ^ mask) for i in range(16)])
        for mask in (low, high, low ^ high)
    )
    return (values + near) + (far + across)


def tree_sum(values):
    if not stepwise():
        return lax.psum(values, ("width", "dp"))
    values = quad_sum(quad_sum(values, 1, 2), 4, 8)
    return values + other_width(values)


def pad_to(values, width, axis):
    missing = width - values.shape[axis]
    if missing == 0:
        return values
    pads = [(0, 0)] * values.ndim
    pads[axis] = (0, missing)
    return jnp.pad(values, pads)


def width_sum(values):
    if lax.axis_size("width") == 2:
        return values.astype(F32) + lax.ppermute(values, "width", [(0, 1), (1, 0)]).astype(F32)
    return jnp.sum(lax.all_gather(values, "width").astype(F32), axis=0)


def per_device(
    tokens,
    cotangent,
    lengths,
    levels,
    step_count,
    weight_in,
    moment_in,
    second_in,
    weight_out,
    moment_out,
    second_out,
    small_params,
    moment_small,
    second_small,
):
    dp = lax.axis_size("dp")
    here = lax.axis_index("dp")
    rows = tokens.shape[0]
    total = rows * dp
    units = E // dp
    own_heads = H // dp
    wide = max(units, 128)
    shard = weight_in.shape[0]

    inputs_f = tokens.astype(F32)
    root = lax.rsqrt(jnp.mean(inputs_f * inputs_f, axis=1, keepdims=True) + NORM_EPS)
    g_in, g_out, conv_w, conv_b, a_log, dt_bias, d_skip = unpack(small_params)
    normed_low = (inputs_f * root * g_in).astype(BF)
    weight_low = weight_in.T.astype(BF)
    ring = dp == 16
    if ring:
        gather = Gather(by_row(normed_low))
        gather.settle()
        gather.advance()
    else:
        normed_all = lax.all_gather(normed_low, "dp", axis=0, tiled=True)
    mine = lax.all_to_all(weight_halves(weight_low, units), "dp", 0, 0)
    mine = mine.transpose(1, 0, 2).reshape(-1, D)
    out_weight_low = by_row(pad_to(weight_out.astype(BF), wide, 0))

    live_units = jnp.right_shift(jnp.int32(E), lax.axis_size("width") - 1 - levels[0])
    live = live_units.astype(F32)
    place, remain = row_places(lengths[0], total)
    place = place[:, None]
    remain = remain[:, None]
    own = lambda v: lax.dynamic_slice_in_dim(v, here * units, units, v.ndim - 1)
    own_h = lambda v: lax.dynamic_slice_in_dim(v, here * own_heads, own_heads, 0)
    unit_mask = (here * units + jnp.arange(units, dtype=jnp.int32) < live_units).astype(F32)
    px = pad_to(
        jnp.concatenate(
            [
                own(conv_w[:, :E]),
                own(conv_b[:E])[None],
                jnp.repeat(own_h(d_skip), P_SIZE)[None],
                own(g_out)[None],
                unit_mask[None],
            ],
            axis=0,
        ),
        wide,
        1,
    )
    pbc = pad_to(jnp.concatenate([conv_w[:, E:], conv_b[None, E:]], axis=0), 8, 0)
    pdt = pad_to(
        pad_to(jnp.stack([own_h(dt_bias), -jnp.exp(own_h(a_log))]), 128, 1), 8, 0
    )

    if ring:
        gather.settle(mine, place, remain)
        gather.advance()
        mine = after(mine, gather.sent)
        released = after(cotangent, gather.sent)
        gather.settle()
        gather.advance()
        weight_own = by_row(join_weight(mine, units, wide, gather.sent))
        gather.take(weight_own, 0, 1)
        gather.take(weight_own, 2)
        gather.settle()
        gather.advance()
        gather.take(weight_own, 3)
        gather.settle()
        gather.sent = ()
        gather.take(weight_own, 4)
        normed_all, projected = gather.filled
    else:
        weight_own = join_weight(mine, units, wide)
        released = after(cotangent, normed_all, weight_own)
        projected = jnp.dot(normed_all, weight_own, preferred_element_type=F32).astype(BF)
    cotangent_all = lax.all_gather(released, "dp", axis=0, tiled=True)
    carried = (jnp.zeros((wide, N), F32),)
    for begin, end in cuts(total // STRETCH, FRONT_PARTS):
        carried = run_forward(
            carried, begin, end - begin, projected, place, remain, px, pbc, pdt
        )
    _, zin, mixed, square, states = carried
    partial_out = jnp.dot(zin, out_weight_low, preferred_element_type=F32).astype(BF)
    summed_out = lax.psum_scatter(partial_out, "dp", scatter_dimension=0, tiled=True)
    g_out_low = lax.dot_general(
        cotangent_all, out_weight_low, (((1,), (1,)), ((), ())), preferred_element_type=F32
    )
    pull_part = jnp.sum(g_out_low * zin.astype(F32), axis=1)
    both = jnp.sum(lax.all_gather(jnp.stack([square[0], pull_part]), "dp"), axis=0)
    rows_in = (place, remain, mixed, g_out_low, pad_to(both, 8, 0), live.reshape(1, 1))
    scale = lax.rsqrt(lax.dynamic_slice_in_dim(both[0], here * rows, rows, 0) / live + NORM_EPS)
    carried = (
        jnp.zeros((wide, N), F32),
        jnp.zeros((16, wide), F32),
        jnp.zeros((16, 2 * N), F32),
        jnp.zeros((8, 128), F32),
    )
    halves = column_halves(weight_own.T)
    for begin, end in reversed(cuts(total // STRETCH, BACK_PARTS)):
        carried = run_backward(
            (after(carried[0], halves),) + carried[1:], begin, end - begin, projected, rows_in, states, px, pbc, pdt
        )
    _, gx, gbc, gdt, g_projected, out_low = carried
    block_out = (
        inputs_f
        + summed_out.astype(F32)
        * scale[:, None]
    ).astype(BF)

    def placed(part, size):
        spots = jnp.zeros(part.shape[:-1] + (size,), F32)
        return lax.dynamic_update_slice_in_dim(
            spots, part, here * part.shape[-1], part.ndim - 1
        )

    conv_part = jnp.concatenate([placed(gx[:5, :units], E), gbc[:5]], axis=1)
    early = jnp.concatenate(
        [
            placed(gx[6, :units], E),
            conv_part.reshape(-1),
            placed(gdt[1, :own_heads], H),
            placed(gdt[0, :own_heads], H),
            placed(jnp.sum(gx[5, :units].reshape(own_heads, P_SIZE), axis=1), H),
        ]
    )
    g_weight = lax.dot_general(
        g_projected, normed_all, (((0,), (0,)), ((), ())), preferred_element_type=F32
    ).astype(BF)
    g_heads = g_weight[2 * wide + 2 * N : 2 * wide + 2 * N + own_heads]
    g_shared = jnp.concatenate(
        [
            g_weight[2 * wide : 2 * wide + 2 * N],
            lax.dynamic_update_slice_in_dim(
                jnp.zeros((H, D), BF), g_heads, here * own_heads, 0
            ),
        ],
        axis=0,
    )
    g_both = jnp.stack([g_weight[:units], g_weight[wide : wide + units]])
    paired = lax.axis_size("width") == 2

    def to_owners(values):
        return lax.all_to_all(
            values.reshape(-1, dp, shard).transpose(1, 0, 2), "dp", 0, 0
        )

    def half(slot):
        return jnp.concatenate(
            [
                lax.dynamic_index_in_dim(g_both, slot, 0, False),
                lax.dynamic_slice_in_dim(g_shared, slot * (SHARED // 2), SHARED // 2, 0),
            ],
            axis=0,
        )

    if stepwise():
        early = quad_sum(early, 1, 2)
    inward = Scatter(g_projected, weight_own.T, halves, g_weight)
    if paired:
        slot = lax.axis_index("width")
        g_kept = half(slot)
        g_got = other_width(half(1 - slot))
    inward.advance()
    g_weight_out = lax.dot_general(
        after(out_low, inward.sent),
        cotangent_all,
        (((0,), (0,)), ((), ())),
        preferred_element_type=F32,
    )[:units].astype(BF)
    if stepwise():
        inward.advance(g_weight_out)
    else:
        inward.advance(g_weight_out)
    if paired:
        g_kept, g_got, _ = lax.optimization_barrier((g_kept, g_got, inward.sent))
        g_half = to_owners((g_kept.astype(F32) + g_got.astype(F32)).astype(BF))
        total_out = other_width(after(g_weight_out, inward.sent))
        inward.advance()
        inward.advance(total_out)
        if stepwise():
            early = quad_sum(after(early, inward.ready()), 4, 8)
        total_out = g_weight_out.astype(F32) + total_out.astype(F32)
        g_half = after(g_half, inward.sent)
        g_shared = jnp.sum(g_half[:, units:].astype(F32), axis=0).astype(BF)
        g_half = g_half[:, :units]
        g_peer = other_width(g_half)
        g_apart = other_width(g_shared)
    else:
        inward.advance()
        inward.advance()
        total_out = width_sum(g_weight_out)
        g_pairs = width_sum(to_owners(g_both.reshape(-1, D)))
        g_gate, g_x = g_pairs[:, :units], g_pairs[:, units:]
        g_apart = lax.psum_scatter(
            g_shared.reshape(SHARED, dp, shard).transpose(1, 0, 2), "dp", scatter_dimension=0
        )
        g_apart = width_sum(g_apart)
    simple = paired and units % 128 == 0 and shard == 128
    step_float = step_count[0].astype(F32)
    new_out, mom_out, sec_out = adamw_step(
        weight_out,
        moment_out,
        second_out,
        after(total_out, inward.sent),
        MATRIX_RATE,
        MATRIX_DECAY,
        step_float,
    )
    if simple:
        base = (1.0 - jnp.power(BETA_ONE, step_float)).reshape(1, 1)
        own = (weight_in.T, moment_in.T, second_in.T)
        size = 4 * units
        blocks = E // size
        moved = adamw_rows(base, own, after(g_half, inward.sent), slot * blocks, size, ())
        g_normed = inward.finish(new_out, g_peer, g_apart, moved)
    elif paired:
        g_normed = inward.finish(new_out, g_peer, g_apart)
    else:
        g_normed = inward.finish(new_out)
    ratio = root * g_in
    lean = jnp.sum(g_in * g_normed * inputs_f, axis=1, keepdims=True)
    g_inputs = ratio * g_normed - inputs_f * (root * root * root / D * lean)
    grad_tokens = (cotangent.astype(F32) + g_inputs).astype(BF)
    g_g_in = jnp.sum(g_normed * inputs_f * root, axis=0)

    if paired:
        g_apart = jnp.concatenate(in_order(g_shared, g_apart), axis=0)
    if simple:
        moved = adamw_rows(base, own, after(g_peer, g_g_in), (1 - slot) * blocks, size, moved)
        moved = adamw_rows(base, own, g_apart, 2 * E // H, H, moved)
        new_in, mom_in, sec_in, low_in = (result.T for result in moved)
    else:
        if paired:
            g_gate, g_x = in_order(g_half, g_peer)
        total_in = jnp.concatenate(
            [
                g_gate.transpose(2, 0, 1).reshape(shard, E),
                g_x.transpose(2, 0, 1).reshape(shard, E),
                g_apart.T,
            ],
            axis=1,
        ).astype(F32)
        new_in, mom_in, sec_in = adamw_step(
            weight_in, moment_in, second_in, total_in, MATRIX_RATE, MATRIX_DECAY, step_float
        )
        low_in = new_in.astype(BF)


    if stepwise():
        small = quad_sum(quad_sum(g_g_in, 1, 2), 4, 8)
        total_small = jnp.concatenate([small, early])
        total_small = total_small + other_width(total_small)
    else:
        total_small = tree_sum(jnp.concatenate([g_g_in, early]))
    rate_table, decay_table = small_table()
    new_small, mom_small, sec_small = adamw_step(
        small_params, moment_small, second_small, total_small, rate_table, decay_table, step_float
    )
    return (
        block_out,
        grad_tokens,
        new_in,
        mom_in,
        sec_in,
        low_in,
        new_out,
        mom_out,
        sec_out,
        new_out.astype(BF),
        new_small,
        mom_small,
        sec_small,
    )


def solution(mesh):
    return jax.shard_map(
        per_device,
        mesh=mesh,
        in_specs=(
            P(("width", "dp"), None),
            P(("width", "dp"), None),
            P("width", None),
            P("width"),
            P(),
            P("dp", None),
            P("dp", None),
            P("dp", None),
            P("dp", None),
            P("dp", None),
            P("dp", None),
            P(),
            P(),
            P(),
        ),
        out_specs=(
            P(("width", "dp"), None),
            P(("width", "dp"), None),
            P("dp", None),
            P("dp", None),
            P("dp", None),
            P("dp", None),
            P("dp", None),
            P("dp", None),
            P("dp", None),
            P("dp", None),
            P(),
            P(),
            P(),
        ),
        check_vma=False,
    )
```
